128 devices in a mesh: xline: 4 (over x), inline: 32 (over y, z, core).
Axes of the slice: x: 4, y: 4, z: 4, core: 2. Of those that a mesh axis runs over, the one named last changes fastest.
Arguments:
- pressure: float32 [1024, 256, 256], P('inline', 'xline'), may hold values from -6 to 6
- vel_inline: float32 [1024, 256, 256], P('inline', 'xline'), may hold values from -6 to 6
- vel_xline: float32 [1024, 256, 256], P('inline', 'xline'), may hold values from -6 to 6
- vel_depth: float32 [1024, 256, 256], P('inline', 'xline'), may hold values from -6 to 6
- modulus: float32 [1024, 256, 256], P('inline', 'xline'), may hold values from 0.5 to 1.5
- buoyancy: float32 [1024, 256, 256], P('inline', 'xline'), may hold values from 0.5 to 1.5
- traces: float32 [98304, 512], P(('xline', 'inline')), may hold values from -6 to 6
- owner: int32 [98304, 1], P(('xline', 'inline')), may hold values from 0 to 127; in each aligned block of 768 rows (0 to 767, 768 to 1535, ...) at most 15 rows name the same one
- node_cell: int32 [98304], P(('xline', 'inline')), may hold values from 0 to 524287
- resample: float32 [4, 512], replicated, may hold values from -0.25 to 0.25
Outputs:
- pressure_out: float32 [1024, 256, 256], P('inline', 'xline')
- inline_out: float32 [1024, 256, 256], P('inline', 'xline')
- xline_out: float32 [1024, 256, 256], P('inline', 'xline')
- depth_out: float32 [1024, 256, 256], P('inline', 'xline')
The draws below stay inside these ranges and needn't reach their ends.
Inputs may be any that keep to these rules, and one draw needn't show every extreme that they name: Among the nodes of one device, at most 15 have the same owner.
All inputs are finite; a program needn't handle non-finite values.
Results may differ from the reference program's by a relative error of at most 0.0002.
Values sent between devices are 32-bit elements; how exact they have to be, the bound alone decides.
A program may use at most 128 MiB of HBM per device.

```python
import math
import jax
import jax.numpy as jnp
import numpy as np
from jax import lax

CI = 32
CX = 64
NZ = 256
STEPS = 4
SAMPLES = 512
TRACE_DEV = 768
NI = 1024
NX = 256
NODES = 98304
CAP = 15
N_INLINE = 32
DEVICES = 128


def set_ends(entries, own_key, least, top_value):
    place = [jax.random.randint(jax.random.fold_in(own_key, axis), (), 0, length) for axis, length in enumerate(entries.shape)]
    longest = entries.shape.index(max(entries.shape))
    next_to = place[:longest] + [(place[longest] + 1) % entries.shape[longest]] + place[longest + 1:]
    return entries.at[tuple(place)].set(least).at[tuple(next_to)].set(top_value)


def levels(rng, shape, split, smallest, high):
    level = 1.0
    for position, blocks in split:
        draws = jax.random.uniform(jax.random.fold_in(jax.random.fold_in(rng, 6), position), (blocks,), jnp.float32, smallest / len(split), high / len(split))
        level = level * jnp.repeat(jnp.exp(draws), shape[position] // blocks).reshape((-1,) + (1,) * (len(shape) - 1 - position))
    return level


def deal_out(key, own, number, rows, number_of, top, reach, slope):
    order = jax.random.permutation(key, number_of)
    heavy_load, ordinary = load_shares(number_of, rows * top, reach, slope, True), load_shares(number_of, rows * top, reach, slope, False)
    places = jnp.arange(number_of)

    def named(tallies, rotation):
        used = int((tallies > 0).sum())
        fixed = max(1, used // 4)
        shifted = fixed + (places - fixed + rotation * (used - fixed)) % max(1, number_of - fixed)
        return jnp.zeros((number_of,), jnp.int32).at[order[jnp.where(places < fixed, places, shifted)]].set(jnp.asarray(tallies, jnp.int32))

    tallies = jnp.where(number % 4 == 0, named(heavy_load, number // 4), named(ordinary, number - number // 4 - 1))
    mixed = jax.random.permutation(jax.random.fold_in(own, 3), number_of)
    donor, sink = mixed[0:number_of // 2 * 2:2], mixed[1:number_of // 2 * 2:2]
    slack = jnp.minimum(tallies[donor] - 1, reach - tallies[sink]) // 2
    slack = jnp.where((donor == order[0]) | (sink == order[0]) | (tallies[sink] == 0), 0, jnp.maximum(slack, 0))
    shifted = jax.random.randint(jax.random.fold_in(own, 4), (number_of // 2,), 0, 1 << 20) % (slack + 1)
    tallies = tallies.at[donor].add(-shifted).at[sink].add(shifted)
    items = jnp.searchsorted(jnp.cumsum(tallies), jnp.arange(rows * top), side="right").astype(jnp.int32)
    listing = items.reshape(top, rows).T
    listing = listing[jax.random.permutation(jax.random.fold_in(own, 1), rows)]
    rotation = jax.random.randint(jax.random.fold_in(own, 2), (rows, 1), 0, top)
    return jnp.take_along_axis(listing, (jnp.arange(top)[None, :] + rotation) % top, axis=1)


def load_shares(count, total, bound, skew, full):
    weights = [(1 << 20) // math.isqrt(grade ** skew) + 1 for grade in range(1, count + 1)]
    largest = bound if full else min(bound, max(-(-total // count), total * weights[0] // sum(weights)))
    least = 1 if total - largest >= count - 1 else 0
    holding, rest = [largest] + [least] * (count - 1), total - largest - least * (count - 1)
    while rest > 0:
        candidates = [i for i in range(1, count) if holding[i] < largest] or [i for i in range(1, count) if holding[i] < bound]
        pool, left = sum([weights[i] for i in candidates]), rest
        for i in candidates:
            extra = min(bound - holding[i], max(1, left * weights[i] // pool), rest)
            holding[i] = holding[i] + extra
            rest = rest - extra
    return np.array(holding)


def normal_values(rng, dims, scale, bound, shards=(), dtype=jnp.bfloat16):
    level = levels(rng, dims, shards, -0.22, 0.18) if shards else 1.0
    values = jax.random.normal(rng, dims, jnp.float32) * scale * level
    return jnp.minimum(jnp.maximum(values, -bound), bound).astype(dtype)


def setup_inputs(seed: int = 0) -> dict:
    seeds = jax.random.split(jax.random.key(seed), 11)
    pressure = normal_values(seeds[0], (NI, NX, NZ), 1.0, 6.0, ((0, 32), (1, 4)), jnp.float32)
    vel_inline = normal_values(seeds[1], (NI, NX, NZ), 1.0, 6.0, ((0, 32), (1, 4)), jnp.float32)
    vel_xline = normal_values(seeds[2], (NI, NX, NZ), 1.0, 6.0, ((0, 32), (1, 4)), jnp.float32)
    vel_depth = normal_values(seeds[3], (NI, NX, NZ), 1.0, 6.0, ((0, 32), (1, 4)), jnp.float32)
    modulus = jnp.clip(jnp.exp(math.log(1.5) - 1.0986123 * jax.random.uniform(seeds[4], (NI, NX, NZ), jnp.float32) ** levels(seeds[4], (NI, NX, NZ), ((0, 32), (1, 4)), -0.2, 0.2)), 0.5, 1.5)
    buoyancy = jnp.clip(jnp.exp(math.log(1.5) - 1.0986123 * jax.random.uniform(seeds[5], (NI, NX, NZ), jnp.float32) ** levels(seeds[5], (NI, NX, NZ), ((0, 32), (1, 4)), -0.2, 0.2)), 0.5, 1.5)
    traces = normal_values(seeds[6], (NODES, SAMPLES), 1.0, 6.0, ((0, 128),), jnp.float32)
    owner_keys = jax.random.split(jax.random.fold_in(seeds[7], 1), NODES // TRACE_DEV)
    owner_turns = jax.random.permutation(jax.random.fold_in(seeds[7], 3), NODES // TRACE_DEV)
    owner = jax.vmap(lambda own, number: deal_out(jax.random.fold_in(seeds[7], 2), own, number, TRACE_DEV, DEVICES, 1, CAP, 2))(owner_keys, owner_turns).reshape((NODES, 1))
    node_cell = set_ends(jax.random.randint(seeds[8], (NODES,), 0, CI * CX * NZ), jax.random.fold_in(seeds[8], 1), 0, (CI * CX * NZ) - 1).astype(jnp.int32)
    resample = normal_values(seeds[9], (STEPS, SAMPLES), SAMPLES ** -0.5, 0.25, (), jnp.float32)
    return dict(pressure=pressure, vel_inline=vel_inline, vel_xline=vel_xline, vel_depth=vel_depth, modulus=modulus, buoyancy=buoyancy, traces=traces, owner=owner, node_cell=node_cell, resample=resample)


COURANT = 0.35


def reference(pressure, vel_inline, vel_xline, vel_depth, modulus, buoyancy, traces, owner, node_cell, resample):
    sources = jnp.dot(traces, resample.T, precision=lax.Precision.HIGHEST, preferred_element_type=jnp.float32)
    owner_id = owner[:, 0].astype(jnp.int32)
    xline_block = owner_id // N_INLINE
    inline_block = owner_id % N_INLINE
    row_index = inline_block * CI + node_cell // (CX * NZ)
    column_index = xline_block * CX + (node_cell // NZ) % CX
    depth_index = node_cell % NZ
    targets = ((row_index * NX + column_index) * NZ + depth_index).astype(jnp.int32)
    weights = COURANT * modulus.reshape(-1)[targets]
    field_shape = pressure.shape
    for step_index in range(STEPS):
        zero_row = jnp.zeros((1, field_shape[1], field_shape[2]), jnp.float32)
        zero_col = jnp.zeros((field_shape[0], 1, field_shape[2]), jnp.float32)
        zero_dep = jnp.zeros((field_shape[0], field_shape[1], 1), jnp.float32)
        grad_inline = jnp.concatenate([pressure[1:], zero_row], 0) - pressure
        grad_xline = jnp.concatenate([pressure[:, 1:], zero_col], 1) - pressure
        grad_depth = jnp.concatenate([pressure[:, :, 1:], zero_dep], 2) - pressure
        vel_inline = vel_inline - COURANT * buoyancy * grad_inline
        vel_xline = vel_xline - COURANT * buoyancy * grad_xline
        vel_depth = vel_depth - COURANT * buoyancy * grad_depth
        divergence = (vel_inline - jnp.concatenate([zero_row, vel_inline[:-1]], 0)) \
            + (vel_xline - jnp.concatenate([zero_col, vel_xline[:, :-1]], 1)) \
            + (vel_depth - jnp.concatenate([zero_dep, vel_depth[:, :, :-1]], 2))
        pressure = pressure - COURANT * modulus * divergence
        pressure = pressure.reshape(-1).at[targets].add(weights * sources[:, step_index]).reshape(field_shape)
    return pressure, vel_inline, vel_xline, vel_depth
```

```python
import jax
import jax.numpy as jnp
from jax import lax
from jax.experimental import pallas as pl
from jax.experimental.pallas import tpu as pltpu
from jax.sharding import PartitionSpec as P

COURANT = 0.35
STEPS = 4
LANES = 128
SUBLANES = 8
SLOT = 8
MESH = pl.DeviceIdType.MESH
VMEM, HBM = pltpu.MemorySpace.VMEM, pltpu.MemorySpace.HBM
F32 = jnp.float32


def lane_ids():
    return lax.broadcasted_iota(jnp.int32, (SUBLANES, LANES), 1)


def row_ids():
    return lax.broadcasted_iota(jnp.int32, (SUBLANES, LANES), 0)


def cols(half):
    return pl.ds(half * LANES, LANES)


def rows(tile):
    return pl.ds(tile * SUBLANES, SUBLANES)


def velocity(p, v_in, v_out, buoyancy, i, tile, next_plane):
    lane = lane_ids()
    (vi, vx, vd), (vi_out, vx_out, vd_out) = v_in, v_out
    here = [p[i, rows(tile), cols(h)] for h in range(2)]
    turned = [pltpu.roll(x, LANES - 1, 1) for x in here]
    deeper = [jnp.where(lane < LANES - 1, turned[0], turned[1]), jnp.where(lane < LANES - 1, turned[1], 0.0)]
    last = p.shape[1] // SUBLANES - 1
    for h in range(2):
        rb = COURANT * buoyancy[i, rows(tile), cols(h)]
        vd_out[i, rows(tile), cols(h)] = vd[i, rows(tile), cols(h)] - rb * (deeper[h] - here[h])
        if next_plane:
            ahead = p[i + 1, rows(tile), cols(h)]
            vi_out[i, rows(tile), cols(h)] = vi[i, rows(tile), cols(h)] - rb * (ahead - here[h])
        if tile < last:
            ahead = p[i, pl.ds(tile * SUBLANES + 1, SUBLANES), cols(h)]
            vx_out[i, rows(tile), cols(h)] = vx[i, rows(tile), cols(h)] - rb * (ahead - here[h])


def velocity_inside(p, v_in, v_out, buoyancy):
    planes, tiles = p.shape[0], p.shape[1] // SUBLANES

    def plane(i, _):
        for tile in range(tiles):
            velocity(p, v_in, v_out, buoyancy, i, tile, True)
        return _

    lax.fori_loop(0, planes - 1, plane, 0)
    for tile in range(tiles):
        velocity(p, v_in, v_out, buoyancy, planes - 1, tile, False)


def velocity_edge(p, v_in, v_out, buoyancy, ahead_i, ahead_x):
    planes, tiles = p.shape[0], p.shape[1] // SUBLANES
    (vi, vx, _), (vi_out, vx_out, _) = v_in, v_out
    i = planes - 1
    for tile in range(tiles):
        for h in range(2):
            at = (i, rows(tile), cols(h))
            rb = COURANT * buoyancy[at]
            vi_out[at] = vi[at] - rb * (ahead_i[rows(tile), cols(h)] - p[at])
    row = row_ids()

    def plane(i, _):
        for h in range(2):
            at = (i, rows(tiles - 1), cols(h))
            here = p[at]
            ahead = jnp.where(
                row < SUBLANES - 1,
                pltpu.roll(here, SUBLANES - 1, 0),
                jnp.broadcast_to(ahead_x[h, pl.ds(i, 1), :], here.shape),
            )
            vx_out[at] = vx[at] - COURANT * buoyancy[at] * (ahead - here)
        return _

    lax.fori_loop(0, planes, plane, 0, unroll=4)


def ghosts(p, first_x, behind_i, behind_x, ghost_in, ghost_out, ghost_b):
    (vi, vx), (vi_out, vx_out), (bi, bx) = ghost_in, ghost_out, ghost_b
    vi_out[...] = vi[...] - COURANT * bi[...] * (p[0] - behind_i[...])
    vx_out[...] = vx[...] - COURANT * bx[...] * (first_x[...] - behind_x[...])


def pressure(p_in, p_out, v, ghost, modulus, i, tile, first, source):
    lane, row = lane_ids(), row_ids()
    vi, vx, vd = v
    ghost_i, ghost_x = ghost
    here = [vd[i, rows(tile), cols(h)] for h in range(2)]
    turned = [pltpu.roll(x, 1, 1) for x in here]
    upper = [jnp.where(lane > 0, turned[0], 0.0), jnp.where(lane > 0, turned[1], turned[0])]
    for h in range(2):
        at = (i, rows(tile), cols(h))
        before_i = ghost_i[rows(tile), cols(h)] if first else vi[i - 1, rows(tile), cols(h)]
        now_x = vx[at]
        if tile > 0:
            before_x = vx[i, pl.ds(tile * SUBLANES - 1, SUBLANES), cols(h)]
        else:
            before_x = jnp.where(
                row > 0,
                pltpu.roll(now_x, 1, 0),
                jnp.broadcast_to(ghost_x[h, pl.ds(i, 1), :], now_x.shape),
            )
        total = (vi[at] - before_i) + (now_x - before_x) + (here[h] - upper[h])
        if source is not None:
            total = total - source(i, tile, h)
        p_out[at] = p_in[at] - COURANT * modulus[at] * total


def shell(planes, tiles, strip):
    for tile in range(tiles):
        strip(0, tile, True)
        strip(planes - 1, tile, False)

    def plane(i, _):
        strip(i, 0, False)
        strip(i, tiles - 1, False)
        return _

    lax.fori_loop(1, planes - 1, plane, 0, unroll=2)


def core(planes, tiles, strip):
    def plane(i, _):
        for tile in range(1, tiles - 1):
            strip(i, tile, False)
        return _

    lax.fori_loop(1, planes - 1, plane, 0)


def take_row(source, row, target):
    def plane(i, _):
        for h in range(2):
            target[h, pl.ds(i, 1), :] = source[i, pl.ds(row, 1), cols(h)]
        return _

    lax.fori_loop(0, source.shape[0], plane, 0, unroll=8)


class Exchange:
    def __init__(self, send_sems, recv_sems):
        self.send_sems, self.recv_sems = send_sems, recv_sems
        self.place = (lax.axis_index("xline"), lax.axis_index("inline"))
        self.count = (lax.axis_size("xline"), lax.axis_size("inline"))
        self.copies = []

    def has(self, axis, step):
        return self.place[axis] < self.count[axis] - 1 if step > 0 else self.place[axis] > 0

    def partner(self, axis, step):
        there = list(self.place)
        there[axis] = jnp.clip(there[axis] + step, 0, self.count[axis] - 1)
        return tuple(there)

    def greet(self, barrier):
        for axis in range(2):
            for step in (-1, 1):
                @pl.when(self.has(axis, step))
                def _():
                    pl.semaphore_signal(
                        barrier, inc=1, device_id=self.partner(axis, step), device_id_type=MESH
                    )

    def met(self, barrier):
        partners = [self.has(axis, step).astype(jnp.int32) for axis in range(2) for step in (-1, 1)]
        pl.semaphore_wait(barrier, sum(partners))

    def send(self, source, target, axis, step, number):
        copy = pltpu.make_async_remote_copy(
            src_ref=source,
            dst_ref=target,
            send_sem=self.send_sems.at[number],
            recv_sem=self.recv_sems.at[number],
            device_id=self.partner(axis, step),
            device_id_type=MESH,
        )

        @pl.when(self.has(axis, step))
        def _():
            copy.start()

        self.copies.append((copy, axis, step))

    def finish(self):
        for copy, axis, step in self.copies:
            @pl.when(self.has(axis, step))
            def _():
                copy.wait_send()

            @pl.when(self.has(axis, -step))
            def _():
                copy.wait_recv()

        self.copies = []


def split(value):
    high = value.astype(jnp.bfloat16).astype(F32)
    return high, value - high


def dot_t(a, b):
    return lax.dot_general(
        a.astype(jnp.bfloat16),
        b.astype(jnp.bfloat16),
        (((1,), (1,)), ((), ())),
        preferred_element_type=F32,
    )


def pack(traces, owner, cell, resample, devices):
    held = traces.shape[0]
    owner_row = owner[...]
    cell_row = cell[...]
    member = lax.broadcasted_iota(jnp.int32, (devices, held), 0) == owner_row
    member = jnp.where(member, 1.0, 0.0)
    earlier = lax.broadcasted_iota(jnp.int32, (LANES, LANES), 0) < lax.broadcasted_iota(
        jnp.int32, (LANES, LANES), 1
    )
    earlier = jnp.where(earlier, 1.0, 0.0).astype(jnp.bfloat16)
    running = jnp.zeros((devices, 1), F32)
    position = []
    for block in range(held // LANES):
        part = member[:, block * LANES : (block + 1) * LANES]
        before = jnp.dot(part.astype(jnp.bfloat16), earlier, preferred_element_type=F32) + running
        position.append(jnp.sum(part * before, axis=0, keepdims=True))
        running = running + jnp.sum(part, axis=1, keepdims=True)
    position = jnp.concatenate(position, axis=1).astype(jnp.int32)

    steps = resample.shape[0]
    filt = jnp.concatenate([resample[...], jnp.zeros((SLOT - steps, resample.shape[1]), F32)], 0)
    filt_high, filt_low = split(filt)
    trace_high, trace_low = split(traces[...])
    both = dot_t(jnp.concatenate([filt_high, filt_low], 0), trace_high)
    fields = both[:SLOT] + both[SLOT:] + dot_t(filt_high, trace_low)
    kind = lax.broadcasted_iota(jnp.int32, (SLOT, held), 0)
    fields = jnp.where(kind == steps, (cell_row // LANES).astype(F32), fields)
    fields = jnp.where(kind == steps + 1, (cell_row % LANES).astype(F32), fields)
    first, rest = split(fields)
    second, third = split(rest)
    packed = []
    for piece in (third, second, first):
        spread = [
            jnp.where(position == q, piece, 0.0) for q in range(LANES // SLOT)
        ]
        packed.append(dot_t(member, jnp.concatenate(spread, 0)))
    return (packed[0] + packed[1]) + packed[2]


def route(
    p_hbm, vi_hbm, vx_hbm, vd_hbm, m_hbm, b_hbm, traces_hbm, owner_hbm, cell_hbm, resample_hbm,
    p, vi, vx, vd, modulus, buoyancy, ghost_i, ghost_x, ghost_bi, ghost_bx, index, values, injected,
    outbox, inbox, behind_i, ahead_i, behind_x, ahead_x, from_vi, from_bi, from_vx, from_bx,
    first_x, last_x, last_vx, last_bx,
    traces, owner, cell, resample,
    load_sems, node_sems, send_sems, recv_sems, post_sem, mail_sem,
):
    devices = lax.axis_size("xline") * lax.axis_size("inline")
    lines = lax.axis_size("inline")
    planes, tiles = p.shape[0], p.shape[1] // SUBLANES
    loads = [
        pltpu.make_async_copy(source, target, load_sems.at[k])
        for k, (source, target) in enumerate(
            ((p_hbm, p), (b_hbm, buoyancy), (vi_hbm, vi), (vx_hbm, vx), (vd_hbm, vd), (m_hbm, modulus))
        )
    ]
    node_loads = [
        pltpu.make_async_copy(source, target, node_sems.at[k])
        for k, (source, target) in enumerate(
            ((owner_hbm, owner), (cell_hbm, cell.at[0]), (resample_hbm, resample), (traces_hbm, traces))
        )
    ]
    for load in node_loads + loads:
        load.start()
    barrier = pltpu.get_barrier_semaphore()
    me = lax.axis_index("xline") * lines + lax.axis_index("inline")

    def other(k):
        there = lax.rem(me + k, devices)
        return there, (there // lines, lax.rem(there, lines))

    def greet(k, _):
        pl.semaphore_signal(barrier, inc=1, device_id=other(k)[1], device_id_type=MESH)
        return _

    lax.fori_loop(1, devices, greet, 0)

    for load in node_loads:
        load.wait()
    packed = pack(traces, owner, cell, resample, devices)
    for row in range(devices):
        outbox[row] = packed[row : row + 1]
    inbox[me] = outbox[me]

    pl.semaphore_wait(barrier, devices - 1)

    def post(k, _):
        there, device = other(k)
        pltpu.make_async_remote_copy(
            src_ref=outbox.at[there],
            dst_ref=inbox.at[me],
            send_sem=post_sem,
            recv_sem=mail_sem,
            device_id=device,
            device_id_type=MESH,
        ).start()
        return _

    lax.fori_loop(1, devices, post, 0)

    halo = Exchange(send_sems, recv_sems)
    for ref in (behind_i, from_vi, from_bi):
        @pl.when(jnp.logical_not(halo.has(1, -1)))
        def _():
            ref[...] = jnp.zeros_like(ref)
    for ref in (behind_x, from_vx, from_bx):
        @pl.when(jnp.logical_not(halo.has(0, -1)))
        def _():
            ref[...] = jnp.zeros_like(ref)

    @pl.when(jnp.logical_not(halo.has(1, 1)))
    def _():
        ahead_i[...] = jnp.zeros_like(ahead_i)

    @pl.when(jnp.logical_not(halo.has(0, 1)))
    def _():
        ahead_x[...] = jnp.zeros_like(ahead_x)

    loads[0].wait()
    halo.send(p.at[planes - 1], behind_i, 1, 1, 0)
    halo.send(p.at[0], ahead_i, 1, -1, 1)
    take_row(p, 0, first_x)
    halo.send(first_x, ahead_x, 0, -1, 2)
    take_row(p, p.shape[1] - 1, last_x)
    halo.send(last_x, behind_x, 0, 1, 3)
    loads[1].wait()
    halo.send(buoyancy.at[planes - 1], from_bi, 1, 1, 4)
    take_row(buoyancy, p.shape[1] - 1, last_bx)
    halo.send(last_bx, from_bx, 0, 1, 5)
    loads[2].wait()
    halo.send(vi.at[planes - 1], from_vi, 1, 1, 6)
    loads[3].wait()
    take_row(vx, p.shape[1] - 1, last_vx)
    halo.send(last_vx, from_vx, 0, 1, 7)
    loads[4].wait()
    loads[5].wait()

    v = (vi, vx, vd)
    velocity_inside(p, v, v, buoyancy)

    def clear(k, _):
        injected[pl.ds(pl.multiple_of(k * 64, 64), 64), :] = jnp.zeros((64, LANES), F32)
        return _

    lax.fori_loop(0, injected.shape[0] // 64, clear, 0)

    halo.finish()
    velocity_edge(p, v, v, buoyancy, ahead_i, ahead_x)
    ghosts(p, first_x, behind_i, behind_x, (from_vi, from_vx), (ghost_i, ghost_x), (from_bi, from_bx))
    ghost_bi[...] = from_bi[...]
    ghost_bx[...] = from_bx[...]

    def strip(i, tile, first):
        pressure(p, p, v, (ghost_i, ghost_x), modulus, i, tile, first, None)

    shell(planes, tiles, strip)
    core(planes, tiles, strip)

    mail = pltpu.make_async_remote_copy(
        src_ref=outbox.at[pl.ds(0, devices - 1)],
        dst_ref=inbox.at[pl.ds(0, devices - 1)],
        send_sem=post_sem,
        recv_sem=mail_sem,
        device_id=other(1)[1],
        device_id_type=MESH,
    )
    mail.wait_send()
    mail.wait_recv()
    arrived = inbox[...].reshape(devices, LANES)
    index[...] = arrived.astype(jnp.int32)
    values[...] = arrived.T


def scatter(index_ref, values, _, injected, index, sem):
    load = pltpu.make_async_copy(index_ref, index, sem)
    load.start()
    load.wait()
    devices = index.shape[0]
    lane = lax.broadcasted_iota(jnp.int32, (STEPS, LANES), 1)
    group = 3

    def sender(d, carry):
        pick = jnp.full((SUBLANES, LANES), d, jnp.int32)
        for start in range(0, 15, group):
            tiles, adds = [], []
            for q in range(start, start + group):
                tile = index[d, q * SLOT + STEPS]
                depth = index[d, q * SLOT + STEPS + 1]
                value = jnp.take_along_axis(values[pl.ds(q * SLOT, SLOT), :], pick, axis=1)[:STEPS]
                tiles.append(tile)
                adds.append(jnp.where(lane == depth, value, 0.0))
            spots = [pl.ds(pl.multiple_of(tile * STEPS, STEPS), STEPS) for tile in tiles]
            old = [injected[spot, :] for spot in spots]
            for b in range(group):
                new = old[b] + adds[b]
                for a in range(b):
                    new = new + jnp.where(tiles[a] == tiles[b], adds[a], 0.0)
                injected[spots[b], :] = new
        return carry

    lax.fori_loop(0, devices, sender, 0)


def advance(
    p_in, vi_in, vx_in, vd_in, modulus, buoyancy, ghost_i_in, ghost_x_in, ghost_bi, ghost_bx, injected,
    p, vi, vx, vd,
    ghost_i, ghost_x, behind_i, ahead_i, behind_x, ahead_x, first_x, last_x, send_sems, recv_sems,
):
    planes, tiles = p.shape[0], p.shape[1] // SUBLANES
    halo = Exchange(None, None)
    barrier = pltpu.get_barrier_semaphore()
    halo.greet(barrier)

    @pl.when(jnp.logical_not(halo.has(1, -1)))
    def _():
        behind_i[...] = jnp.zeros_like(behind_i)

    @pl.when(jnp.logical_not(halo.has(0, -1)))
    def _():
        behind_x[...] = jnp.zeros_like(behind_x)

    @pl.when(jnp.logical_not(halo.has(1, 1)))
    def _():
        ahead_i[...] = jnp.zeros_like(ahead_i)

    @pl.when(jnp.logical_not(halo.has(0, 1)))
    def _():
        ahead_x[...] = jnp.zeros_like(ahead_x)

    def source(step):
        def strip(i, tile, h):
            row = ((i * p.shape[1] + tile * SUBLANES) * 2 + h) * STEPS + step
            return injected[pl.ds(row, SUBLANES, stride=2 * STEPS), :]

        return strip

    def send(step):
        halo.send_sems, halo.recv_sems = send_sems.at[step], recv_sems.at[step]
        halo.send(p.at[planes - 1], behind_i.at[step], 1, 1, 0)
        halo.send(p.at[0], ahead_i.at[step], 1, -1, 1)
        take_row(p, 0, first_x.at[step])
        halo.send(first_x.at[step], ahead_x.at[step], 0, -1, 2)
        take_row(p, p.shape[1] - 1, last_x.at[step])
        halo.send(last_x.at[step], behind_x.at[step], 0, 1, 3)

    def inject(i, tile, first):
        del first
        spread = source(0)
        for h in range(2):
            at = (i, rows(tile), cols(h))
            p[at] = p_in[at] + COURANT * modulus[at] * spread(i, tile, h)

    shell(planes, tiles, inject)
    halo.met(barrier)
    send(0)
    core(planes, tiles, inject)

    v = (vi, vx, vd)
    for step in range(1, STEPS):
        v_in = (vi_in, vx_in, vd_in) if step == 1 else v
        ghost_in = (ghost_i_in, ghost_x_in) if step == 1 else (ghost_i, ghost_x)
        velocity_inside(p, v_in, v, buoyancy)
        halo.finish()
        velocity_edge(p, v_in, v, buoyancy, ahead_i.at[step - 1], ahead_x.at[step - 1])
        ghosts(
            p, first_x.at[step - 1], behind_i.at[step - 1], behind_x.at[step - 1],
            ghost_in, (ghost_i, ghost_x), (ghost_bi, ghost_bx),
        )

        def strip(i, tile, first):
            pressure(p, p, v, (ghost_i, ghost_x), modulus, i, tile, first, source(step))

        shell(planes, tiles, strip)
        if step < STEPS - 1:
            send(step)
        core(planes, tiles, strip)


def shards(
    pressure_in, vel_inline, vel_xline, vel_depth, modulus, buoyancy, traces, owner, node_cell, resample
):
    planes, wide, deep = pressure_in.shape
    devices = lax.axis_size("xline") * lax.axis_size("inline")
    held = traces.shape[0]
    field = (planes, wide, deep)
    plane, column = (wide, deep), (2, planes, LANES)
    injection = (planes * wide * deep // LANES * STEPS, LANES)
    vmem = pl.BlockSpec(memory_space=VMEM)
    hbm = pl.BlockSpec(memory_space=HBM)
    dma = pltpu.SemaphoreType.DMA

    state = pl.pallas_call(
        route,
        out_shape=[VMEM(field, F32)] * 6
        + [VMEM(plane, F32), VMEM(column, F32)] * 2
        + [VMEM((devices, LANES), jnp.int32), VMEM((LANES, devices), F32), VMEM(injection, F32)],
        in_specs=[hbm] * 10,
        out_specs=[vmem] * 13,
        scratch_shapes=[VMEM((devices, 1, LANES), F32)] * 2
        + [VMEM(plane, F32)] * 2
        + [VMEM(column, F32)] * 2
        + [VMEM(plane, F32)] * 2
        + [VMEM(column, F32)] * 6
        + [
            VMEM(traces.shape, F32), VMEM((1, held), jnp.int32), VMEM((1, held), jnp.int32),
            VMEM(resample.shape, F32),
        ]
        + [dma((6,)), dma((4,)), dma((8,)), dma((8,)), dma, dma],
        compiler_params=pltpu.CompilerParams(collective_id=0, has_side_effects=True, vmem_limit_bytes=16 * 2**20),
        name="route",
    )(
        *(
            pltpu.with_memory_space_constraint(x, HBM)
            for x in (
                pressure_in, vel_inline, vel_xline, vel_depth, modulus, buoyancy,
                traces, owner.reshape(1, held), node_cell, resample,
            )
        )
    )
    *fields, index, values, cleared = state
    injected = pl.pallas_call(
        scatter,
        out_shape=VMEM(injection, F32),
        in_specs=[vmem] * 3,
        out_specs=vmem,
        scratch_shapes=[pltpu.SMEM((devices, LANES), jnp.int32), dma],
        input_output_aliases={2: 0},
        compiler_params=pltpu.CompilerParams(vmem_limit_bytes=16 * 2**20),
        name="scatter",
    )(index, values, cleared)
    rounds = STEPS - 1
    return pl.pallas_call(
        advance,
        out_shape=[VMEM(field, F32)] * 4,
        in_specs=[vmem] * 11,
        out_specs=[vmem] * 4,
        scratch_shapes=[VMEM(plane, F32), VMEM(column, F32)]
        + [VMEM((rounds, *plane), F32)] * 2
        + [VMEM((rounds, *column), F32)] * 4
        + [dma((rounds, 4)), dma((rounds, 4))],
        compiler_params=pltpu.CompilerParams(collective_id=1, has_side_effects=True, vmem_limit_bytes=16 * 2**20),
        name="advance",
    )(*fields, injected)


def solution(mesh):
    field = P("inline", "xline", None)
    nodes = ("xline", "inline")
    return jax.shard_map(
        shards,
        mesh=mesh,
        in_specs=(field,) * 6 + (P(nodes, None), P(nodes, None), P(nodes), P()),
        out_specs=(field,) * 4,
        check_vma=False,
    )
```

```python
import jax
import jax.numpy as jnp
from jax import lax
from jax.experimental import pallas as pl
from jax.experimental.pallas import tpu as pltpu
from jax.sharding import PartitionSpec as P

COURANT = 0.35
STEPS = 4
LANES = 128
SUBLANES = 8
SLOT = 8
MESH = pl.DeviceIdType.MESH
VMEM, HBM = pltpu.MemorySpace.VMEM, pltpu.MemorySpace.HBM
F32 = jnp.float32
LIMIT = 16 * 2**20


def lane_ids():
    return lax.broadcasted_iota(jnp.int32, (SUBLANES, LANES), 1)


def row_ids():
    return lax.broadcasted_iota(jnp.int32, (SUBLANES, LANES), 0)


def cols(half):
    return pl.ds(half * LANES, LANES)


def rows(tile):
    return pl.ds(tile * SUBLANES, SUBLANES)


def velocity(p, v_in, v_out, buoyancy, i, tile, next_plane):
    lane = lane_ids()
    (vi, vx, vd), (vi_out, vx_out, vd_out) = v_in, v_out
    here = [p[i, rows(tile), cols(h)] for h in range(2)]
    turned = [pltpu.roll(x, LANES - 1, 1) for x in here]
    deeper = [jnp.where(lane < LANES - 1, turned[0], turned[1]), jnp.where(lane < LANES - 1, turned[1], 0.0)]
    last = p.shape[1] // SUBLANES - 1
    for h in range(2):
        rb = COURANT * buoyancy[i, rows(tile), cols(h)]
        vd_out[i, rows(tile), cols(h)] = vd[i, rows(tile), cols(h)] - rb * (deeper[h] - here[h])
        if next_plane:
            ahead = p[i + 1, rows(tile), cols(h)]
            vi_out[i, rows(tile), cols(h)] = vi[i, rows(tile), cols(h)] - rb * (ahead - here[h])
        if tile < last:
            ahead = p[i, pl.ds(tile * SUBLANES + 1, SUBLANES), cols(h)]
            vx_out[i, rows(tile), cols(h)] = vx[i, rows(tile), cols(h)] - rb * (ahead - here[h])


def velocity_inside(p, v_in, v_out, buoyancy):
    planes, tiles = p.shape[0], p.shape[1] // SUBLANES

    def plane(i, _):
        for tile in range(tiles):
            velocity(p, v_in, v_out, buoyancy, i, tile, True)
        return _

    lax.fori_loop(0, planes - 1, plane, 0, unroll=6)
    for tile in range(tiles):
        velocity(p, v_in, v_out, buoyancy, planes - 1, tile, False)


def velocity_edge(p, v_in, v_out, buoyancy, ahead_i, ahead_x):
    planes, tiles = p.shape[0], p.shape[1] // SUBLANES
    (vi, vx, _), (vi_out, vx_out, _) = v_in, v_out
    i = planes - 1
    for tile in range(tiles):
        for h in range(2):
            at = (i, rows(tile), cols(h))
            rb = COURANT * buoyancy[at]
            vi_out[at] = vi[at] - rb * (ahead_i[rows(tile), cols(h)] - p[at])
    row = row_ids()

    def plane(i, _):
        for h in range(2):
            at = (i, rows(tiles - 1), cols(h))
            here = p[at]
            ahead = jnp.where(
                row < SUBLANES - 1,
                pltpu.roll(here, SUBLANES - 1, 0),
                jnp.broadcast_to(ahead_x[h, pl.ds(i, 1), :], here.shape),
            )
            vx_out[at] = vx[at] - COURANT * buoyancy[at] * (ahead - here)
        return _

    lax.fori_loop(0, planes, plane, 0, unroll=16)


def ghosts(p, first_x, behind_i, behind_x, ghost_in, ghost_out, ghost_b):
    (vi, vx), (vi_out, vx_out), (bi, bx) = ghost_in, ghost_out, ghost_b
    vi_out[...] = vi[...] - COURANT * bi[...] * (p[0] - behind_i[...])
    vx_out[...] = vx[...] - COURANT * bx[...] * (first_x[...] - behind_x[...])


def pressure(p_in, p_out, v, ghost, modulus, i, tile, first, source):
    lane, row = lane_ids(), row_ids()
    vi, vx, vd = v
    ghost_i, ghost_x = ghost
    here = [vd[i, rows(tile), cols(h)] for h in range(2)]
    turned = [pltpu.roll(x, 1, 1) for x in here]
    upper = [jnp.where(lane > 0, turned[0], 0.0), jnp.where(lane > 0, turned[1], turned[0])]
    for h in range(2):
        at = (i, rows(tile), cols(h))
        before_i = ghost_i[rows(tile), cols(h)] if first else vi[i - 1, rows(tile), cols(h)]
        now_x = vx[at]
        if tile > 0:
            before_x = vx[i, pl.ds(tile * SUBLANES - 1, SUBLANES), cols(h)]
        else:
            before_x = jnp.where(
                row > 0,
                pltpu.roll(now_x, 1, 0),
                jnp.broadcast_to(ghost_x[h, pl.ds(i, 1), :], now_x.shape),
            )
        total = (vi[at] - before_i) + (now_x - before_x) + (here[h] - upper[h])
        if source is not None:
            total = total - source(i, tile, h)
        p_out[at] = p_in[at] - COURANT * modulus[at] * total


def source(injected, wide, step):
    def strip(i, tile, h):
        row = ((i * wide + tile * SUBLANES) * 2 + h) * STEPS + step
        return injected[pl.ds(row, SUBLANES, stride=2 * STEPS), :]

    return strip


def shell(planes, tiles, strip):
    for tile in range(tiles):
        strip(0, tile, True)
        strip(planes - 1, tile, False)

    def plane(i, _):
        strip(i, 0, False)
        strip(i, tiles - 1, False)
        return _

    lax.fori_loop(1, planes - 1, plane, 0, unroll=15)


def core(planes, tiles, strip):
    def plane(i, _):
        for tile in range(1, tiles - 1):
            strip(i, tile, False)
        return _

    lax.fori_loop(1, planes - 1, plane, 0, unroll=6)


def take_row(source, row, target):
    def plane(i, _):
        for h in range(2):
            target[h, pl.ds(i, 1), :] = source[i, pl.ds(row, 1), cols(h)]
        return _

    lax.fori_loop(0, source.shape[0], plane, 0, unroll=16)


class Exchange:
    def __init__(self, send_sems, recv_sems):
        self.send_sems, self.recv_sems = send_sems, recv_sems
        self.place = (lax.axis_index("xline"), lax.axis_index("inline"))
        self.count = (lax.axis_size("xline"), lax.axis_size("inline"))
        self.copies = []

    def has(self, axis, step):
        return self.place[axis] < self.count[axis] - 1 if step > 0 else self.place[axis] > 0

    def partner(self, axis, step):
        there = list(self.place)
        there[axis] = jnp.clip(there[axis] + step, 0, self.count[axis] - 1)
        return tuple(there)

    def greet(self, barrier):
        for axis in range(2):
            for step in (-1, 1):
                @pl.when(self.has(axis, step))
                def _():
                    pl.semaphore_signal(
                        barrier, inc=1, device_id=self.partner(axis, step), device_id_type=MESH
                    )

    def met(self, barrier):
        partners = [self.has(axis, step).astype(jnp.int32) for axis in range(2) for step in (-1, 1)]
        pl.semaphore_wait(barrier, sum(partners))

    def send(self, source, target, axis, step, number):
        copy = pltpu.make_async_remote_copy(
            src_ref=source,
            dst_ref=target,
            send_sem=self.send_sems.at[number],
            recv_sem=self.recv_sems.at[number],
            device_id=self.partner(axis, step),
            device_id_type=MESH,
        )

        @pl.when(self.has(axis, step))
        def _():
            copy.start()

        self.copies.append((copy, axis, step))

    def finish(self):
        for copy, axis, step in self.copies:
            @pl.when(self.has(axis, step))
            def _():
                copy.wait_send()

            @pl.when(self.has(axis, -step))
            def _():
                copy.wait_recv()

        self.copies = []


def split(value):
    high = value.astype(jnp.bfloat16).astype(F32)
    return high, value - high


def dot_t(a, b):
    return lax.dot_general(
        a.astype(jnp.bfloat16),
        b.astype(jnp.bfloat16),
        (((1,), (1,)), ((), ())),
        preferred_element_type=F32,
    )


def pack(traces, owner, cell, resample, devices):
    held = traces.shape[0]
    owner_row = owner[...]
    cell_row = cell[...]
    member = lax.broadcasted_iota(jnp.int32, (devices, held), 0) == owner_row
    member = jnp.where(member, 1.0, 0.0)
    earlier = lax.broadcasted_iota(jnp.int32, (LANES, LANES), 0) < lax.broadcasted_iota(
        jnp.int32, (LANES, LANES), 1
    )
    earlier = jnp.where(earlier, 1.0, 0.0).astype(jnp.bfloat16)
    running = jnp.zeros((devices, 1), F32)
    position = []
    for block in range(held // LANES):
        part = member[:, block * LANES : (block + 1) * LANES]
        before = jnp.dot(part.astype(jnp.bfloat16), earlier, preferred_element_type=F32) + running
        position.append(jnp.sum(part * before, axis=0, keepdims=True))
        running = running + jnp.sum(part, axis=1, keepdims=True)
    position = jnp.concatenate(position, axis=1).astype(jnp.int32)

    steps = resample.shape[0]
    filt = jnp.concatenate([resample[...], jnp.zeros((SLOT - steps, resample.shape[1]), F32)], 0)
    filt_high, filt_low = split(filt)
    trace_high, trace_low = split(traces[...])
    both = dot_t(jnp.concatenate([filt_high, filt_low], 0), trace_high)
    fields = both[:SLOT] + both[SLOT:] + dot_t(filt_high, trace_low)
    kind = lax.broadcasted_iota(jnp.int32, (SLOT, held), 0)
    fields = jnp.where(kind == steps, cell_row.astype(F32), fields)
    first, rest = split(fields)
    second, third = split(rest)
    packed = []
    for piece in (third, second, first):
        spread = [
            jnp.where(position == q, piece, 0.0) for q in range(LANES // SLOT)
        ]
        packed.append(dot_t(member, jnp.concatenate(spread, 0)))
    return (packed[0] + packed[1]) + packed[2]


def route(
    p_hbm, vi_hbm, vx_hbm, vd_hbm, m_hbm, b_hbm, traces_hbm, owner_hbm, cell_hbm, resample_hbm,
    p, vi, vx, vd, modulus, buoyancy, ghost_i, ghost_x, ghost_bi, ghost_bx, index, values, injected,
    outbox, inbox, behind_i, ahead_i, behind_x, ahead_x, from_vi, from_bi, from_vx, from_bx,
    first_x, last_x, last_vx, last_bx,
    traces, owner, cell, resample,
    load_sems, node_sems, send_sems, recv_sems, post_sem, mail_sem,
):
    devices = lax.axis_size("xline") * lax.axis_size("inline")
    lines = lax.axis_size("inline")
    planes, tiles = p.shape[0], p.shape[1] // SUBLANES
    loads = [
        pltpu.make_async_copy(source, target, load_sems.at[k])
        for k, (source, target) in enumerate(
            ((p_hbm, p), (b_hbm, buoyancy), (vi_hbm, vi), (vx_hbm, vx), (vd_hbm, vd), (m_hbm, modulus))
        )
    ]
    node_loads = [
        pltpu.make_async_copy(source, target, node_sems.at[k])
        for k, (source, target) in enumerate(
            ((owner_hbm, owner), (cell_hbm, cell.at[0]), (resample_hbm, resample), (traces_hbm, traces))
        )
    ]
    for load in node_loads + loads:
        load.start()
    barrier = pltpu.get_barrier_semaphore()
    me = lax.axis_index("xline") * lines + lax.axis_index("inline")

    def other(k):
        there = lax.rem(me + k, devices)
        return there, (there // lines, lax.rem(there, lines))

    def greet(k, _):
        pl.semaphore_signal(barrier, inc=1, device_id=other(k)[1], device_id_type=MESH)
        return _

    lax.fori_loop(1, devices, greet, 0)

    for load in node_loads:
        load.wait()
    packed = pack(traces, owner, cell, resample, devices)
    for row in range(devices):
        outbox[row] = packed[row : row + 1]
    inbox[me] = outbox[me]

    pl.semaphore_wait(barrier, devices - 1)

    def post(k, _):
        there, device = other(k)
        pltpu.make_async_remote_copy(
            src_ref=outbox.at[there],
            dst_ref=inbox.at[me],
            send_sem=post_sem,
            recv_sem=mail_sem,
            device_id=device,
            device_id_type=MESH,
        ).start()
        return _

    lax.fori_loop(1, devices, post, 0)

    halo = Exchange(send_sems, recv_sems)
    for ref in (behind_i, from_vi, from_bi):
        @pl.when(jnp.logical_not(halo.has(1, -1)))
        def _():
            ref[...] = jnp.zeros_like(ref)
    for ref in (behind_x, from_vx, from_bx):
        @pl.when(jnp.logical_not(halo.has(0, -1)))
        def _():
            ref[...] = jnp.zeros_like(ref)

    @pl.when(jnp.logical_not(halo.has(1, 1)))
    def _():
        ahead_i[...] = jnp.zeros_like(ahead_i)

    @pl.when(jnp.logical_not(halo.has(0, 1)))
    def _():
        ahead_x[...] = jnp.zeros_like(ahead_x)

    loads[0].wait()
    halo.send(p.at[planes - 1], behind_i, 1, 1, 0)
    halo.send(p.at[0], ahead_i, 1, -1, 1)
    take_row(p, 0, first_x)
    halo.send(first_x, ahead_x, 0, -1, 2)
    take_row(p, p.shape[1] - 1, last_x)
    halo.send(last_x, behind_x, 0, 1, 3)
    loads[1].wait()
    halo.send(buoyancy.at[planes - 1], from_bi, 1, 1, 4)
    take_row(buoyancy, p.shape[1] - 1, last_bx)
    halo.send(last_bx, from_bx, 0, 1, 5)
    loads[2].wait()
    halo.send(vi.at[planes - 1], from_vi, 1, 1, 6)
    loads[3].wait()
    take_row(vx, p.shape[1] - 1, last_vx)
    halo.send(last_vx, from_vx, 0, 1, 7)
    loads[4].wait()
    loads[5].wait()

    v = (vi, vx, vd)
    velocity_inside(p, v, v, buoyancy)

    def clear(k, _):
        injected[pl.ds(pl.multiple_of(k * 64, 64), 64), :] = jnp.zeros((64, LANES), F32)
        return _

    lax.fori_loop(0, injected.shape[0] // 64, clear, 0)

    halo.finish()
    velocity_edge(p, v, v, buoyancy, ahead_i, ahead_x)
    ghosts(p, first_x, behind_i, behind_x, (from_vi, from_vx), (ghost_i, ghost_x), (from_bi, from_bx))
    ghost_bi[...] = from_bi[...]
    ghost_bx[...] = from_bx[...]

    def strip(i, tile, first):
        pressure(p, p, v, (ghost_i, ghost_x), modulus, i, tile, first, None)

    shell(planes, tiles, strip)
    core(planes, tiles, strip)

    mail = pltpu.make_async_remote_copy(
        src_ref=outbox.at[pl.ds(0, devices - 1)],
        dst_ref=inbox.at[pl.ds(0, devices - 1)],
        send_sem=post_sem,
        recv_sem=mail_sem,
        device_id=other(1)[1],
        device_id_type=MESH,
    )
    mail.wait_send()
    mail.wait_recv()
    values[...] = inbox[...].reshape(devices, LANES).T
    index[...] = values[pl.ds(STEPS, LANES // SLOT, stride=SLOT), :].astype(jnp.int32)


def scatter(index_ref, values, _, injected, index, sem):
    load = pltpu.make_async_copy(index_ref, index, sem)
    load.start()
    devices = values.shape[1]
    lane = lax.broadcasted_iota(jnp.int32, (STEPS, LANES), 1)
    slots, group = 15, 3

    def spread(d):
        pick = jnp.full((SUBLANES, LANES), d, jnp.int32)
        return [
            jnp.take_along_axis(values[pl.ds(q * SLOT, SLOT), :], pick, axis=1)[:STEPS]
            for q in range(slots)
        ]

    def sender(d, now):
        later = spread(jnp.minimum(d + 1, devices - 1))
        for start in range(0, slots, group):
            tiles, adds = [], []
            for q in range(start, start + group):
                cell = index[q, d]
                tiles.append(lax.shift_right_logical(cell, 7))
                adds.append(jnp.where(lane == (cell & (LANES - 1)), now[q], 0.0))
            spots = [pl.ds(pl.multiple_of(tile * STEPS, STEPS), STEPS) for tile in tiles]
            old = [injected[spot, :] for spot in spots]
            for b in range(group):
                new = old[b] + adds[b]
                for a in range(b):
                    new = new + jnp.where(tiles[a] == tiles[b], adds[a], 0.0)
                injected[spots[b], :] = new
        return later

    first = spread(0)
    load.wait()
    lax.fori_loop(0, devices, sender, first, unroll=4)


def advance(
    p_in, vi_in, vx_in, vd_in, modulus, buoyancy, ghost_i_in, ghost_x_in, ghost_bi, ghost_bx, injected,
    p, vi, vx, vd, ghost_i, ghost_x,
    behind_i, ahead_i, behind_x, ahead_x, first_x, last_x, send_sems, recv_sems,
):
    planes, tiles = p.shape[0], p.shape[1] // SUBLANES
    halo = Exchange(None, None)
    barrier = pltpu.get_barrier_semaphore()
    halo.greet(barrier)

    @pl.when(jnp.logical_not(halo.has(1, -1)))
    def _():
        behind_i[...] = jnp.zeros_like(behind_i)

    @pl.when(jnp.logical_not(halo.has(0, -1)))
    def _():
        behind_x[...] = jnp.zeros_like(behind_x)

    @pl.when(jnp.logical_not(halo.has(1, 1)))
    def _():
        ahead_i[...] = jnp.zeros_like(ahead_i)

    @pl.when(jnp.logical_not(halo.has(0, 1)))
    def _():
        ahead_x[...] = jnp.zeros_like(ahead_x)

    def send(step):
        halo.send_sems, halo.recv_sems = send_sems.at[step], recv_sems.at[step]
        halo.send(p.at[planes - 1], behind_i.at[step], 1, 1, 0)
        halo.send(p.at[0], ahead_i.at[step], 1, -1, 1)
        take_row(p, 0, first_x.at[step])
        halo.send(first_x.at[step], ahead_x.at[step], 0, -1, 2)
        take_row(p, p.shape[1] - 1, last_x.at[step])
        halo.send(last_x.at[step], behind_x.at[step], 0, 1, 3)

    def inject(i, tile, first):
        del first
        spread = source(injected, p.shape[1], 0)
        for h in range(2):
            at = (i, rows(tile), cols(h))
            p[at] = p_in[at] + COURANT * modulus[at] * spread(i, tile, h)

    shell(planes, tiles, inject)
    halo.met(barrier)
    send(0)
    core(planes, tiles, inject)

    v = (vi, vx, vd)
    for step in range(1, STEPS):
        v_in = (vi_in, vx_in, vd_in) if step == 1 else v
        ghost_in = (ghost_i_in, ghost_x_in) if step == 1 else (ghost_i, ghost_x)
        velocity_inside(p, v_in, v, buoyancy)
        halo.finish()
        velocity_edge(p, v_in, v, buoyancy, ahead_i.at[step - 1], ahead_x.at[step - 1])
        ghosts(
            p, first_x.at[step - 1], behind_i.at[step - 1], behind_x.at[step - 1],
            ghost_in, (ghost_i, ghost_x), (ghost_bi, ghost_bx),
        )

        if step == STEPS - 1:
            break
        spread = source(injected, p.shape[1], step)

        def strip(i, tile, first):
            pressure(p, p, v, (ghost_i, ghost_x), modulus, i, tile, first, spread)

        shell(planes, tiles, strip)
        send(step)
        core(planes, tiles, strip)


def finish(
    p_in, vi, vx, vd, ghost_i, ghost_x, modulus, injected,
    p_out, vi_out, vx_out, vd_out,
    p, sems,
):
    planes, tiles = p_in.shape[0], p_in.shape[1] // SUBLANES
    copies = [
        pltpu.make_async_copy(source, target, sems.at[k])
        for k, (source, target) in enumerate(((vi, vi_out), (vx, vx_out), (vd, vd_out)))
    ]
    for copy in copies:
        copy.start()
    spread = source(injected, p_in.shape[1], STEPS - 1)
    v, ghost = (vi, vx, vd), (ghost_i, ghost_x)
    chunks = 4
    size = planes // chunks

    def plane(i, _):
        for tile in range(tiles):
            pressure(p_in, p, v, ghost, modulus, i, tile, False, spread)
        return _

    for chunk in range(chunks):
        start = chunk * size
        if chunk == 0:
            for tile in range(tiles):
                pressure(p_in, p, v, ghost, modulus, 0, tile, True, spread)
        lax.fori_loop(max(start, 1), start + size, plane, 0, unroll=size if chunk else size - 1)
        part = pl.ds(start, size)
        copies.append(pltpu.make_async_copy(p.at[part], p_out.at[part], sems.at[3 + chunk]))
        copies[-1].start()
    for copy in copies:
        copy.wait()


def shards(
    pressure_in, vel_inline, vel_xline, vel_depth, modulus, buoyancy, traces, owner, node_cell, resample
):
    planes, wide, deep = pressure_in.shape
    devices = lax.axis_size("xline") * lax.axis_size("inline")
    held = traces.shape[0]
    field = (planes, wide, deep)
    plane, column = (wide, deep), (2, planes, LANES)
    injection = (planes * wide * deep // LANES * STEPS, LANES)
    vmem = pl.BlockSpec(memory_space=VMEM)
    hbm = pl.BlockSpec(memory_space=HBM)
    dma = pltpu.SemaphoreType.DMA

    state = pl.pallas_call(
        route,
        out_shape=[VMEM(field, F32)] * 6
        + [VMEM(plane, F32), VMEM(column, F32)] * 2
        + [VMEM((LANES // SLOT, devices), jnp.int32), VMEM((LANES, devices), F32), VMEM(injection, F32)],
        in_specs=[hbm] * 10,
        out_specs=[vmem] * 13,
        scratch_shapes=[VMEM((devices, 1, LANES), F32)] * 2
        + [VMEM(plane, F32)] * 2
        + [VMEM(column, F32)] * 2
        + [VMEM(plane, F32)] * 2
        + [VMEM(column, F32)] * 6
        + [
            VMEM(traces.shape, F32), VMEM((1, held), jnp.int32), VMEM((1, held), jnp.int32),
            VMEM(resample.shape, F32),
        ]
        + [dma((6,)), dma((4,)), dma((8,)), dma((8,)), dma, dma],
        compiler_params=pltpu.CompilerParams(collective_id=0, has_side_effects=True, vmem_limit_bytes=LIMIT),
        name="route",
    )(
        *(
            pltpu.with_memory_space_constraint(x, HBM)
            for x in (
                pressure_in, vel_inline, vel_xline, vel_depth, modulus, buoyancy,
                traces, owner.reshape(1, held), node_cell, resample,
            )
        )
    )
    *fields, index, values, cleared = state
    injected = pl.pallas_call(
        scatter,
        out_shape=VMEM(injection, F32),
        in_specs=[vmem] * 3,
        out_specs=vmem,
        scratch_shapes=[pltpu.SMEM((LANES // SLOT, devices), jnp.int32), dma],
        input_output_aliases={2: 0},
        compiler_params=pltpu.CompilerParams(vmem_limit_bytes=LIMIT),
        name="scatter",
    )(index, values, cleared)
    rounds = STEPS - 1
    *fields, ghost_i, ghost_x = pl.pallas_call(
        advance,
        out_shape=[VMEM(field, F32)] * 4 + [VMEM(plane, F32), VMEM(column, F32)],
        in_specs=[vmem] * 11,
        out_specs=[vmem] * 6,
        scratch_shapes=[VMEM((rounds, *plane), F32)] * 2
        + [VMEM((rounds, *column), F32)] * 4
        + [dma((rounds, 4)), dma((rounds, 4))],
        compiler_params=pltpu.CompilerParams(
            collective_id=1, has_side_effects=True, vmem_limit_bytes=LIMIT
        ),
        name="advance",
    )(*fields, injected)
    modulus = state[4]
    return pl.pallas_call(
        finish,
        out_shape=[HBM(field, F32)] * 4,
        in_specs=[vmem] * 8,
        out_specs=[hbm] * 4,
        scratch_shapes=[VMEM(field, F32), dma((7,))],
        compiler_params=pltpu.CompilerParams(vmem_limit_bytes=LIMIT),
        name="finish",
    )(*fields, ghost_i, ghost_x, modulus, injected)


def solution(mesh):
    field = P("inline", "xline", None)
    nodes = ("xline", "inline")
    return jax.shard_map(
        shards,
        mesh=mesh,
        in_specs=(field,) * 6 + (P(nodes, None), P(nodes, None), P(nodes), P()),
        out_specs=(field,) * 4,
        check_vma=False,
    )
```

```python
import jax
import jax.numpy as jnp
from jax import lax
from jax.experimental import pallas as pl
from jax.experimental.pallas import tpu as pltpu
from jax.sharding import PartitionSpec as P

COURANT = 0.35
STEPS = 4
LANES = 128
SUBLANES = 8
SLOT = 8
NEAR = 8
MESH = pl.DeviceIdType.MESH
VMEM, HBM = pltpu.MemorySpace.VMEM, pltpu.MemorySpace.HBM
F32 = jnp.float32
LIMIT = 16 * 2**20


def lane_ids():
    return lax.broadcasted_iota(jnp.int32, (SUBLANES, LANES), 1)


def row_ids():
    return lax.broadcasted_iota(jnp.int32, (SUBLANES, LANES), 0)


def cols(half):
    return pl.ds(half * LANES, LANES)


def rows(tile):
    return pl.ds(tile * SUBLANES, SUBLANES)


def velocity(p, v_in, v_out, buoyancy, i, tile, next_plane):
    lane = lane_ids()
    (vi, vx, vd), (vi_out, vx_out, vd_out) = v_in, v_out
    here = [p[i, rows(tile), cols(h)] for h in range(2)]
    turned = [pltpu.roll(x, LANES - 1, 1) for x in here]
    deeper = [jnp.where(lane < LANES - 1, turned[0], turned[1]), jnp.where(lane < LANES - 1, turned[1], 0.0)]
    last = p.shape[1] // SUBLANES - 1
    for h in range(2):
        rb = COURANT * buoyancy[i, rows(tile), cols(h)]
        vd_out[i, rows(tile), cols(h)] = vd[i, rows(tile), cols(h)] - rb * (deeper[h] - here[h])
        if next_plane:
            ahead = p[i + 1, rows(tile), cols(h)]
            vi_out[i, rows(tile), cols(h)] = vi[i, rows(tile), cols(h)] - rb * (ahead - here[h])
        if tile < last:
            ahead = p[i, pl.ds(tile * SUBLANES + 1, SUBLANES), cols(h)]
            vx_out[i, rows(tile), cols(h)] = vx[i, rows(tile), cols(h)] - rb * (ahead - here[h])


def velocity_inside(p, v_in, v_out, buoyancy):
    planes, tiles = p.shape[0], p.shape[1] // SUBLANES

    def plane(i, _):
        for tile in range(tiles):
            velocity(p, v_in, v_out, buoyancy, i, tile, True)
        return _

    lax.fori_loop(0, planes - 1, plane, 0, unroll=6)
    for tile in range(tiles):
        velocity(p, v_in, v_out, buoyancy, planes - 1, tile, False)


def velocity_edge(p, v_in, v_out, buoyancy, ahead_i, ahead_x):
    planes, tiles = p.shape[0], p.shape[1] // SUBLANES
    (vi, vx, _), (vi_out, vx_out, _) = v_in, v_out
    i = planes - 1
    for tile in range(tiles):
        for h in range(2):
            at = (i, rows(tile), cols(h))
            rb = COURANT * buoyancy[at]
            vi_out[at] = vi[at] - rb * (ahead_i[rows(tile), cols(h)] - p[at])
    row = row_ids()

    def plane(i, _):
        for h in range(2):
            at = (i, rows(tiles - 1), cols(h))
            here = p[at]
            ahead = jnp.where(
                row < SUBLANES - 1,
                pltpu.roll(here, SUBLANES - 1, 0),
                jnp.broadcast_to(ahead_x[h, pl.ds(i, 1), :], here.shape),
            )
            vx_out[at] = vx[at] - COURANT * buoyancy[at] * (ahead - here)
        return _

    lax.fori_loop(0, planes, plane, 0, unroll=16)


def ghosts(p, first_x, behind_i, behind_x, ghost_in, ghost_out, ghost_b):
    (vi, vx), (vi_out, vx_out), (bi, bx) = ghost_in, ghost_out, ghost_b
    vi_out[...] = vi[...] - COURANT * bi[...] * (p[0] - behind_i[...])
    vx_out[...] = vx[...] - COURANT * bx[...] * (first_x[...] - behind_x[...])


def pressure(p_in, p_out, v, ghost, modulus, i, tile, first, source):
    lane, row = lane_ids(), row_ids()
    vi, vx, vd = v
    ghost_i, ghost_x = ghost
    here = [vd[i, rows(tile), cols(h)] for h in range(2)]
    turned = [pltpu.roll(x, 1, 1) for x in here]
    upper = [jnp.where(lane > 0, turned[0], 0.0), jnp.where(lane > 0, turned[1], turned[0])]
    for h in range(2):
        at = (i, rows(tile), cols(h))
        before_i = ghost_i[rows(tile), cols(h)] if first else vi[i - 1, rows(tile), cols(h)]
        now_x = vx[at]
        if tile > 0:
            before_x = vx[i, pl.ds(tile * SUBLANES - 1, SUBLANES), cols(h)]
        else:
            before_x = jnp.where(
                row > 0,
                pltpu.roll(now_x, 1, 0),
                jnp.broadcast_to(ghost_x[h, pl.ds(i, 1), :], now_x.shape),
            )
        total = (vi[at] - before_i) + (now_x - before_x) + (here[h] - upper[h])
        if source is not None:
            total = total - source(i, tile, h)
        p_out[at] = p_in[at] - COURANT * modulus[at] * total


def source(injected, wide, step):
    def strip(i, tile, h):
        row = ((i * wide + tile * SUBLANES) * 2 + h) * STEPS + step
        return injected[pl.ds(row, SUBLANES, stride=2 * STEPS), :]

    return strip


def shell(planes, tiles, strip):
    for tile in range(tiles):
        strip(0, tile, True)
        strip(planes - 1, tile, False)

    def plane(i, _):
        strip(i, 0, False)
        strip(i, tiles - 1, False)
        return _

    lax.fori_loop(1, planes - 1, plane, 0, unroll=15)


def core(planes, tiles, strip):
    def plane(i, _):
        for tile in range(1, tiles - 1):
            strip(i, tile, False)
        return _

    lax.fori_loop(1, planes - 1, plane, 0, unroll=6)


def take_row(source, row, target):
    def plane(i, _):
        for h in range(2):
            target[h, pl.ds(i, 1), :] = source[i, pl.ds(row, 1), cols(h)]
        return _

    lax.fori_loop(0, source.shape[0], plane, 0, unroll=16)


class Exchange:
    def __init__(self, send_sems, recv_sems):
        self.send_sems, self.recv_sems = send_sems, recv_sems
        self.place = (lax.axis_index("xline"), lax.axis_index("inline"))
        self.count = (lax.axis_size("xline"), lax.axis_size("inline"))
        self.copies = []

    def has(self, axis, step):
        return self.place[axis] < self.count[axis] - 1 if step > 0 else self.place[axis] > 0

    def partner(self, axis, step):
        there = list(self.place)
        there[axis] = jnp.clip(there[axis] + step, 0, self.count[axis] - 1)
        return tuple(there)

    def greet(self, barrier):
        for axis in range(2):
            for step in (-1, 1):
                @pl.when(self.has(axis, step))
                def _():
                    pl.semaphore_signal(
                        barrier, inc=1, device_id=self.partner(axis, step), device_id_type=MESH
                    )

    def met(self, barrier):
        partners = [self.has(axis, step).astype(jnp.int32) for axis in range(2) for step in (-1, 1)]
        pl.semaphore_wait(barrier, sum(partners))

    def send(self, source, target, axis, step, number):
        copy = pltpu.make_async_remote_copy(
            src_ref=source,
            dst_ref=target,
            send_sem=self.send_sems.at[number],
            recv_sem=self.recv_sems.at[number],
            device_id=self.partner(axis, step),
            device_id_type=MESH,
        )

        @pl.when(self.has(axis, step))
        def _():
            copy.start()

        self.copies.append((copy, axis, step))

    def finish(self):
        for copy, axis, step in self.copies:
            @pl.when(self.has(axis, step))
            def _():
                copy.wait_send()

            @pl.when(self.has(axis, -step))
            def _():
                copy.wait_recv()

        self.copies = []


def split(value):
    high = value.astype(jnp.bfloat16).astype(F32)
    return high, value - high


def dot_t(a, b):
    return lax.dot_general(
        a.astype(jnp.bfloat16),
        b.astype(jnp.bfloat16),
        (((1,), (1,)), ((), ())),
        preferred_element_type=F32,
    )


def pack(traces, owner, cell, resample, devices):
    held = traces.shape[0]
    owner_row = owner[...]
    cell_row = cell[...]
    member = lax.broadcasted_iota(jnp.int32, (devices, held), 0) == owner_row
    member = jnp.where(member, 1.0, 0.0)
    earlier = lax.broadcasted_iota(jnp.int32, (LANES, LANES), 0) < lax.broadcasted_iota(
        jnp.int32, (LANES, LANES), 1
    )
    earlier = jnp.where(earlier, 1.0, 0.0).astype(jnp.bfloat16)
    running = jnp.zeros((devices, 1), F32)
    position = []
    for block in range(held // LANES):
        part = member[:, block * LANES : (block + 1) * LANES]
        before = jnp.dot(part.astype(jnp.bfloat16), earlier, preferred_element_type=F32) + running
        position.append(jnp.sum(part * before, axis=0, keepdims=True))
        running = running + jnp.sum(part, axis=1, keepdims=True)
    position = jnp.concatenate(position, axis=1).astype(jnp.int32)

    steps = resample.shape[0]
    filt = jnp.concatenate([resample[...], jnp.zeros((SLOT - steps, resample.shape[1]), F32)], 0)
    filt_high, filt_low = split(filt)
    trace_high, trace_low = split(traces[...])
    both = dot_t(jnp.concatenate([filt_high, filt_low], 0), trace_high)
    fields = both[:SLOT] + both[SLOT:] + dot_t(filt_high, trace_low)
    kind = lax.broadcasted_iota(jnp.int32, (SLOT, held), 0)
    fields = jnp.where(kind == steps, cell_row.astype(F32), fields)
    first, rest = split(fields)
    second, third = split(rest)
    packed = []
    for piece in (third, second, first):
        spread = [
            jnp.where(position == q, piece, 0.0) for q in range(LANES // SLOT)
        ]
        packed.append(dot_t(member, jnp.concatenate(spread, 0)))
    return (packed[0] + packed[1]) + packed[2]


def route(
    p_hbm, vi_hbm, vx_hbm, vd_hbm, m_hbm, b_hbm, traces_hbm, owner_hbm, cell_hbm, resample_hbm,
    p, vi, vx, vd, modulus, buoyancy, ghost_i, ghost_x, ghost_bi, ghost_bx, index, values, injected,
    outbox, relay, inbox, behind_i, ahead_i, behind_x, ahead_x, from_vi, from_bi, from_vx, from_bx,
    first_x, last_x, last_vx, last_bx,
    traces, owner, cell, resample,
    load_sems, node_sems, send_sems, recv_sems, post_sems, mail_sems,
):
    devices = lax.axis_size("xline") * lax.axis_size("inline")
    lines = lax.axis_size("inline")
    planes, tiles = p.shape[0], p.shape[1] // SUBLANES
    loads = [
        pltpu.make_async_copy(source, target, load_sems.at[k])
        for k, (source, target) in enumerate(
            ((p_hbm, p), (b_hbm, buoyancy), (vi_hbm, vi), (vx_hbm, vx), (vd_hbm, vd), (m_hbm, modulus))
        )
    ]
    node_loads = [
        pltpu.make_async_copy(source, target, node_sems.at[k])
        for k, (source, target) in enumerate(
            ((owner_hbm, owner), (cell_hbm, cell.at[0]), (resample_hbm, resample), (traces_hbm, traces))
        )
    ]
    for load in node_loads + loads:
        load.start()
    barrier = pltpu.get_barrier_semaphore()
    xline, inline = lax.axis_index("xline"), lax.axis_index("inline")
    blocks = lines // NEAR
    groups = devices // NEAR
    group, near = xline * blocks + inline // NEAR, lax.rem(inline, NEAR)

    def far_partner(k):
        there = lax.rem(group + k, groups)
        return there, (there // blocks, lax.rem(there, blocks) * NEAR + near)

    def near_partner(k):
        there = lax.rem(near + k, NEAR)
        return there, (xline, inline - near + there)

    def greet(device):
        pl.semaphore_signal(barrier, inc=1, device_id=device, device_id_type=MESH)

    def greet_far(k, _):
        greet(far_partner(k)[1])
        return _

    def greet_near(k, _):
        greet(near_partner(k)[1])
        return _

    lax.fori_loop(1, groups, greet_far, 0, unroll=True)
    lax.fori_loop(1, NEAR, greet_near, 0, unroll=True)
    crosses = []
    for edge, step, end in ((NEAR - 1, 1, lines - 1), (0, -1, 0)):
        cross = jnp.logical_and(near == edge, inline != end)
        crosses.append(cross.astype(jnp.int32))

        @pl.when(cross)
        def _():
            greet((xline, jnp.clip(inline + step, 0, lines - 1)))

    for load in node_loads:
        load.wait()
    packed = pack(traces, owner, cell, resample, devices)
    for row in range(devices):
        outbox[row] = packed[row : row + 1]
    for row in range(NEAR):
        relay[row, group] = outbox[group * NEAR + row]

    pl.semaphore_wait(barrier, groups - 1 + NEAR - 1 + sum(crosses))

    def post_far(k, _):
        there, device = far_partner(k)
        pltpu.make_async_remote_copy(
            src_ref=outbox.at[pl.ds(there * NEAR, NEAR)],
            dst_ref=relay.at[:, group],
            send_sem=post_sems.at[0],
            recv_sem=mail_sems.at[0],
            device_id=device,
            device_id_type=MESH,
        ).start()
        return _

    lax.fori_loop(1, groups, post_far, 0, unroll=True)

    halo = Exchange(send_sems, recv_sems)
    for ref in (behind_i, from_vi, from_bi):
        @pl.when(jnp.logical_not(halo.has(1, -1)))
        def _():
            ref[...] = jnp.zeros_like(ref)
    for ref in (behind_x, from_vx, from_bx):
        @pl.when(jnp.logical_not(halo.has(0, -1)))
        def _():
            ref[...] = jnp.zeros_like(ref)

    @pl.when(jnp.logical_not(halo.has(1, 1)))
    def _():
        ahead_i[...] = jnp.zeros_like(ahead_i)

    @pl.when(jnp.logical_not(halo.has(0, 1)))
    def _():
        ahead_x[...] = jnp.zeros_like(ahead_x)

    loads[0].wait()
    halo.send(p.at[planes - 1], behind_i, 1, 1, 0)
    halo.send(p.at[0], ahead_i, 1, -1, 1)
    take_row(p, 0, first_x)
    halo.send(first_x, ahead_x, 0, -1, 2)
    take_row(p, p.shape[1] - 1, last_x)
    halo.send(last_x, behind_x, 0, 1, 3)
    loads[1].wait()
    halo.send(buoyancy.at[planes - 1], from_bi, 1, 1, 4)
    take_row(buoyancy, p.shape[1] - 1, last_bx)
    halo.send(last_bx, from_bx, 0, 1, 5)
    loads[2].wait()
    halo.send(vi.at[planes - 1], from_vi, 1, 1, 6)
    loads[3].wait()
    take_row(vx, p.shape[1] - 1, last_vx)
    halo.send(last_vx, from_vx, 0, 1, 7)
    loads[4].wait()
    loads[5].wait()

    v = (vi, vx, vd)
    velocity_inside(p, v, v, buoyancy)

    far_mail = pltpu.make_async_remote_copy(
        src_ref=outbox.at[pl.ds(0, devices - NEAR)],
        dst_ref=relay.at[:, pl.ds(0, groups - 1)],
        send_sem=post_sems.at[0],
        recv_sem=mail_sems.at[0],
        device_id=far_partner(1)[1],
        device_id_type=MESH,
    )
    far_mail.wait_send()
    far_mail.wait_recv()

    def post_near(k, _):
        there, device = near_partner(k)
        pltpu.make_async_remote_copy(
            src_ref=relay.at[there],
            dst_ref=inbox.at[near],
            send_sem=post_sems.at[1],
            recv_sem=mail_sems.at[1],
            device_id=device,
            device_id_type=MESH,
        ).start()
        return _

    lax.fori_loop(1, NEAR, post_near, 0, unroll=True)
    inbox[near] = relay[near]

    def clear(k, _):
        injected[pl.ds(pl.multiple_of(k * 64, 64), 64), :] = jnp.zeros((64, LANES), F32)
        return _

    lax.fori_loop(0, injected.shape[0] // 64, clear, 0)

    halo.finish()
    velocity_edge(p, v, v, buoyancy, ahead_i, ahead_x)
    ghosts(p, first_x, behind_i, behind_x, (from_vi, from_vx), (ghost_i, ghost_x), (from_bi, from_bx))
    ghost_bi[...] = from_bi[...]
    ghost_bx[...] = from_bx[...]

    def strip(i, tile, first):
        pressure(p, p, v, (ghost_i, ghost_x), modulus, i, tile, first, None)

    shell(planes, tiles, strip)
    core(planes, tiles, strip)

    near_mail = pltpu.make_async_remote_copy(
        src_ref=relay.at[pl.ds(0, NEAR - 1)],
        dst_ref=inbox.at[pl.ds(0, NEAR - 1)],
        send_sem=post_sems.at[1],
        recv_sem=mail_sems.at[1],
        device_id=near_partner(1)[1],
        device_id_type=MESH,
    )
    near_mail.wait_send()
    near_mail.wait_recv()
    values[...] = inbox[...].reshape(devices, LANES).T
    index[...] = values[pl.ds(STEPS, LANES // SLOT, stride=SLOT), :].astype(jnp.int32)


def scatter(index_ref, values, _, injected, index, sem):
    load = pltpu.make_async_copy(index_ref, index, sem)
    load.start()
    devices = values.shape[1]
    lane = lax.broadcasted_iota(jnp.int32, (STEPS, LANES), 1)
    slots, group = 15, 3

    def spread(d):
        pick = jnp.full((SUBLANES, LANES), d, jnp.int32)
        return [
            jnp.take_along_axis(values[pl.ds(q * SLOT, SLOT), :], pick, axis=1)[:STEPS]
            for q in range(slots)
        ]

    def sender(d, now):
        later = spread(jnp.minimum(d + 1, devices - 1))
        for start in range(0, slots, group):
            tiles, adds = [], []
            for q in range(start, start + group):
                cell = index[q, d]
                tiles.append(lax.shift_right_logical(cell, 7))
                adds.append(jnp.where(lane == (cell & (LANES - 1)), now[q], 0.0))
            spots = [pl.ds(pl.multiple_of(tile * STEPS, STEPS), STEPS) for tile in tiles]
            old = [injected[spot, :] for spot in spots]
            for b in range(group):
                new = old[b] + adds[b]
                for a in range(b):
                    new = new + jnp.where(tiles[a] == tiles[b], adds[a], 0.0)
                injected[spots[b], :] = new
        return later

    first = spread(0)
    load.wait()
    lax.fori_loop(0, devices, sender, first, unroll=4)


def advance(
    p_in, vi_in, vx_in, vd_in, modulus, buoyancy, ghost_i_in, ghost_x_in, ghost_bi, ghost_bx, injected,
    p, vi, vx, vd, ghost_i, ghost_x,
    behind_i, ahead_i, behind_x, ahead_x, first_x, last_x, send_sems, recv_sems,
):
    planes, tiles = p.shape[0], p.shape[1] // SUBLANES
    halo = Exchange(None, None)
    barrier = pltpu.get_barrier_semaphore()
    halo.greet(barrier)

    @pl.when(jnp.logical_not(halo.has(1, -1)))
    def _():
        behind_i[...] = jnp.zeros_like(behind_i)

    @pl.when(jnp.logical_not(halo.has(0, -1)))
    def _():
        behind_x[...] = jnp.zeros_like(behind_x)

    @pl.when(jnp.logical_not(halo.has(1, 1)))
    def _():
        ahead_i[...] = jnp.zeros_like(ahead_i)

    @pl.when(jnp.logical_not(halo.has(0, 1)))
    def _():
        ahead_x[...] = jnp.zeros_like(ahead_x)

    def send(step):
        halo.send_sems, halo.recv_sems = send_sems.at[step], recv_sems.at[step]
        halo.send(p.at[planes - 1], behind_i.at[step], 1, 1, 0)
        halo.send(p.at[0], ahead_i.at[step], 1, -1, 1)
        take_row(p, 0, first_x.at[step])
        halo.send(first_x.at[step], ahead_x.at[step], 0, -1, 2)
        take_row(p, p.shape[1] - 1, last_x.at[step])
        halo.send(last_x.at[step], behind_x.at[step], 0, 1, 3)

    def inject(i, tile, first):
        del first
        spread = source(injected, p.shape[1], 0)
        for h in range(2):
            at = (i, rows(tile), cols(h))
            p[at] = p_in[at] + COURANT * modulus[at] * spread(i, tile, h)

    shell(planes, tiles, inject)
    halo.met(barrier)
    send(0)
    core(planes, tiles, inject)

    v = (vi, vx, vd)
    for step in range(1, STEPS):
        v_in = (vi_in, vx_in, vd_in) if step == 1 else v
        ghost_in = (ghost_i_in, ghost_x_in) if step == 1 else (ghost_i, ghost_x)
        velocity_inside(p, v_in, v, buoyancy)
        halo.finish()
        velocity_edge(p, v_in, v, buoyancy, ahead_i.at[step - 1], ahead_x.at[step - 1])
        ghosts(
            p, first_x.at[step - 1], behind_i.at[step - 1], behind_x.at[step - 1],
            ghost_in, (ghost_i, ghost_x), (ghost_bi, ghost_bx),
        )

        if step == STEPS - 1:
            break
        spread = source(injected, p.shape[1], step)

        def strip(i, tile, first):
            pressure(p, p, v, (ghost_i, ghost_x), modulus, i, tile, first, spread)

        shell(planes, tiles, strip)
        send(step)
        core(planes, tiles, strip)


def finish(
    p_in, vi, vx, vd, ghost_i, ghost_x, modulus, injected,
    p_out, vi_out, vx_out, vd_out,
    p, sems,
):
    planes, tiles = p_in.shape[0], p_in.shape[1] // SUBLANES
    copies = [
        pltpu.make_async_copy(source, target, sems.at[k])
        for k, (source, target) in enumerate(((vi, vi_out), (vx, vx_out), (vd, vd_out)))
    ]
    for copy in copies:
        copy.start()
    spread = source(injected, p_in.shape[1], STEPS - 1)
    v, ghost = (vi, vx, vd), (ghost_i, ghost_x)
    chunks = 4
    size = planes // chunks

    def plane(i, _):
        for tile in range(tiles):
            pressure(p_in, p, v, ghost, modulus, i, tile, False, spread)
        return _

    for chunk in range(chunks):
        start = chunk * size
        if chunk == 0:
            for tile in range(tiles):
                pressure(p_in, p, v, ghost, modulus, 0, tile, True, spread)
        lax.fori_loop(max(start, 1), start + size, plane, 0, unroll=size if chunk else size - 1)
        part = pl.ds(start, size)
        copies.append(pltpu.make_async_copy(p.at[part], p_out.at[part], sems.at[3 + chunk]))
        copies[-1].start()
    for copy in copies:
        copy.wait()


def shards(
    pressure_in, vel_inline, vel_xline, vel_depth, modulus, buoyancy, traces, owner, node_cell, resample
):
    planes, wide, deep = pressure_in.shape
    devices = lax.axis_size("xline") * lax.axis_size("inline")
    held = traces.shape[0]
    field = (planes, wide, deep)
    plane, column = (wide, deep), (2, planes, LANES)
    injection = (planes * wide * deep // LANES * STEPS, LANES)
    vmem = pl.BlockSpec(memory_space=VMEM)
    hbm = pl.BlockSpec(memory_space=HBM)
    dma = pltpu.SemaphoreType.DMA

    state = pl.pallas_call(
        route,
        out_shape=[VMEM(field, F32)] * 6
        + [VMEM(plane, F32), VMEM(column, F32)] * 2
        + [VMEM((LANES // SLOT, devices), jnp.int32), VMEM((LANES, devices), F32), VMEM(injection, F32)],
        in_specs=[hbm] * 10,
        out_specs=[vmem] * 13,
        scratch_shapes=[VMEM((devices, 1, LANES), F32)]
        + [VMEM((NEAR, devices // NEAR, 1, LANES), F32)] * 2
        + [VMEM(plane, F32)] * 2
        + [VMEM(column, F32)] * 2
        + [VMEM(plane, F32)] * 2
        + [VMEM(column, F32)] * 6
        + [
            VMEM(traces.shape, F32), VMEM((1, held), jnp.int32), VMEM((1, held), jnp.int32),
            VMEM(resample.shape, F32),
        ]
        + [dma((6,)), dma((4,)), dma((8,)), dma((8,)), dma((2,)), dma((2,))],
        compiler_params=pltpu.CompilerParams(collective_id=0, has_side_effects=True, vmem_limit_bytes=LIMIT),
        name="route",
    )(
        *(
            pltpu.with_memory_space_constraint(x, HBM)
            for x in (
                pressure_in, vel_inline, vel_xline, vel_depth, modulus, buoyancy,
                traces, owner.reshape(1, held), node_cell, resample,
            )
        )
    )
    *fields, index, values, cleared = state
    injected = pl.pallas_call(
        scatter,
        out_shape=VMEM(injection, F32),
        in_specs=[vmem] * 3,
        out_specs=vmem,
        scratch_shapes=[pltpu.SMEM((LANES // SLOT, devices), jnp.int32), dma],
        input_output_aliases={2: 0},
        compiler_params=pltpu.CompilerParams(vmem_limit_bytes=LIMIT),
        name="scatter",
    )(index, values, cleared)
    rounds = STEPS - 1
    *fields, ghost_i, ghost_x = pl.pallas_call(
        advance,
        out_shape=[VMEM(field, F32)] * 4 + [VMEM(plane, F32), VMEM(column, F32)],
        in_specs=[vmem] * 11,
        out_specs=[vmem] * 6,
        scratch_shapes=[VMEM((rounds, *plane), F32)] * 2
        + [VMEM((rounds, *column), F32)] * 4
        + [dma((rounds, 4)), dma((rounds, 4))],
        compiler_params=pltpu.CompilerParams(
            collective_id=1, has_side_effects=True, vmem_limit_bytes=LIMIT
        ),
        name="advance",
    )(*fields, injected)
    modulus = state[4]
    return pl.pallas_call(
        finish,
        out_shape=[HBM(field, F32)] * 4,
        in_specs=[vmem] * 8,
        out_specs=[hbm] * 4,
        scratch_shapes=[VMEM(field, F32), dma((7,))],
        compiler_params=pltpu.CompilerParams(vmem_limit_bytes=LIMIT),
        name="finish",
    )(*fields, ghost_i, ghost_x, modulus, injected)


def solution(mesh):
    field = P("inline", "xline", None)
    nodes = ("xline", "inline")
    return jax.shard_map(
        shards,
        mesh=mesh,
        in_specs=(field,) * 6 + (P(nodes, None), P(nodes, None), P(nodes), P()),
        out_specs=(field,) * 4,
        check_vma=False,
    )
```

```python
import jax
import jax.numpy as jnp
from jax import lax
from jax.experimental import pallas as pl
from jax.experimental.pallas import tpu as pltpu
from jax.sharding import PartitionSpec as P

COURANT = 0.35
STEPS = 4
LANES = 128
SUBLANES = 8
SLOT = 8
NEAR = 8
MESH = pl.DeviceIdType.MESH
VMEM, HBM = pltpu.MemorySpace.VMEM, pltpu.MemorySpace.HBM
F32 = jnp.float32
LIMIT = 16 * 2**20


def lane_ids():
    return lax.broadcasted_iota(jnp.int32, (SUBLANES, LANES), 1)


def row_ids():
    return lax.broadcasted_iota(jnp.int32, (SUBLANES, LANES), 0)


def cols(half):
    return pl.ds(half * LANES, LANES)


def rows(tile):
    return pl.ds(tile * SUBLANES, SUBLANES)


def velocity(p, v_in, v_out, buoyancy, i, tile, next_plane):
    lane = lane_ids()
    (vi, vx, vd), (vi_out, vx_out, vd_out) = v_in, v_out
    here = [p[i, rows(tile), cols(h)] for h in range(2)]
    turned = [pltpu.roll(x, LANES - 1, 1) for x in here]
    deeper = [jnp.where(lane < LANES - 1, turned[0], turned[1]), jnp.where(lane < LANES - 1, turned[1], 0.0)]
    last = p.shape[1] // SUBLANES - 1
    for h in range(2):
        rb = COURANT * buoyancy[i, rows(tile), cols(h)]
        vd_out[i, rows(tile), cols(h)] = vd[i, rows(tile), cols(h)] - rb * (deeper[h] - here[h])
        if next_plane:
            ahead = p[i + 1, rows(tile), cols(h)]
            vi_out[i, rows(tile), cols(h)] = vi[i, rows(tile), cols(h)] - rb * (ahead - here[h])
        if tile < last:
            ahead = p[i, pl.ds(tile * SUBLANES + 1, SUBLANES), cols(h)]
            vx_out[i, rows(tile), cols(h)] = vx[i, rows(tile), cols(h)] - rb * (ahead - here[h])


def velocity_inside(p, v_in, v_out, buoyancy):
    planes, tiles = p.shape[0], p.shape[1] // SUBLANES

    def plane(i, _):
        for tile in range(tiles):
            velocity(p, v_in, v_out, buoyancy, i, tile, True)
        return _

    lax.fori_loop(0, planes - 1, plane, 0, unroll=6)
    for tile in range(tiles):
        velocity(p, v_in, v_out, buoyancy, planes - 1, tile, False)


def velocity_next(p, v_in, v_out, buoyancy, ahead_i):
    planes, tiles = p.shape[0], p.shape[1] // SUBLANES
    for tile in range(tiles):
        for h in range(2):
            at = (planes - 1, rows(tile), cols(h))
            v_out[0][at] = v_in[0][at] - COURANT * buoyancy[at] * (ahead_i[rows(tile), cols(h)] - p[at])


def velocity_side(p, v_in, v_out, buoyancy, ahead_x, i):
    row = row_ids()
    for h in range(2):
        at = (i, rows(p.shape[1] // SUBLANES - 1), cols(h))
        here = p[at]
        ahead = jnp.where(
            row < SUBLANES - 1,
            pltpu.roll(here, SUBLANES - 1, 0),
            jnp.broadcast_to(ahead_x[h, pl.ds(i, 1), :], here.shape),
        )
        v_out[1][at] = v_in[1][at] - COURANT * buoyancy[at] * (ahead - here)


def between(planes, work, unroll):
    def plane(i, _):
        work(i)
        return _

    lax.fori_loop(1, planes - 1, plane, 0, unroll=unroll)


def ghosts(p, first_x, behind_i, behind_x, ghost_in, ghost_out, ghost_b):
    (vi, vx), (vi_out, vx_out), (bi, bx) = ghost_in, ghost_out, ghost_b
    vi_out[...] = vi[...] - COURANT * bi[...] * (p[0] - behind_i[...])
    vx_out[...] = vx[...] - COURANT * bx[...] * (first_x[...] - behind_x[...])


def pressure(p_in, p_out, v, ghost, modulus, i, tile, first, source):
    lane, row = lane_ids(), row_ids()
    vi, vx, vd = v
    ghost_i, ghost_x = ghost
    here = [vd[i, rows(tile), cols(h)] for h in range(2)]
    turned = [pltpu.roll(x, 1, 1) for x in here]
    upper = [jnp.where(lane > 0, turned[0], 0.0), jnp.where(lane > 0, turned[1], turned[0])]
    for h in range(2):
        at = (i, rows(tile), cols(h))
        before_i = ghost_i[rows(tile), cols(h)] if first else vi[i - 1, rows(tile), cols(h)]
        now_x = vx[at]
        if tile > 0:
            before_x = vx[i, pl.ds(tile * SUBLANES - 1, SUBLANES), cols(h)]
        else:
            before_x = jnp.where(
                row > 0,
                pltpu.roll(now_x, 1, 0),
                jnp.broadcast_to(ghost_x[h, pl.ds(i, 1), :], now_x.shape),
            )
        total = (vi[at] - before_i) + (now_x - before_x) + (here[h] - upper[h])
        if source is not None:
            total = total - source(i, tile, h)
        p_out[at] = p_in[at] - COURANT * modulus[at] * total


def source(injected, wide, step):
    def strip(i, tile, h):
        row = ((i * wide + tile * SUBLANES) * 2 + h) * STEPS + step
        return injected[pl.ds(row, SUBLANES, stride=2 * STEPS), :]

    return strip


def ends(planes, tiles, strip):
    for tile in range(tiles):
        strip(0, tile, True)
        strip(planes - 1, tile, False)


def sides(planes, tiles, strip):
    def work(i):
        strip(i, 0, False)
        strip(i, tiles - 1, False)

    between(planes, work, 15)


def core(planes, tiles, strip):
    def work(i):
        for tile in range(1, tiles - 1):
            strip(i, tile, False)

    between(planes, work, 6)


def take_row(source, row, target):
    def plane(i, _):
        for h in range(2):
            target[h, pl.ds(i, 1), :] = source[i, pl.ds(row, 1), cols(h)]
        return _

    lax.fori_loop(0, source.shape[0], plane, 0, unroll=16)


class Exchange:
    def __init__(self, send_sems, recv_sems):
        self.send_sems, self.recv_sems = send_sems, recv_sems
        self.place = (lax.axis_index("xline"), lax.axis_index("inline"))
        self.count = (lax.axis_size("xline"), lax.axis_size("inline"))
        self.copies = []

    def has(self, axis, step):
        return self.place[axis] < self.count[axis] - 1 if step > 0 else self.place[axis] > 0

    def partner(self, axis, step):
        there = list(self.place)
        there[axis] = jnp.clip(there[axis] + step, 0, self.count[axis] - 1)
        return tuple(there)

    def greet(self, barrier):
        for axis in range(2):
            for step in (-1, 1):
                @pl.when(self.has(axis, step))
                def _():
                    pl.semaphore_signal(
                        barrier, inc=1, device_id=self.partner(axis, step), device_id_type=MESH
                    )

    def met(self, barrier):
        partners = [self.has(axis, step).astype(jnp.int32) for axis in range(2) for step in (-1, 1)]
        pl.semaphore_wait(barrier, sum(partners))

    def send(self, source, target, axis, step, number):
        copy = pltpu.make_async_remote_copy(
            src_ref=source,
            dst_ref=target,
            send_sem=self.send_sems.at[number],
            recv_sem=self.recv_sems.at[number],
            device_id=self.partner(axis, step),
            device_id_type=MESH,
        )

        @pl.when(self.has(axis, step))
        def _():
            copy.start()

        self.copies.append((copy, axis, step))

    def finish(self):
        for copy, axis, step in self.copies:
            @pl.when(self.has(axis, step))
            def _():
                copy.wait_send()

            @pl.when(self.has(axis, -step))
            def _():
                copy.wait_recv()

        self.copies = []


def split(value):
    high = value.astype(jnp.bfloat16).astype(F32)
    return high, value - high


def dot_t(a, b):
    return lax.dot_general(
        a.astype(jnp.bfloat16),
        b.astype(jnp.bfloat16),
        (((1,), (1,)), ((), ())),
        preferred_element_type=F32,
    )


def pack(traces, owner, cell, resample, devices):
    held = traces.shape[0]
    owner_row = owner[...]
    cell_row = cell[...]
    member = lax.broadcasted_iota(jnp.int32, (devices, held), 0) == owner_row
    member = jnp.where(member, 1.0, 0.0)
    earlier = lax.broadcasted_iota(jnp.int32, (LANES, LANES), 0) < lax.broadcasted_iota(
        jnp.int32, (LANES, LANES), 1
    )
    earlier = jnp.where(earlier, 1.0, 0.0).astype(jnp.bfloat16)
    running = jnp.zeros((devices, 1), F32)
    position = []
    for block in range(held // LANES):
        part = member[:, block * LANES : (block + 1) * LANES]
        before = jnp.dot(part.astype(jnp.bfloat16), earlier, preferred_element_type=F32) + running
        position.append(jnp.sum(part * before, axis=0, keepdims=True))
        running = running + jnp.sum(part, axis=1, keepdims=True)
    position = jnp.concatenate(position, axis=1).astype(jnp.int32)

    steps = resample.shape[0]
    filt = jnp.concatenate([resample[...], jnp.zeros((SLOT - steps, resample.shape[1]), F32)], 0)
    filt_high, filt_low = split(filt)
    trace_high, trace_low = split(traces[...])
    both = dot_t(jnp.concatenate([filt_high, filt_low], 0), trace_high)
    fields = both[:SLOT] + both[SLOT:] + dot_t(filt_high, trace_low)
    kind = lax.broadcasted_iota(jnp.int32, (SLOT, held), 0)
    fields = jnp.where(kind == steps, cell_row.astype(F32), fields)
    first, rest = split(fields)
    second, third = split(rest)
    packed = []
    for piece in (third, second, first):
        spread = [
            jnp.where(position == q, piece, 0.0) for q in range(LANES // SLOT)
        ]
        packed.append(dot_t(member, jnp.concatenate(spread, 0)))
    return (packed[0] + packed[1]) + packed[2]


def route(
    p_hbm, vi_hbm, vx_hbm, vd_hbm, m_hbm, b_hbm, traces_hbm, owner_hbm, cell_hbm, resample_hbm,
    p, vi, vx, vd, modulus, buoyancy, ghost_i, ghost_x, ghost_bi, ghost_bx, index, values, injected,
    outbox, inbox, behind_i, ahead_i, behind_x, ahead_x, from_vi, from_bi, from_vx, from_bx,
    first_x, last_x, last_vx, last_bx,
    traces, owner, cell, resample,
    load_sems, node_sems, send_sems, recv_sems, post_sem, mail_sem, all_in,
):
    devices = lax.axis_size("xline") * lax.axis_size("inline")
    lines = lax.axis_size("inline")
    planes, tiles = p.shape[0], p.shape[1] // SUBLANES
    loads = [
        pltpu.make_async_copy(source, target, load_sems.at[k])
        for k, (source, target) in enumerate(
            ((p_hbm, p), (b_hbm, buoyancy), (vi_hbm, vi), (vx_hbm, vx), (vd_hbm, vd), (m_hbm, modulus))
        )
    ]
    node_loads = [
        pltpu.make_async_copy(source, target, node_sems.at[k])
        for k, (source, target) in enumerate(
            ((owner_hbm, owner), (cell_hbm, cell.at[0]), (resample_hbm, resample), (traces_hbm, traces))
        )
    ]
    for load in node_loads + loads:
        load.start()
    barrier = pltpu.get_barrier_semaphore()
    xline, inline = lax.axis_index("xline"), lax.axis_index("inline")
    wide, blocks = lax.axis_size("xline"), lines // NEAR
    block, near = inline // NEAR, lax.rem(inline, NEAR)
    me = xline * lines + inline
    near_offsets = range(1, NEAR)
    far_offsets = [(dx, dy) for dx in range(wide) for dy in range(blocks) if dx or dy]

    def partner(dx, dy, dn):
        return (lax.rem(xline + dx, wide), lax.rem(block + dy, blocks) * NEAR + lax.rem(near + dn, NEAR))

    def greet(semaphore, offsets):
        for offset in offsets:
            pl.semaphore_signal(
                semaphore, inc=1, device_id=partner(*offset), device_id_type=MESH
            )

    beside = [(0, 0, dn) for dn in near_offsets]
    greet(barrier, beside + [(dx, dy, 0) for dx, dy in far_offsets])

    for load in node_loads:
        load.wait()
    pl.semaphore_wait(barrier, len(beside) + len(far_offsets))
    greet(all_in, beside)
    packed = pack(traces, owner, cell, resample, devices)
    for row in range(devices):
        outbox[row] = packed[row : row + 1]
    inbox[me] = outbox[me]
    pl.semaphore_wait(all_in, len(beside))

    def hops(offset, length):
        return min(offset, length - offset)

    def post(dx, dy, dn):
        device = partner(dx, dy, dn)
        pltpu.make_async_remote_copy(
            src_ref=outbox.at[device[0] * lines + device[1]],
            dst_ref=inbox.at[me],
            send_sem=post_sem,
            recv_sem=mail_sem,
            device_id=device,
            device_id_type=MESH,
        ).start()

    for dx, dy in sorted(
        [(0, 0)] + far_offsets, key=lambda o: -(hops(o[0], wide) + hops(o[1], blocks))
    ):
        def post_near(k, _):
            post(dx, dy, lax.rem(k + 3, NEAR))
            return _

        own = int(dx == 0 and dy == 0)
        lax.fori_loop(0, NEAR - own, post_near if not own else lambda k, _: (post(0, 0, k + 1), _)[1], 0)

    halo = Exchange(send_sems, recv_sems)
    for ref in (behind_i, from_vi, from_bi):
        @pl.when(jnp.logical_not(halo.has(1, -1)))
        def _():
            ref[...] = jnp.zeros_like(ref)
    for ref in (behind_x, from_vx, from_bx):
        @pl.when(jnp.logical_not(halo.has(0, -1)))
        def _():
            ref[...] = jnp.zeros_like(ref)

    @pl.when(jnp.logical_not(halo.has(1, 1)))
    def _():
        ahead_i[...] = jnp.zeros_like(ahead_i)

    @pl.when(jnp.logical_not(halo.has(0, 1)))
    def _():
        ahead_x[...] = jnp.zeros_like(ahead_x)

    loads[0].wait()
    halo.send(p.at[planes - 1], behind_i, 1, 1, 0)
    halo.send(p.at[0], ahead_i, 1, -1, 1)
    take_row(p, 0, first_x)
    halo.send(first_x, ahead_x, 0, -1, 2)
    take_row(p, p.shape[1] - 1, last_x)
    halo.send(last_x, behind_x, 0, 1, 3)
    loads[1].wait()
    halo.send(buoyancy.at[planes - 1], from_bi, 1, 1, 4)
    take_row(buoyancy, p.shape[1] - 1, last_bx)
    halo.send(last_bx, from_bx, 0, 1, 5)
    loads[2].wait()
    halo.send(vi.at[planes - 1], from_vi, 1, 1, 6)
    loads[3].wait()
    take_row(vx, p.shape[1] - 1, last_vx)
    halo.send(last_vx, from_vx, 0, 1, 7)
    loads[4].wait()
    loads[5].wait()

    v = (vi, vx, vd)
    velocity_inside(p, v, v, buoyancy)

    def clear(k, _):
        injected[pl.ds(pl.multiple_of(k * 64, 64), 64), :] = jnp.zeros((64, LANES), F32)
        return _

    lax.fori_loop(0, injected.shape[0] // 64, clear, 0)

    halo.finish()
    velocity_next(p, v, v, buoyancy, ahead_i)
    for i in (0, planes - 1):
        velocity_side(p, v, v, buoyancy, ahead_x, i)
    between(planes, lambda i: velocity_side(p, v, v, buoyancy, ahead_x, i), 15)
    ghosts(p, first_x, behind_i, behind_x, (from_vi, from_vx), (ghost_i, ghost_x), (from_bi, from_bx))
    ghost_bi[...] = from_bi[...]
    ghost_bx[...] = from_bx[...]

    def strip(i, tile, first):
        pressure(p, p, v, (ghost_i, ghost_x), modulus, i, tile, first, None)

    ends(planes, tiles, strip)
    sides(planes, tiles, strip)
    core(planes, tiles, strip)

    mail = pltpu.make_async_remote_copy(
        src_ref=outbox.at[pl.ds(0, devices - 1)],
        dst_ref=inbox.at[pl.ds(0, devices - 1)],
        send_sem=post_sem,
        recv_sem=mail_sem,
        device_id=partner(0, 0, 1),
        device_id_type=MESH,
    )
    mail.wait_send()
    mail.wait_recv()
    values[...] = inbox[...].reshape(devices, LANES).T
    index[...] = values[pl.ds(STEPS, LANES // SLOT, stride=SLOT), :].astype(jnp.int32)


def scatter(index_ref, values, _, injected, index, sem):
    load = pltpu.make_async_copy(index_ref, index, sem)
    load.start()
    devices = values.shape[1]
    lane = lax.broadcasted_iota(jnp.int32, (STEPS, LANES), 1)
    slots, group = 15, 3

    def spread(d):
        pick = jnp.full((SUBLANES, LANES), d, jnp.int32)
        return [
            jnp.take_along_axis(values[pl.ds(q * SLOT, SLOT), :], pick, axis=1)[:STEPS]
            for q in range(slots)
        ]

    def sender(d, now):
        later = spread(jnp.minimum(d + 1, devices - 1))
        for start in range(0, slots, group):
            tiles, adds = [], []
            for q in range(start, start + group):
                cell = index[q, d]
                tiles.append(lax.shift_right_logical(cell, 7))
                adds.append(jnp.where(lane == (cell & (LANES - 1)), now[q], 0.0))
            spots = [pl.ds(pl.multiple_of(tile * STEPS, STEPS), STEPS) for tile in tiles]
            old = [injected[spot, :] for spot in spots]
            for b in range(group):
                new = old[b] + adds[b]
                for a in range(b):
                    new = new + jnp.where(tiles[a] == tiles[b], adds[a], 0.0)
                injected[spots[b], :] = new
        return later

    first = spread(0)
    load.wait()
    lax.fori_loop(0, devices, sender, first, unroll=4)


def advance(
    p_in, vi_in, vx_in, vd_in, modulus, buoyancy, ghost_i_in, ghost_x_in, ghost_bi, ghost_bx, injected,
    p, vi, vx, vd, ghost_i, ghost_x,
    behind_i, ahead_i, behind_x, ahead_x, first_x, last_x, send_sems, recv_sems,
):
    planes, tiles = p.shape[0], p.shape[1] // SUBLANES
    halo = Exchange(None, None)
    barrier = pltpu.get_barrier_semaphore()
    halo.greet(barrier)

    @pl.when(jnp.logical_not(halo.has(1, -1)))
    def _():
        behind_i[...] = jnp.zeros_like(behind_i)

    @pl.when(jnp.logical_not(halo.has(0, -1)))
    def _():
        behind_x[...] = jnp.zeros_like(behind_x)

    @pl.when(jnp.logical_not(halo.has(1, 1)))
    def _():
        ahead_i[...] = jnp.zeros_like(ahead_i)

    @pl.when(jnp.logical_not(halo.has(0, 1)))
    def _():
        ahead_x[...] = jnp.zeros_like(ahead_x)

    def send_planes(step):
        halo.send_sems, halo.recv_sems = send_sems.at[step], recv_sems.at[step]
        halo.send(p.at[planes - 1], behind_i.at[step], 1, 1, 0)
        halo.send(p.at[0], ahead_i.at[step], 1, -1, 1)

    def send_rows(step):
        take_row(p, 0, first_x.at[step])
        halo.send(first_x.at[step], ahead_x.at[step], 0, -1, 2)
        take_row(p, p.shape[1] - 1, last_x.at[step])
        halo.send(last_x.at[step], behind_x.at[step], 0, 1, 3)

    def inject(i, tile, first):
        del first
        spread = source(injected, p.shape[1], 0)
        for h in range(2):
            at = (i, rows(tile), cols(h))
            p[at] = p_in[at] + COURANT * modulus[at] * spread(i, tile, h)

    ends(planes, tiles, inject)
    halo.met(barrier)
    send_planes(0)
    sides(planes, tiles, inject)
    send_rows(0)
    core(planes, tiles, inject)

    v = (vi, vx, vd)
    for step in range(1, STEPS):
        last = step == STEPS - 1
        v_in = (vi_in, vx_in, vd_in) if step == 1 else v
        ghost_in = (ghost_i_in, ghost_x_in) if step == 1 else (ghost_i, ghost_x)
        spread = source(injected, p.shape[1], step)

        def strip(i, tile, first):
            pressure(p, p, v, (ghost_i, ghost_x), modulus, i, tile, first, spread)

        velocity_inside(p, v_in, v, buoyancy)
        if last:
            core(planes, tiles, strip)
        halo.finish()

        def side(i):
            velocity_side(p, v_in, v, buoyancy, ahead_x.at[step - 1], i)

        velocity_next(p, v_in, v, buoyancy, ahead_i.at[step - 1])
        side(0)
        side(planes - 1)
        ghosts(
            p, first_x.at[step - 1], behind_i.at[step - 1], behind_x.at[step - 1],
            ghost_in, (ghost_i, ghost_x), (ghost_bi, ghost_bx),
        )
        if not last:
            ends(planes, tiles, strip)
            send_planes(step)
        between(planes, side, 15)
        if not last:
            sides(planes, tiles, strip)
            send_rows(step)
            core(planes, tiles, strip)


def finish(
    p_in, vi, vx, vd, ghost_i, ghost_x, modulus, injected,
    p_out, vi_out, vx_out, vd_out,
    p, sems,
):
    planes, tiles = p_in.shape[0], p_in.shape[1] // SUBLANES
    copies = []

    def leave(source_ref, target):
        copies.append(pltpu.make_async_copy(source_ref, target, sems.at[len(copies)]))
        copies[-1].start()

    for source_ref, target in ((vi, vi_out), (vx, vx_out), (vd, vd_out)):
        leave(source_ref, target)
    inner = pl.ds(1, planes - 2)
    middle = (inner, pl.ds(SUBLANES, (tiles - 2) * SUBLANES))
    leave(p_in.at[middle], p_out.at[middle])
    spread = source(injected, p_in.shape[1], STEPS - 1)

    def strip(i, tile, first):
        pressure(p_in, p, (vi, vx, vd), (ghost_i, ghost_x), modulus, i, tile, first, spread)

    ends(planes, tiles, strip)
    for end in (0, planes - 1):
        leave(p.at[end], p_out.at[end])
    sides(planes, tiles, strip)
    for tile in (0, tiles - 1):
        side = (inner, rows(tile))
        leave(p.at[side], p_out.at[side])
    for copy in copies:
        copy.wait()


def shards(
    pressure_in, vel_inline, vel_xline, vel_depth, modulus, buoyancy, traces, owner, node_cell, resample
):
    planes, wide, deep = pressure_in.shape
    devices = lax.axis_size("xline") * lax.axis_size("inline")
    held = traces.shape[0]
    field = (planes, wide, deep)
    plane, column = (wide, deep), (2, planes, LANES)
    injection = (planes * wide * deep // LANES * STEPS, LANES)
    vmem = pl.BlockSpec(memory_space=VMEM)
    hbm = pl.BlockSpec(memory_space=HBM)
    dma = pltpu.SemaphoreType.DMA

    state = pl.pallas_call(
        route,
        out_shape=[VMEM(field, F32)] * 6
        + [VMEM(plane, F32), VMEM(column, F32)] * 2
        + [VMEM((LANES // SLOT, devices), jnp.int32), VMEM((LANES, devices), F32), VMEM(injection, F32)],
        in_specs=[hbm] * 10,
        out_specs=[vmem] * 13,
        scratch_shapes=[VMEM((devices, 1, LANES), F32)] * 2
        + [VMEM(plane, F32)] * 2
        + [VMEM(column, F32)] * 2
        + [VMEM(plane, F32)] * 2
        + [VMEM(column, F32)] * 6
        + [
            VMEM(traces.shape, F32), VMEM((1, held), jnp.int32), VMEM((1, held), jnp.int32),
            VMEM(resample.shape, F32),
        ]
        + [dma((6,)), dma((4,)), dma((8,)), dma((8,)), dma, dma, pltpu.SemaphoreType.REGULAR],
        compiler_params=pltpu.CompilerParams(collective_id=0, has_side_effects=True, vmem_limit_bytes=LIMIT),
        name="route",
    )(
        *(
            pltpu.with_memory_space_constraint(x, HBM)
            for x in (
                pressure_in, vel_inline, vel_xline, vel_depth, modulus, buoyancy,
                traces, owner.reshape(1, held), node_cell, resample,
            )
        )
    )
    *fields, index, values, cleared = state
    injected = pl.pallas_call(
        scatter,
        out_shape=VMEM(injection, F32),
        in_specs=[vmem] * 3,
        out_specs=vmem,
        scratch_shapes=[pltpu.SMEM((LANES // SLOT, devices), jnp.int32), dma],
        input_output_aliases={2: 0},
        compiler_params=pltpu.CompilerParams(vmem_limit_bytes=LIMIT),
        name="scatter",
    )(index, values, cleared)
    rounds = STEPS - 1
    *fields, ghost_i, ghost_x = pl.pallas_call(
        advance,
        out_shape=[VMEM(field, F32)] * 4 + [VMEM(plane, F32), VMEM(column, F32)],
        in_specs=[vmem] * 11,
        out_specs=[vmem] * 6,
        scratch_shapes=[VMEM((rounds, *plane), F32)] * 2
        + [VMEM((rounds, *column), F32)] * 4
        + [dma((rounds, 4)), dma((rounds, 4))],
        compiler_params=pltpu.CompilerParams(
            collective_id=1, has_side_effects=True, vmem_limit_bytes=LIMIT
        ),
        name="advance",
    )(*fields, injected)
    modulus = state[4]
    return pl.pallas_call(
        finish,
        out_shape=[HBM(field, F32)] * 4,
        in_specs=[vmem] * 8,
        out_specs=[hbm] * 4,
        scratch_shapes=[VMEM(field, F32), dma((8,))],
        compiler_params=pltpu.CompilerParams(vmem_limit_bytes=LIMIT),
        name="finish",
    )(*fields, ghost_i, ghost_x, modulus, injected)


def solution(mesh):
    field = P("inline", "xline", None)
    nodes = ("xline", "inline")
    return jax.shard_map(
        shards,
        mesh=mesh,
        in_specs=(field,) * 6 + (P(nodes, None), P(nodes, None), P(nodes), P()),
        out_specs=(field,) * 4,
        check_vma=False,
    )
```

```python
import jax
import jax.numpy as jnp
from jax import lax
from jax.experimental import pallas as pl
from jax.experimental.pallas import tpu as pltpu
from jax.sharding import PartitionSpec as P

COURANT = 0.35
STEPS = 4
LANES = 128
SUBLANES = 8
SLOT = 8
NEAR = 8
MESH = pl.DeviceIdType.MESH
VMEM, HBM = pltpu.MemorySpace.VMEM, pltpu.MemorySpace.HBM
F32 = jnp.float32
MIB = 2**20


def lane_ids():
    return lax.broadcasted_iota(jnp.int32, (SUBLANES, LANES), 1)


def row_ids():
    return lax.broadcasted_iota(jnp.int32, (SUBLANES, LANES), 0)


def cols(half):
    return pl.ds(half * LANES, LANES)


def rows(tile):
    return pl.ds(tile * SUBLANES, SUBLANES)


def velocity(p, v_in, v_out, buoyancy, i, tile, next_plane):
    lane = lane_ids()
    (vi, vx, vd), (vi_out, vx_out, vd_out) = v_in, v_out
    here = [p[i, rows(tile), cols(h)] for h in range(2)]
    turned = [pltpu.roll(x, LANES - 1, 1) for x in here]
    deeper = [jnp.where(lane < LANES - 1, turned[0], turned[1]), jnp.where(lane < LANES - 1, turned[1], 0.0)]
    last = p.shape[1] // SUBLANES - 1
    for h in range(2):
        rb = COURANT * buoyancy[i, rows(tile), cols(h)]
        vd_out[i, rows(tile), cols(h)] = vd[i, rows(tile), cols(h)] - rb * (deeper[h] - here[h])
        if next_plane:
            ahead = p[i + 1, rows(tile), cols(h)]
            vi_out[i, rows(tile), cols(h)] = vi[i, rows(tile), cols(h)] - rb * (ahead - here[h])
        if tile < last:
            ahead = p[i, pl.ds(tile * SUBLANES + 1, SUBLANES), cols(h)]
            vx_out[i, rows(tile), cols(h)] = vx[i, rows(tile), cols(h)] - rb * (ahead - here[h])


def velocity_inside(p, v_in, v_out, buoyancy):
    planes, tiles = p.shape[0], p.shape[1] // SUBLANES

    def plane(i, _):
        for tile in range(tiles):
            velocity(p, v_in, v_out, buoyancy, i, tile, True)
        return _

    lax.fori_loop(0, planes - 1, plane, 0, unroll=6)
    for tile in range(tiles):
        velocity(p, v_in, v_out, buoyancy, planes - 1, tile, False)


def velocity_next(p, v_in, v_out, buoyancy, ahead_i):
    planes, tiles = p.shape[0], p.shape[1] // SUBLANES
    for tile in range(tiles):
        for h in range(2):
            at = (planes - 1, rows(tile), cols(h))
            v_out[0][at] = v_in[0][at] - COURANT * buoyancy[at] * (ahead_i[rows(tile), cols(h)] - p[at])


def velocity_side(p, v_in, v_out, buoyancy, ahead_x, i):
    row = row_ids()
    for h in range(2):
        at = (i, rows(p.shape[1] // SUBLANES - 1), cols(h))
        here = p[at]
        ahead = jnp.where(
            row < SUBLANES - 1,
            pltpu.roll(here, SUBLANES - 1, 0),
            jnp.broadcast_to(ahead_x[h, pl.ds(i, 1), :], here.shape),
        )
        v_out[1][at] = v_in[1][at] - COURANT * buoyancy[at] * (ahead - here)


def between(planes, work, unroll):
    def plane(i, _):
        work(i)
        return _

    lax.fori_loop(1, planes - 1, plane, 0, unroll=unroll)


def ghosts(p, first_x, behind_i, behind_x, ghost_in, ghost_out, ghost_b):
    (vi, vx), (vi_out, vx_out), (bi, bx) = ghost_in, ghost_out, ghost_b
    vi_out[...] = vi[...] - COURANT * bi[...] * (p[0] - behind_i[...])
    vx_out[...] = vx[...] - COURANT * bx[...] * (first_x[...] - behind_x[...])


def pressure(p_in, p_out, v, ghost, modulus, i, tile, first, source):
    lane, row = lane_ids(), row_ids()
    vi, vx, vd = v
    ghost_i, ghost_x = ghost
    here = [vd[i, rows(tile), cols(h)] for h in range(2)]
    turned = [pltpu.roll(x, 1, 1) for x in here]
    upper = [jnp.where(lane > 0, turned[0], 0.0), jnp.where(lane > 0, turned[1], turned[0])]
    for h in range(2):
        at = (i, rows(tile), cols(h))
        before_i = ghost_i[rows(tile), cols(h)] if first else vi[i - 1, rows(tile), cols(h)]
        now_x = vx[at]
        if tile > 0:
            before_x = vx[i, pl.ds(tile * SUBLANES - 1, SUBLANES), cols(h)]
        else:
            before_x = jnp.where(
                row > 0,
                pltpu.roll(now_x, 1, 0),
                jnp.broadcast_to(ghost_x[h, pl.ds(i, 1), :], now_x.shape),
            )
        total = (vi[at] - before_i) + (now_x - before_x) + (here[h] - upper[h])
        if source is not None:
            total = total - source(i, tile, h)
        p_out[at] = p_in[at] - COURANT * modulus[at] * total


def source(injected, wide, step):
    def strip(i, tile, h):
        row = ((i * wide + tile * SUBLANES) * 2 + h) * STEPS + step
        at = pl.ds(row, SUBLANES, stride=2 * STEPS)
        return injected[0][at, :] + injected[1][at, :]

    return strip


def ends(planes, tiles, strip):
    for tile in range(tiles):
        strip(0, tile, True)
        strip(planes - 1, tile, False)


def sides(planes, tiles, strip):
    def work(i):
        strip(i, 0, False)
        strip(i, tiles - 1, False)

    between(planes, work, 15)


def core(planes, tiles, strip):
    def work(i):
        for tile in range(1, tiles - 1):
            strip(i, tile, False)

    between(planes, work, 6)


def take_row(source, row, target):
    def plane(i, _):
        for h in range(2):
            target[h, pl.ds(i, 1), :] = source[i, pl.ds(row, 1), cols(h)]
        return _

    lax.fori_loop(0, source.shape[0], plane, 0, unroll=16)


class Exchange:
    def __init__(self, send_sems, recv_sems):
        self.send_sems, self.recv_sems = send_sems, recv_sems
        self.place = (lax.axis_index("xline"), lax.axis_index("inline"))
        self.count = (lax.axis_size("xline"), lax.axis_size("inline"))
        self.copies = []

    def has(self, axis, step):
        return self.place[axis] < self.count[axis] - 1 if step > 0 else self.place[axis] > 0

    def partner(self, axis, step):
        there = list(self.place)
        there[axis] = jnp.clip(there[axis] + step, 0, self.count[axis] - 1)
        return tuple(there)

    def greet(self, barrier):
        for axis in range(2):
            for step in (-1, 1):
                @pl.when(self.has(axis, step))
                def _():
                    pl.semaphore_signal(
                        barrier, inc=1, device_id=self.partner(axis, step), device_id_type=MESH
                    )

    def met(self, barrier):
        partners = [self.has(axis, step).astype(jnp.int32) for axis in range(2) for step in (-1, 1)]
        pl.semaphore_wait(barrier, sum(partners))

    def send(self, source, target, axis, step, number):
        copy = pltpu.make_async_remote_copy(
            src_ref=source,
            dst_ref=target,
            send_sem=self.send_sems.at[number],
            recv_sem=self.recv_sems.at[number],
            device_id=self.partner(axis, step),
            device_id_type=MESH,
        )

        @pl.when(self.has(axis, step))
        def _():
            copy.start()

        self.copies.append((copy, axis, step))

    def finish(self):
        for copy, axis, step in self.copies:
            @pl.when(self.has(axis, step))
            def _():
                copy.wait_send()

            @pl.when(self.has(axis, -step))
            def _():
                copy.wait_recv()

        self.copies = []


def split(value):
    high = value.astype(jnp.bfloat16).astype(F32)
    return high, value - high


def dot_t(a, b):
    return lax.dot_general(
        a.astype(jnp.bfloat16),
        b.astype(jnp.bfloat16),
        (((1,), (1,)), ((), ())),
        preferred_element_type=F32,
    )


def pack(traces, owner, cell, resample, devices):
    held = traces.shape[0]
    owner_row = owner[...]
    cell_row = cell[...]
    member = lax.broadcasted_iota(jnp.int32, (devices, held), 0) == owner_row
    member = jnp.where(member, 1.0, 0.0)
    earlier = lax.broadcasted_iota(jnp.int32, (LANES, LANES), 0) < lax.broadcasted_iota(
        jnp.int32, (LANES, LANES), 1
    )
    earlier = jnp.where(earlier, 1.0, 0.0).astype(jnp.bfloat16)
    running = jnp.zeros((devices, 1), F32)
    position = []
    for block in range(held // LANES):
        part = member[:, block * LANES : (block + 1) * LANES]
        before = jnp.dot(part.astype(jnp.bfloat16), earlier, preferred_element_type=F32) + running
        position.append(jnp.sum(part * before, axis=0, keepdims=True))
        running = running + jnp.sum(part, axis=1, keepdims=True)
    position = jnp.concatenate(position, axis=1).astype(jnp.int32)

    steps = resample.shape[0]
    filt = jnp.concatenate([resample[...], jnp.zeros((SLOT - steps, resample.shape[1]), F32)], 0)
    filt_high, filt_low = split(filt)
    trace_high, trace_low = split(traces[...])
    both = dot_t(jnp.concatenate([filt_high, filt_low], 0), trace_high)
    fields = both[:SLOT] + both[SLOT:] + dot_t(filt_high, trace_low)
    kind = lax.broadcasted_iota(jnp.int32, (SLOT, held), 0)
    fields = jnp.where(kind == steps, cell_row.astype(F32), fields)
    first, rest = split(fields)
    second, third = split(rest)
    packed = []
    for piece in (third, second, first):
        spread = [
            jnp.where(position == q, piece, 0.0) for q in range(LANES // SLOT)
        ]
        packed.append(dot_t(member, jnp.concatenate(spread, 0)))
    return (packed[0] + packed[1]) + packed[2]


def route(
    p_hbm, vi_hbm, vx_hbm, vd_hbm, m_hbm, b_hbm, traces_hbm, owner_hbm, cell_hbm, resample_hbm,
    p, vi, vx, vd, modulus, buoyancy, ghost_i, ghost_x, ghost_bi, ghost_bx, index, values, injected_a, injected_b,
    outbox, inbox, behind_i, ahead_i, behind_x, ahead_x, from_vi, from_bi, from_vx, from_bx,
    first_x, last_x, last_vx, last_bx,
    traces, owner, cell, resample,
    load_sems, node_sems, send_sems, recv_sems, post_sem, mail_sem, all_in,
):
    devices = lax.axis_size("xline") * lax.axis_size("inline")
    lines = lax.axis_size("inline")
    planes, tiles = p.shape[0], p.shape[1] // SUBLANES
    injected = (injected_a, injected_b)
    loads = [
        pltpu.make_async_copy(source, target, load_sems.at[k])
        for k, (source, target) in enumerate(
            ((p_hbm, p), (b_hbm, buoyancy), (vx_hbm, vx), (vi_hbm, vi), (vd_hbm, vd), (m_hbm, modulus))
        )
    ]
    node_loads = [
        pltpu.make_async_copy(source, target, node_sems.at[k])
        for k, (source, target) in enumerate(
            ((owner_hbm, owner), (cell_hbm, cell.at[0]), (resample_hbm, resample), (traces_hbm, traces))
        )
    ]
    for load in node_loads:
        load.start()
    barrier = pltpu.get_barrier_semaphore()
    xline, inline = lax.axis_index("xline"), lax.axis_index("inline")
    wide, blocks = lax.axis_size("xline"), lines // NEAR
    block, near = inline // NEAR, lax.rem(inline, NEAR)
    me = xline * lines + inline
    near_offsets = range(1, NEAR)
    far_offsets = [(dx, dy) for dx in range(wide) for dy in range(blocks) if dx or dy]

    def partner(dx, dy, dn):
        return (lax.rem(xline + dx, wide), lax.rem(block + dy, blocks) * NEAR + lax.rem(near + dn, NEAR))

    def greet(semaphore, offsets):
        for offset in offsets:
            pl.semaphore_signal(
                semaphore, inc=1, device_id=partner(*offset), device_id_type=MESH
            )

    beside = [(0, 0, dn) for dn in near_offsets]
    greet(barrier, beside + [(dx, dy, 0) for dx, dy in far_offsets])

    for load in loads[:2]:
        load.start()
    for load in node_loads:
        load.wait()
    for load in loads[2:]:
        load.start()
    pl.semaphore_wait(barrier, len(beside) + len(far_offsets))
    greet(all_in, beside)
    packed = pack(traces, owner, cell, resample, devices)
    for row in range(devices):
        outbox[row] = packed[row : row + 1]
    inbox[me] = outbox[me]
    pl.semaphore_wait(all_in, len(beside))

    halo = Exchange(send_sems, recv_sems)
    for ref in (behind_i, from_vi, from_bi):
        @pl.when(jnp.logical_not(halo.has(1, -1)))
        def _():
            ref[...] = jnp.zeros_like(ref)
    for ref in (behind_x, from_vx, from_bx):
        @pl.when(jnp.logical_not(halo.has(0, -1)))
        def _():
            ref[...] = jnp.zeros_like(ref)

    @pl.when(jnp.logical_not(halo.has(1, 1)))
    def _():
        ahead_i[...] = jnp.zeros_like(ahead_i)

    @pl.when(jnp.logical_not(halo.has(0, 1)))
    def _():
        ahead_x[...] = jnp.zeros_like(ahead_x)

    last = planes - 1
    halo.send(p_hbm.at[last], behind_i, 1, 1, 0)
    halo.send(p_hbm.at[0], ahead_i, 1, -1, 1)
    halo.send(vi_hbm.at[last], from_vi, 1, 1, 6)
    halo.send(b_hbm.at[last], from_bi, 1, 1, 4)

    def hops(offset, length):
        return min(offset, length - offset)

    def post(dx, dy, dn):
        device = partner(dx, dy, dn)
        pltpu.make_async_remote_copy(
            src_ref=outbox.at[device[0] * lines + device[1]],
            dst_ref=inbox.at[me],
            send_sem=post_sem,
            recv_sem=mail_sem,
            device_id=device,
            device_id_type=MESH,
        ).start()

    for dx, dy in sorted(
        [(0, 0)] + far_offsets, key=lambda o: -(hops(o[0], wide) + hops(o[1], blocks))
    ):
        def post_near(k, _):
            post(dx, dy, lax.rem(k + 3, NEAR))
            return _

        own = int(dx == 0 and dy == 0)
        lax.fori_loop(0, NEAR - own, post_near if not own else lambda k, _: (post(0, 0, k + 1), _)[1], 0)

    loads[0].wait()
    take_row(p, 0, first_x)
    halo.send(first_x, ahead_x, 0, -1, 2)
    take_row(p, p.shape[1] - 1, last_x)
    halo.send(last_x, behind_x, 0, 1, 3)
    loads[1].wait()
    take_row(buoyancy, p.shape[1] - 1, last_bx)
    halo.send(last_bx, from_bx, 0, 1, 5)
    loads[2].wait()
    take_row(vx, p.shape[1] - 1, last_vx)
    halo.send(last_vx, from_vx, 0, 1, 7)

    def clear(k, _):
        for ref in injected:
            ref[pl.ds(pl.multiple_of(k * 64, 64), 64), :] = jnp.zeros((64, LANES), F32)
        return _

    lax.fori_loop(0, injected[0].shape[0] // 64, clear, 0)
    loads[3].wait()
    loads[4].wait()
    v = (vi, vx, vd)
    velocity_inside(p, v, v, buoyancy)
    loads[5].wait()

    def strip(i, tile, first):
        pressure(p, p, v, (ghost_i, ghost_x), modulus, i, tile, first, None)

    core(planes, tiles, strip)
    halo.finish()
    velocity_next(p, v, v, buoyancy, ahead_i)
    for i in (0, planes - 1):
        velocity_side(p, v, v, buoyancy, ahead_x, i)
    between(planes, lambda i: velocity_side(p, v, v, buoyancy, ahead_x, i), 15)
    ghosts(p, first_x, behind_i, behind_x, (from_vi, from_vx), (ghost_i, ghost_x), (from_bi, from_bx))
    ghost_bi[...] = from_bi[...]
    ghost_bx[...] = from_bx[...]
    ends(planes, tiles, strip)
    sides(planes, tiles, strip)

    mail = pltpu.make_async_remote_copy(
        src_ref=outbox.at[pl.ds(0, devices - 1)],
        dst_ref=inbox.at[pl.ds(0, devices - 1)],
        send_sem=post_sem,
        recv_sem=mail_sem,
        device_id=partner(0, 0, 1),
        device_id_type=MESH,
    )
    mail.wait_send()
    mail.wait_recv()
    values[...] = inbox[...].reshape(devices, LANES).T
    index[...] = values[pl.ds(STEPS, LANES // SLOT, stride=SLOT), :].astype(jnp.int32)


def scatter(index_ref, values, _a, _b, injected_a, injected_b, index, sem):
    load = pltpu.make_async_copy(index_ref, index, sem)
    load.start()
    injected = (injected_a, injected_b)
    share = values.shape[1] // len(injected)
    lane = lax.broadcasted_iota(jnp.int32, (STEPS, LANES), 1)
    slots, group = 15, 2

    def spread(d):
        pick = jnp.full((SUBLANES, LANES), d, jnp.int32)
        return [
            jnp.take_along_axis(values[pl.ds(q * SLOT, SLOT), :], pick, axis=1)[:STEPS]
            for q in range(slots)
        ]

    def add(target, d, now, numbers):
        tiles, adds = [], []
        for q in numbers:
            cell = index[q, d]
            tiles.append(lax.shift_right_logical(cell, 7))
            adds.append(jnp.where(lane == (cell & (LANES - 1)), now[q], 0.0))
        spots = [pl.ds(pl.multiple_of(tile * STEPS, STEPS), STEPS) for tile in tiles]
        old = [target[spot, :] for spot in spots]
        for b in range(len(numbers)):
            new = old[b] + adds[b]
            for a in range(b):
                new = new + jnp.where(tiles[a] == tiles[b], adds[a], 0.0)
            target[spots[b], :] = new

    def sender(d, now):
        later = [
            spread(jnp.minimum(d + 1, share - 1) + k * share) for k in range(len(injected))
        ]
        for start in range(0, slots, group):
            for k, target in enumerate(injected):
                add(target, d + k * share, now[k], range(start, min(start + group, slots)))
        return later

    first = [spread(k * share) for k in range(len(injected))]
    load.wait()
    lax.fori_loop(0, share, sender, first, unroll=4)


def advance(
    p_in, vi_in, vx_in, vd_in, modulus, buoyancy, ghost_i_in, ghost_x_in, ghost_bi, ghost_bx, injected_a, injected_b,
    p, vi, vx, vd, ghost_i, ghost_x,
    behind_i, ahead_i, behind_x, ahead_x, first_x, last_x, send_sems, recv_sems,
):
    planes, tiles = p.shape[0], p.shape[1] // SUBLANES
    injected = (injected_a, injected_b)
    halo = Exchange(None, None)
    barrier = pltpu.get_barrier_semaphore()
    halo.greet(barrier)

    @pl.when(jnp.logical_not(halo.has(1, -1)))
    def _():
        behind_i[...] = jnp.zeros_like(behind_i)

    @pl.when(jnp.logical_not(halo.has(0, -1)))
    def _():
        behind_x[...] = jnp.zeros_like(behind_x)

    @pl.when(jnp.logical_not(halo.has(1, 1)))
    def _():
        ahead_i[...] = jnp.zeros_like(ahead_i)

    @pl.when(jnp.logical_not(halo.has(0, 1)))
    def _():
        ahead_x[...] = jnp.zeros_like(ahead_x)

    def send_planes(step):
        halo.send_sems, halo.recv_sems = send_sems.at[step], recv_sems.at[step]
        halo.send(p.at[planes - 1], behind_i.at[step], 1, 1, 0)
        halo.send(p.at[0], ahead_i.at[step], 1, -1, 1)

    def send_rows(step):
        take_row(p, 0, first_x.at[step])
        halo.send(first_x.at[step], ahead_x.at[step], 0, -1, 2)
        take_row(p, p.shape[1] - 1, last_x.at[step])
        halo.send(last_x.at[step], behind_x.at[step], 0, 1, 3)

    def inject(i, tile, first):
        del first
        spread = source(injected, p.shape[1], 0)
        for h in range(2):
            at = (i, rows(tile), cols(h))
            p[at] = p_in[at] + COURANT * modulus[at] * spread(i, tile, h)

    ends(planes, tiles, inject)
    halo.met(barrier)
    send_planes(0)
    sides(planes, tiles, inject)
    send_rows(0)
    core(planes, tiles, inject)

    v = (vi, vx, vd)
    for step in range(1, STEPS):
        last = step == STEPS - 1
        v_in = (vi_in, vx_in, vd_in) if step == 1 else v
        ghost_in = (ghost_i_in, ghost_x_in) if step == 1 else (ghost_i, ghost_x)
        spread = source(injected, p.shape[1], step)

        def strip(i, tile, first):
            pressure(p, p, v, (ghost_i, ghost_x), modulus, i, tile, first, spread)

        velocity_inside(p, v_in, v, buoyancy)
        if last:
            core(planes, tiles, strip)
        halo.finish()

        def side(i):
            velocity_side(p, v_in, v, buoyancy, ahead_x.at[step - 1], i)

        velocity_next(p, v_in, v, buoyancy, ahead_i.at[step - 1])
        side(0)
        side(planes - 1)
        ghosts(
            p, first_x.at[step - 1], behind_i.at[step - 1], behind_x.at[step - 1],
            ghost_in, (ghost_i, ghost_x), (ghost_bi, ghost_bx),
        )
        if not last:
            ends(planes, tiles, strip)
            send_planes(step)
        between(planes, side, 15)
        if not last:
            sides(planes, tiles, strip)
            send_rows(step)
            core(planes, tiles, strip)


def finish(
    p_in, vi, vx, vd, ghost_i, ghost_x, modulus, injected_a, injected_b,
    p_out, vi_out, vx_out, vd_out,
    p, sems,
):
    planes, tiles = p_in.shape[0], p_in.shape[1] // SUBLANES
    copies = []

    def leave(source_ref, target):
        copies.append(pltpu.make_async_copy(source_ref, target, sems.at[len(copies)]))
        copies[-1].start()

    for source_ref, target in ((vi, vi_out), (vx, vx_out), (vd, vd_out)):
        leave(source_ref, target)
    inner = pl.ds(1, planes - 2)
    middle = (inner, pl.ds(SUBLANES, (tiles - 2) * SUBLANES))
    leave(p_in.at[middle], p_out.at[middle])
    spread = source((injected_a, injected_b), p_in.shape[1], STEPS - 1)

    def strip(i, tile, first):
        pressure(p_in, p, (vi, vx, vd), (ghost_i, ghost_x), modulus, i, tile, first, spread)

    ends(planes, tiles, strip)
    for end in (0, planes - 1):
        leave(p.at[end], p_out.at[end])
    sides(planes, tiles, strip)
    for tile in (0, tiles - 1):
        side = (inner, rows(tile))
        leave(p.at[side], p_out.at[side])
    for copy in copies:
        copy.wait()


def shards(
    pressure_in, vel_inline, vel_xline, vel_depth, modulus, buoyancy, traces, owner, node_cell, resample
):
    planes, wide, deep = pressure_in.shape
    devices = lax.axis_size("xline") * lax.axis_size("inline")
    held = traces.shape[0]
    field = (planes, wide, deep)
    plane, column = (wide, deep), (2, planes, LANES)
    injection = (planes * wide * deep // LANES * STEPS, LANES)
    vmem = pl.BlockSpec(memory_space=VMEM)
    hbm = pl.BlockSpec(memory_space=HBM)
    dma = pltpu.SemaphoreType.DMA

    state = pl.pallas_call(
        route,
        out_shape=[VMEM(field, F32)] * 6
        + [VMEM(plane, F32), VMEM(column, F32)] * 2
        + [VMEM((LANES // SLOT, devices), jnp.int32), VMEM((LANES, devices), F32)]
        + [VMEM(injection, F32)] * 2,
        in_specs=[hbm] * 10,
        out_specs=[vmem] * 14,
        scratch_shapes=[VMEM((devices, 1, LANES), F32)] * 2
        + [VMEM(plane, F32)] * 2
        + [VMEM(column, F32)] * 2
        + [VMEM(plane, F32)] * 2
        + [VMEM(column, F32)] * 6
        + [
            VMEM(traces.shape, F32), VMEM((1, held), jnp.int32), VMEM((1, held), jnp.int32),
            VMEM(resample.shape, F32),
        ]
        + [dma((6,)), dma((4,)), dma((8,)), dma((8,)), dma, dma, pltpu.SemaphoreType.REGULAR],
        compiler_params=pltpu.CompilerParams(collective_id=0, has_side_effects=True, vmem_limit_bytes=8 * MIB),
        name="route",
    )(
        *(
            pltpu.with_memory_space_constraint(x, HBM)
            for x in (
                pressure_in, vel_inline, vel_xline, vel_depth, modulus, buoyancy,
                traces, owner.reshape(1, held), node_cell, resample,
            )
        )
    )
    *fields, index, values, cleared_a, cleared_b = state
    injected = pl.pallas_call(
        scatter,
        out_shape=[VMEM(injection, F32)] * 2,
        in_specs=[vmem] * 4,
        out_specs=[vmem] * 2,
        scratch_shapes=[pltpu.SMEM((LANES // SLOT, devices), jnp.int32), dma],
        input_output_aliases={2: 0, 3: 1},
        compiler_params=pltpu.CompilerParams(vmem_limit_bytes=2 * MIB),
        name="scatter",
    )(index, values, cleared_a, cleared_b)
    rounds = STEPS - 1
    *fields, ghost_i, ghost_x = pl.pallas_call(
        advance,
        out_shape=[VMEM(field, F32)] * 4 + [VMEM(plane, F32), VMEM(column, F32)],
        in_specs=[vmem] * 12,
        out_specs=[vmem] * 6,
        scratch_shapes=[VMEM((rounds, *plane), F32)] * 2
        + [VMEM((rounds, *column), F32)] * 4
        + [dma((rounds, 4)), dma((rounds, 4))],
        compiler_params=pltpu.CompilerParams(
            collective_id=1, has_side_effects=True, vmem_limit_bytes=4 * MIB
        ),
        name="advance",
    )(*fields, *injected)
    modulus = state[4]
    return pl.pallas_call(
        finish,
        out_shape=[HBM(field, F32)] * 4,
        in_specs=[vmem] * 9,
        out_specs=[hbm] * 4,
        scratch_shapes=[VMEM(field, F32), dma((8,))],
        compiler_params=pltpu.CompilerParams(vmem_limit_bytes=4 * MIB),
        name="finish",
    )(*fields, ghost_i, ghost_x, modulus, *injected)


def solution(mesh):
    field = P("inline", "xline", None)
    nodes = ("xline", "inline")
    return jax.shard_map(
        shards,
        mesh=mesh,
        in_specs=(field,) * 6 + (P(nodes, None), P(nodes, None), P(nodes), P()),
        out_specs=(field,) * 4,
        check_vma=False,
    )
```

```python
import jax
import jax.numpy as jnp
from jax import lax
from jax.experimental import pallas as pl
from jax.experimental.pallas import tpu as pltpu
from jax.sharding import PartitionSpec as P

COURANT = 0.35
STEPS = 4
LANES = 128
SUBLANES = 8
SLOT = 8
NEAR = 8
MESH = pl.DeviceIdType.MESH
VMEM, HBM = pltpu.MemorySpace.VMEM, pltpu.MemorySpace.HBM
F32 = jnp.float32
MIB = 2**20


def lane_ids():
    return lax.broadcasted_iota(jnp.int32, (SUBLANES, LANES), 1)


def row_ids():
    return lax.broadcasted_iota(jnp.int32, (SUBLANES, LANES), 0)


def cols(half):
    return pl.ds(half * LANES, LANES)


def rows(tile):
    return pl.ds(tile * SUBLANES, SUBLANES)


def velocity(p, v_in, v_out, buoyancy, i, tile, next_plane):
    lane = lane_ids()
    (vi, vx, vd), (vi_out, vx_out, vd_out) = v_in, v_out
    here = [p[i, rows(tile), cols(h)] for h in range(2)]
    turned = [pltpu.roll(x, LANES - 1, 1) for x in here]
    deeper = [jnp.where(lane < LANES - 1, turned[0], turned[1]), jnp.where(lane < LANES - 1, turned[1], 0.0)]
    last = p.shape[1] // SUBLANES - 1
    for h in range(2):
        rb = COURANT * buoyancy[i, rows(tile), cols(h)]
        vd_out[i, rows(tile), cols(h)] = vd[i, rows(tile), cols(h)] - rb * (deeper[h] - here[h])
        if next_plane:
            ahead = p[i + 1, rows(tile), cols(h)]
            vi_out[i, rows(tile), cols(h)] = vi[i, rows(tile), cols(h)] - rb * (ahead - here[h])
        if tile < last:
            ahead = p[i, pl.ds(tile * SUBLANES + 1, SUBLANES), cols(h)]
            vx_out[i, rows(tile), cols(h)] = vx[i, rows(tile), cols(h)] - rb * (ahead - here[h])


def velocity_inside(p, v_in, v_out, buoyancy):
    planes, tiles = p.shape[0], p.shape[1] // SUBLANES

    def plane(i, _):
        for tile in range(tiles):
            velocity(p, v_in, v_out, buoyancy, i, tile, True)
        return _

    lax.fori_loop(0, planes - 1, plane, 0, unroll=6)
    for tile in range(tiles):
        velocity(p, v_in, v_out, buoyancy, planes - 1, tile, False)


def velocity_next(p, v_in, v_out, buoyancy, ahead_i):
    planes, tiles = p.shape[0], p.shape[1] // SUBLANES
    for tile in range(tiles):
        for h in range(2):
            at = (planes - 1, rows(tile), cols(h))
            v_out[0][at] = v_in[0][at] - COURANT * buoyancy[at] * (ahead_i[rows(tile), cols(h)] - p[at])


def velocity_side(p, v_in, v_out, buoyancy, ahead_x, i):
    row = row_ids()
    for h in range(2):
        at = (i, rows(p.shape[1] // SUBLANES - 1), cols(h))
        here = p[at]
        ahead = jnp.where(
            row < SUBLANES - 1,
            pltpu.roll(here, SUBLANES - 1, 0),
            jnp.broadcast_to(ahead_x[h, pl.ds(i, 1), :], here.shape),
        )
        v_out[1][at] = v_in[1][at] - COURANT * buoyancy[at] * (ahead - here)


def between(planes, work, unroll):
    def plane(i, _):
        work(i)
        return _

    lax.fori_loop(1, planes - 1, plane, 0, unroll=unroll)


def ghosts(p, first_x, behind_i, behind_x, ghost_in, ghost_out, ghost_b):
    (vi, vx), (vi_out, vx_out), (bi, bx) = ghost_in, ghost_out, ghost_b
    vi_out[...] = vi[...] - COURANT * bi[...] * (p[0] - behind_i[...])
    vx_out[...] = vx[...] - COURANT * bx[...] * (first_x[...] - behind_x[...])


def pressure(p_in, p_out, v, ghost, modulus, i, tile, first, source):
    lane, row = lane_ids(), row_ids()
    vi, vx, vd = v
    ghost_i, ghost_x = ghost
    here = [vd[i, rows(tile), cols(h)] for h in range(2)]
    turned = [pltpu.roll(x, 1, 1) for x in here]
    upper = [jnp.where(lane > 0, turned[0], 0.0), jnp.where(lane > 0, turned[1], turned[0])]
    for h in range(2):
        at = (i, rows(tile), cols(h))
        before_i = ghost_i[rows(tile), cols(h)] if first else vi[i - 1, rows(tile), cols(h)]
        now_x = vx[at]
        if tile > 0:
            before_x = vx[i, pl.ds(tile * SUBLANES - 1, SUBLANES), cols(h)]
        else:
            before_x = jnp.where(
                row > 0,
                pltpu.roll(now_x, 1, 0),
                jnp.broadcast_to(ghost_x[h, pl.ds(i, 1), :], now_x.shape),
            )
        total = (vi[at] - before_i) + (now_x - before_x) + (here[h] - upper[h])
        if source is not None:
            total = total - source(i, tile, h)
        p_out[at] = p_in[at] - COURANT * modulus[at] * total


def source(injected, wide, step):
    def strip(i, tile, h):
        row = ((i * wide + tile * SUBLANES) * 2 + h) * STEPS + step
        at = pl.ds(row, SUBLANES, stride=2 * STEPS)
        return injected[0][at, :] + injected[1][at, :]

    return strip


def ends(planes, tiles, strip):
    for tile in range(tiles):
        strip(0, tile, True)
        strip(planes - 1, tile, False)


def sides(planes, tiles, strip):
    def work(i):
        strip(i, 0, False)
        strip(i, tiles - 1, False)

    between(planes, work, planes - 2)


def core(planes, tiles, strip):
    def work(i):
        for tile in range(1, tiles - 1):
            strip(i, tile, False)

    between(planes, work, 6)


def take_row(source, row, target):
    def plane(i, _):
        for h in range(2):
            target[h, pl.ds(i, 1), :] = source[i, pl.ds(row, 1), cols(h)]
        return _

    lax.fori_loop(0, source.shape[0], plane, 0, unroll=16)


class Exchange:
    def __init__(self, send_sems, recv_sems):
        self.send_sems, self.recv_sems = send_sems, recv_sems
        self.place = (lax.axis_index("xline"), lax.axis_index("inline"))
        self.count = (lax.axis_size("xline"), lax.axis_size("inline"))
        self.copies = []

    def has(self, axis, step):
        return self.place[axis] < self.count[axis] - 1 if step > 0 else self.place[axis] > 0

    def partner(self, axis, step):
        there = list(self.place)
        there[axis] = jnp.clip(there[axis] + step, 0, self.count[axis] - 1)
        return tuple(there)

    def greet(self, barrier):
        for axis in range(2):
            for step in (-1, 1):
                @pl.when(self.has(axis, step))
                def _():
                    pl.semaphore_signal(
                        barrier, inc=1, device_id=self.partner(axis, step), device_id_type=MESH
                    )

    def met(self, barrier):
        partners = [self.has(axis, step).astype(jnp.int32) for axis in range(2) for step in (-1, 1)]
        pl.semaphore_wait(barrier, sum(partners))

    def send(self, source, target, axis, step, number):
        copy = pltpu.make_async_remote_copy(
            src_ref=source,
            dst_ref=target,
            send_sem=self.send_sems.at[number],
            recv_sem=self.recv_sems.at[number],
            device_id=self.partner(axis, step),
            device_id_type=MESH,
        )

        @pl.when(self.has(axis, step))
        def _():
            copy.start()

        self.copies.append((copy, axis, step))

    def finish(self):
        for copy, axis, step in self.copies:
            @pl.when(self.has(axis, step))
            def _():
                copy.wait_send()

            @pl.when(self.has(axis, -step))
            def _():
                copy.wait_recv()

        self.copies = []


def split(value):
    high = value.astype(jnp.bfloat16).astype(F32)
    return high, value - high


def dot_t(a, b):
    return lax.dot_general(
        a.astype(jnp.bfloat16),
        b.astype(jnp.bfloat16),
        (((1,), (1,)), ((), ())),
        preferred_element_type=F32,
    )


def pack(traces, owner, cell, resample, devices):
    held = traces.shape[0]
    owner_row = owner[...]
    cell_row = cell[...]
    member = lax.broadcasted_iota(jnp.int32, (devices, held), 0) == owner_row
    member = jnp.where(member, 1.0, 0.0)
    earlier = lax.broadcasted_iota(jnp.int32, (LANES, LANES), 0) < lax.broadcasted_iota(
        jnp.int32, (LANES, LANES), 1
    )
    earlier = jnp.where(earlier, 1.0, 0.0).astype(jnp.bfloat16)
    running = jnp.zeros((devices, 1), F32)
    position = []
    for block in range(held // LANES):
        part = member[:, block * LANES : (block + 1) * LANES]
        before = jnp.dot(part.astype(jnp.bfloat16), earlier, preferred_element_type=F32) + running
        position.append(jnp.sum(part * before, axis=0, keepdims=True))
        running = running + jnp.sum(part, axis=1, keepdims=True)
    position = jnp.concatenate(position, axis=1).astype(jnp.int32)

    steps = resample.shape[0]
    filt = jnp.concatenate([resample[...], jnp.zeros((SLOT - steps, resample.shape[1]), F32)], 0)
    filt_high, filt_low = split(filt)
    trace_high, trace_low = split(traces[...])
    both = dot_t(jnp.concatenate([filt_high, filt_low], 0), trace_high)
    fields = both[:SLOT] + both[SLOT:] + dot_t(filt_high, trace_low)
    kind = lax.broadcasted_iota(jnp.int32, (SLOT, held), 0)
    fields = jnp.where(kind == steps, cell_row.astype(F32), fields)
    first, rest = split(fields)
    second, third = split(rest)
    packed = []
    for piece in (third, second, first):
        spread = [
            jnp.where(position == q, piece, 0.0) for q in range(LANES // SLOT)
        ]
        packed.append(dot_t(member, jnp.concatenate(spread, 0)))
    return (packed[0] + packed[1]) + packed[2]


def route(
    p_hbm, vi_hbm, vx_hbm, vd_hbm, m_hbm, b_hbm, traces_hbm, owner_hbm, cell_hbm, resample_hbm,
    p, vi, vx, vd, modulus, buoyancy, ghost_i, ghost_x, ghost_bi, ghost_bx, index, values, injected_a, injected_b,
    outbox, inbox, behind_i, ahead_i, behind_x, ahead_x, from_vi, from_bi, from_vx, from_bx,
    first_x, last_x, last_vx, last_bx,
    traces, owner, cell, resample,
    load_sems, node_sems, send_sems, recv_sems, post_sem, mail_sem, all_in,
):
    devices = lax.axis_size("xline") * lax.axis_size("inline")
    lines = lax.axis_size("inline")
    planes, tiles = p.shape[0], p.shape[1] // SUBLANES
    injected = (injected_a, injected_b)
    loads = [
        pltpu.make_async_copy(source, target, load_sems.at[k])
        for k, (source, target) in enumerate(
            ((p_hbm, p), (b_hbm, buoyancy), (vx_hbm, vx), (vi_hbm, vi), (vd_hbm, vd), (m_hbm, modulus))
        )
    ]
    node_loads = [
        pltpu.make_async_copy(source, target, node_sems.at[k])
        for k, (source, target) in enumerate(
            ((owner_hbm, owner), (cell_hbm, cell.at[0]), (resample_hbm, resample), (traces_hbm, traces))
        )
    ]
    for load in node_loads:
        load.start()
    barrier = pltpu.get_barrier_semaphore()
    xline, inline = lax.axis_index("xline"), lax.axis_index("inline")
    wide, blocks = lax.axis_size("xline"), lines // NEAR
    block, near = inline // NEAR, lax.rem(inline, NEAR)
    me = xline * lines + inline
    near_offsets = range(1, NEAR)
    far_offsets = [(dx, dy) for dx in range(wide) for dy in range(blocks) if dx or dy]

    def partner(dx, dy, dn):
        return (lax.rem(xline + dx, wide), lax.rem(block + dy, blocks) * NEAR + lax.rem(near + dn, NEAR))

    def greet(semaphore, offsets):
        for offset in offsets:
            pl.semaphore_signal(
                semaphore, inc=1, device_id=partner(*offset), device_id_type=MESH
            )

    beside = [(0, 0, dn) for dn in near_offsets]
    greet(barrier, beside + [(dx, dy, 0) for dx, dy in far_offsets])

    for load in loads[:2]:
        load.start()
    for load in node_loads:
        load.wait()
    for load in loads[2:]:
        load.start()
    pl.semaphore_wait(barrier, len(beside) + len(far_offsets))
    greet(all_in, beside)
    packed = pack(traces, owner, cell, resample, devices)
    for row in range(devices):
        outbox[row] = packed[row : row + 1]
    inbox[me] = outbox[me]
    pl.semaphore_wait(all_in, len(beside))

    halo = Exchange(send_sems, recv_sems)
    for ref in (behind_i, from_vi, from_bi):
        @pl.when(jnp.logical_not(halo.has(1, -1)))
        def _():
            ref[...] = jnp.zeros_like(ref)
    for ref in (behind_x, from_vx, from_bx):
        @pl.when(jnp.logical_not(halo.has(0, -1)))
        def _():
            ref[...] = jnp.zeros_like(ref)

    @pl.when(jnp.logical_not(halo.has(1, 1)))
    def _():
        ahead_i[...] = jnp.zeros_like(ahead_i)

    @pl.when(jnp.logical_not(halo.has(0, 1)))
    def _():
        ahead_x[...] = jnp.zeros_like(ahead_x)

    last = planes - 1
    halo.send(p_hbm.at[last], behind_i, 1, 1, 0)
    halo.send(p_hbm.at[0], ahead_i, 1, -1, 1)
    halo.send(vi_hbm.at[last], from_vi, 1, 1, 6)
    halo.send(b_hbm.at[last], from_bi, 1, 1, 4)

    def hops(offset, length):
        return min(offset, length - offset)

    def post(dx, dy, dn):
        device = partner(dx, dy, dn)
        pltpu.make_async_remote_copy(
            src_ref=outbox.at[device[0] * lines + device[1]],
            dst_ref=inbox.at[me],
            send_sem=post_sem,
            recv_sem=mail_sem,
            device_id=device,
            device_id_type=MESH,
        ).start()

    for dx, dy in sorted(
        [(0, 0)] + far_offsets, key=lambda o: -(hops(o[0], wide) + hops(o[1], blocks))
    ):
        def post_near(k, _):
            post(dx, dy, lax.rem(k + 3, NEAR))
            return _

        own = int(dx == 0 and dy == 0)
        lax.fori_loop(0, NEAR - own, post_near if not own else lambda k, _: (post(0, 0, k + 1), _)[1], 0)

    loads[0].wait()
    take_row(p, 0, first_x)
    halo.send(first_x, ahead_x, 0, -1, 2)
    take_row(p, p.shape[1] - 1, last_x)
    halo.send(last_x, behind_x, 0, 1, 3)
    loads[1].wait()
    take_row(buoyancy, p.shape[1] - 1, last_bx)
    halo.send(last_bx, from_bx, 0, 1, 5)
    loads[2].wait()
    take_row(vx, p.shape[1] - 1, last_vx)
    halo.send(last_vx, from_vx, 0, 1, 7)

    def clear(k, _):
        for ref in injected:
            ref[pl.ds(pl.multiple_of(k * 64, 64), 64), :] = jnp.zeros((64, LANES), F32)
        return _

    lax.fori_loop(0, injected[0].shape[0] // 64, clear, 0)
    loads[3].wait()
    loads[4].wait()
    v = (vi, vx, vd)
    velocity_inside(p, v, v, buoyancy)
    loads[5].wait()

    def strip(i, tile, first):
        pressure(p, p, v, (ghost_i, ghost_x), modulus, i, tile, first, None)

    core(planes, tiles, strip)
    halo.finish()
    velocity_next(p, v, v, buoyancy, ahead_i)
    for i in (0, planes - 1):
        velocity_side(p, v, v, buoyancy, ahead_x, i)
    between(planes, lambda i: velocity_side(p, v, v, buoyancy, ahead_x, i), 15)
    ghosts(p, first_x, behind_i, behind_x, (from_vi, from_vx), (ghost_i, ghost_x), (from_bi, from_bx))
    ghost_bi[...] = from_bi[...]
    ghost_bx[...] = from_bx[...]
    ends(planes, tiles, strip)
    sides(planes, tiles, strip)

    mail = pltpu.make_async_remote_copy(
        src_ref=outbox.at[pl.ds(0, devices - 1)],
        dst_ref=inbox.at[pl.ds(0, devices - 1)],
        send_sem=post_sem,
        recv_sem=mail_sem,
        device_id=partner(0, 0, 1),
        device_id_type=MESH,
    )
    mail.wait_send()
    mail.wait_recv()
    values[...] = inbox[...].reshape(devices, LANES).T
    index[...] = values[pl.ds(STEPS, LANES // SLOT, stride=SLOT), :].astype(jnp.int32)


def scatter(index_ref, values, _a, _b, injected_a, injected_b, index, sem):
    load = pltpu.make_async_copy(index_ref, index, sem)
    load.start()
    injected = (injected_a, injected_b)
    share = values.shape[1] // len(injected)
    lane = lax.broadcasted_iota(jnp.int32, (STEPS, LANES), 1)
    slots, group = 15, 2

    def spread(d):
        pick = jnp.full((SUBLANES, LANES), d, jnp.int32)
        return [
            jnp.take_along_axis(values[pl.ds(q * SLOT, SLOT), :], pick, axis=1)[:STEPS]
            for q in range(slots)
        ]

    def add(target, d, now, numbers):
        tiles, adds = [], []
        for q in numbers:
            cell = index[q, d]
            tiles.append(lax.shift_right_logical(cell, 7))
            depth = jnp.full(lane.shape, cell, jnp.int32) & (LANES - 1)
            adds.append(jnp.where(lane == depth, now[q], 0.0))
        spots = [pl.ds(pl.multiple_of(tile * STEPS, STEPS), STEPS) for tile in tiles]
        old = [target[spot, :] for spot in spots]
        for b in range(len(numbers)):
            new = old[b] + adds[b]
            for a in range(b):
                new = new + jnp.where(tiles[a] == tiles[b], adds[a], 0.0)
            target[spots[b], :] = new

    def sender(d, now):
        later = [
            spread(jnp.minimum(d + 1, share - 1) + k * share) for k in range(len(injected))
        ]
        for start in range(0, slots, group):
            for k, target in enumerate(injected):
                add(target, d + k * share, now[k], range(start, min(start + group, slots)))
        return later

    first = [spread(k * share) for k in range(len(injected))]
    load.wait()
    lax.fori_loop(0, share, sender, first, unroll=4)


def advance(
    p_in, vi_in, vx_in, vd_in, modulus, buoyancy, ghost_i_in, ghost_x_in, ghost_bi, ghost_bx, injected_a, injected_b,
    p, vi, vx, vd, ghost_i, ghost_x,
    behind_i, ahead_i, behind_x, ahead_x, first_x, last_x, send_sems, recv_sems,
):
    planes, tiles = p.shape[0], p.shape[1] // SUBLANES
    injected = (injected_a, injected_b)
    halo = Exchange(None, None)
    barrier = pltpu.get_barrier_semaphore()
    halo.greet(barrier)

    @pl.when(jnp.logical_not(halo.has(1, -1)))
    def _():
        behind_i[...] = jnp.zeros_like(behind_i)

    @pl.when(jnp.logical_not(halo.has(0, -1)))
    def _():
        behind_x[...] = jnp.zeros_like(behind_x)

    @pl.when(jnp.logical_not(halo.has(1, 1)))
    def _():
        ahead_i[...] = jnp.zeros_like(ahead_i)

    @pl.when(jnp.logical_not(halo.has(0, 1)))
    def _():
        ahead_x[...] = jnp.zeros_like(ahead_x)

    def send_planes(step):
        halo.send_sems, halo.recv_sems = send_sems.at[step], recv_sems.at[step]
        halo.send(p.at[planes - 1], behind_i.at[step], 1, 1, 0)
        halo.send(p.at[0], ahead_i.at[step], 1, -1, 1)

    def send_rows(step):
        take_row(p, 0, first_x.at[step])
        halo.send(first_x.at[step], ahead_x.at[step], 0, -1, 2)
        take_row(p, p.shape[1] - 1, last_x.at[step])
        halo.send(last_x.at[step], behind_x.at[step], 0, 1, 3)

    def inject(i, tile, first):
        del first
        spread = source(injected, p.shape[1], 0)
        for h in range(2):
            at = (i, rows(tile), cols(h))
            p[at] = p_in[at] + COURANT * modulus[at] * spread(i, tile, h)

    ends(planes, tiles, inject)
    sides(planes, tiles, inject)
    halo.met(barrier)
    send_planes(0)
    send_rows(0)
    core(planes, tiles, inject)

    v = (vi, vx, vd)
    for step in range(1, STEPS):
        last = step == STEPS - 1
        v_in = (vi_in, vx_in, vd_in) if step == 1 else v
        ghost_in = (ghost_i_in, ghost_x_in) if step == 1 else (ghost_i, ghost_x)
        spread = source(injected, p.shape[1], step)

        def strip(i, tile, first):
            pressure(p, p, v, (ghost_i, ghost_x), modulus, i, tile, first, spread)

        velocity_inside(p, v_in, v, buoyancy)
        halo.finish()

        def side(i):
            velocity_side(p, v_in, v, buoyancy, ahead_x.at[step - 1], i)

        velocity_next(p, v_in, v, buoyancy, ahead_i.at[step - 1])
        side(0)
        side(planes - 1)
        ghosts(
            p, first_x.at[step - 1], behind_i.at[step - 1], behind_x.at[step - 1],
            ghost_in, (ghost_i, ghost_x), (ghost_bi, ghost_bx),
        )
        if not last:
            ends(planes, tiles, strip)
            send_planes(step)
        between(planes, side, planes - 2)
        if not last:
            sides(planes, tiles, strip)
            send_rows(step)
            core(planes, tiles, strip)


def finish(
    p_in, vi, vx, vd, ghost_i, ghost_x, modulus, injected_a, injected_b,
    p_out, vi_out, vx_out, vd_out,
    p, sems,
):
    planes, tiles = p_in.shape[0], p_in.shape[1] // SUBLANES
    copies = []

    def leave(source_ref, target):
        copies.append(pltpu.make_async_copy(source_ref, target, sems.at[len(copies)]))
        copies[-1].start()

    for source_ref, target in ((vi, vi_out), (vx, vx_out), (vd, vd_out)):
        leave(source_ref, target)
    spread = source((injected_a, injected_b), p_in.shape[1], STEPS - 1)
    size = planes // 4

    def plane(i, first):
        for tile in range(tiles):
            pressure(p_in, p, (vi, vx, vd), (ghost_i, ghost_x), modulus, i, tile, first, spread)

    def inner(i, _):
        plane(i, False)
        return _

    for start in range(0, planes, size):
        if start == 0:
            plane(0, True)
        head = max(start, 1)
        lax.fori_loop(head, start + size, inner, 0, unroll=start + size - head)
        leave(p.at[pl.ds(start, size)], p_out.at[pl.ds(start, size)])
    for copy in copies:
        copy.wait()


def shards(
    pressure_in, vel_inline, vel_xline, vel_depth, modulus, buoyancy, traces, owner, node_cell, resample
):
    planes, wide, deep = pressure_in.shape
    devices = lax.axis_size("xline") * lax.axis_size("inline")
    held = traces.shape[0]
    field = (planes, wide, deep)
    plane, column = (wide, deep), (2, planes, LANES)
    injection = (planes * wide * deep // LANES * STEPS, LANES)
    vmem = pl.BlockSpec(memory_space=VMEM)
    hbm = pl.BlockSpec(memory_space=HBM)
    dma = pltpu.SemaphoreType.DMA

    state = pl.pallas_call(
        route,
        out_shape=[VMEM(field, F32)] * 6
        + [VMEM(plane, F32), VMEM(column, F32)] * 2
        + [VMEM((LANES // SLOT, devices), jnp.int32), VMEM((LANES, devices), F32)]
        + [VMEM(injection, F32)] * 2,
        in_specs=[hbm] * 10,
        out_specs=[vmem] * 14,
        scratch_shapes=[VMEM((devices, 1, LANES), F32)] * 2
        + [VMEM(plane, F32)] * 2
        + [VMEM(column, F32)] * 2
        + [VMEM(plane, F32)] * 2
        + [VMEM(column, F32)] * 6
        + [
            VMEM(traces.shape, F32), VMEM((1, held), jnp.int32), VMEM((1, held), jnp.int32),
            VMEM(resample.shape, F32),
        ]
        + [dma((6,)), dma((4,)), dma((8,)), dma((8,)), dma, dma, pltpu.SemaphoreType.REGULAR],
        compiler_params=pltpu.CompilerParams(collective_id=0, has_side_effects=True, vmem_limit_bytes=8 * MIB),
        name="route",
    )(
        *(
            pltpu.with_memory_space_constraint(x, HBM)
            for x in (
                pressure_in, vel_inline, vel_xline, vel_depth, modulus, buoyancy,
                traces, owner.reshape(1, held), node_cell, resample,
            )
        )
    )
    *fields, index, values, cleared_a, cleared_b = state
    injected = pl.pallas_call(
        scatter,
        out_shape=[VMEM(injection, F32)] * 2,
        in_specs=[vmem] * 4,
        out_specs=[vmem] * 2,
        scratch_shapes=[pltpu.SMEM((LANES // SLOT, devices), jnp.int32), dma],
        input_output_aliases={2: 0, 3: 1},
        compiler_params=pltpu.CompilerParams(vmem_limit_bytes=2 * MIB),
        name="scatter",
    )(index, values, cleared_a, cleared_b)
    rounds = STEPS - 1
    *fields, ghost_i, ghost_x = pl.pallas_call(
        advance,
        out_shape=[VMEM(field, F32)] * 4 + [VMEM(plane, F32), VMEM(column, F32)],
        in_specs=[vmem] * 12,
        out_specs=[vmem] * 6,
        scratch_shapes=[VMEM((rounds, *plane), F32)] * 2
        + [VMEM((rounds, *column), F32)] * 4
        + [dma((rounds, 4)), dma((rounds, 4))],
        compiler_params=pltpu.CompilerParams(
            collective_id=1, has_side_effects=True, vmem_limit_bytes=4 * MIB
        ),
        name="advance",
    )(*fields, *injected)
    modulus = state[4]
    return pl.pallas_call(
        finish,
        out_shape=[HBM(field, F32)] * 4,
        in_specs=[vmem] * 9,
        out_specs=[hbm] * 4,
        scratch_shapes=[VMEM(field, F32), dma((8,))],
        compiler_params=pltpu.CompilerParams(vmem_limit_bytes=4 * MIB),
        name="finish",
    )(*fields, ghost_i, ghost_x, modulus, *injected)


def solution(mesh):
    field = P("inline", "xline", None)
    nodes = ("xline", "inline")
    return jax.shard_map(
        shards,
        mesh=mesh,
        in_specs=(field,) * 6 + (P(nodes, None), P(nodes, None), P(nodes), P()),
        out_specs=(field,) * 4,
        check_vma=False,
    )
```

```python
import jax
import jax.numpy as jnp
from jax import lax
from jax.experimental import pallas as pl
from jax.experimental.pallas import tpu as pltpu
from jax.sharding import PartitionSpec as P

COURANT = 0.35
STEPS = 4
LANES = 128
SUBLANES = 8
SLOT = 8
NEAR = 8
MESH = pl.DeviceIdType.MESH
VMEM, HBM = pltpu.MemorySpace.VMEM, pltpu.MemorySpace.HBM
F32 = jnp.float32
MIB = 2**20


def lane_ids():
    return lax.broadcasted_iota(jnp.int32, (SUBLANES, LANES), 1)


def row_ids():
    return lax.broadcasted_iota(jnp.int32, (SUBLANES, LANES), 0)


def cols(half):
    return pl.ds(half * LANES, LANES)


def rows(tile):
    return pl.ds(tile * SUBLANES, SUBLANES)


def velocity(p, v_in, v_out, buoyancy, i, tile, next_plane):
    lane = lane_ids()
    (vi, vx, vd), (vi_out, vx_out, vd_out) = v_in, v_out
    here = [p[i, rows(tile), cols(h)] for h in range(2)]
    turned = [pltpu.roll(x, LANES - 1, 1) for x in here]
    deeper = [jnp.where(lane < LANES - 1, turned[0], turned[1]), jnp.where(lane < LANES - 1, turned[1], 0.0)]
    last = p.shape[1] // SUBLANES - 1
    for h in range(2):
        rb = COURANT * buoyancy[i, rows(tile), cols(h)]
        vd_out[i, rows(tile), cols(h)] = vd[i, rows(tile), cols(h)] - rb * (deeper[h] - here[h])
        if next_plane:
            ahead = p[i + 1, rows(tile), cols(h)]
            vi_out[i, rows(tile), cols(h)] = vi[i, rows(tile), cols(h)] - rb * (ahead - here[h])
        if tile < last:
            ahead = p[i, pl.ds(tile * SUBLANES + 1, SUBLANES), cols(h)]
            vx_out[i, rows(tile), cols(h)] = vx[i, rows(tile), cols(h)] - rb * (ahead - here[h])


def velocity_inside(p, v_in, v_out, buoyancy):
    planes, tiles = p.shape[0], p.shape[1] // SUBLANES

    def plane(i, _):
        for tile in range(tiles):
            velocity(p, v_in, v_out, buoyancy, i, tile, True)
        return _

    lax.fori_loop(0, planes - 1, plane, 0, unroll=6)
    for tile in range(tiles):
        velocity(p, v_in, v_out, buoyancy, planes - 1, tile, False)


def velocity_next(p, v_in, v_out, buoyancy, ahead_i):
    planes, tiles = p.shape[0], p.shape[1] // SUBLANES
    for tile in range(tiles):
        for h in range(2):
            at = (planes - 1, rows(tile), cols(h))
            v_out[0][at] = v_in[0][at] - COURANT * buoyancy[at] * (ahead_i[rows(tile), cols(h)] - p[at])


def velocity_side(p, v_in, v_out, buoyancy, ahead_x, i):
    row = row_ids()
    for h in range(2):
        at = (i, rows(p.shape[1] // SUBLANES - 1), cols(h))
        here = p[at]
        ahead = jnp.where(
            row < SUBLANES - 1,
            pltpu.roll(here, SUBLANES - 1, 0),
            jnp.broadcast_to(ahead_x[h, pl.ds(i, 1), :], here.shape),
        )
        v_out[1][at] = v_in[1][at] - COURANT * buoyancy[at] * (ahead - here)


def between(planes, work, unroll):
    def plane(i, _):
        work(i)
        return _

    lax.fori_loop(1, planes - 1, plane, 0, unroll=unroll)


def ghosts(p, first_x, behind_i, behind_x, ghost_in, ghost_out, ghost_b):
    (vi, vx), (vi_out, vx_out), (bi, bx) = ghost_in, ghost_out, ghost_b
    vi_out[...] = vi[...] - COURANT * bi[...] * (p[0] - behind_i[...])
    vx_out[...] = vx[...] - COURANT * bx[...] * (first_x[...] - behind_x[...])


def pressure(p_in, p_out, v, ghost, modulus, i, tile, first, source):
    lane, row = lane_ids(), row_ids()
    vi, vx, vd = v
    ghost_i, ghost_x = ghost
    here = [vd[i, rows(tile), cols(h)] for h in range(2)]
    turned = [pltpu.roll(x, 1, 1) for x in here]
    upper = [jnp.where(lane > 0, turned[0], 0.0), jnp.where(lane > 0, turned[1], turned[0])]
    for h in range(2):
        at = (i, rows(tile), cols(h))
        before_i = ghost_i[rows(tile), cols(h)] if first else vi[i - 1, rows(tile), cols(h)]
        now_x = vx[at]
        if tile > 0:
            before_x = vx[i, pl.ds(tile * SUBLANES - 1, SUBLANES), cols(h)]
        else:
            before_x = jnp.where(
                row > 0,
                pltpu.roll(now_x, 1, 0),
                jnp.broadcast_to(ghost_x[h, pl.ds(i, 1), :], now_x.shape),
            )
        total = (vi[at] - before_i) + (now_x - before_x) + (here[h] - upper[h])
        if source is not None:
            total = total - source(i, tile, h)
        p_out[at] = p_in[at] - COURANT * modulus[at] * total


def source(injected, wide, step):
    def strip(i, tile, h):
        row = ((i * wide + tile * SUBLANES) * 2 + h) * STEPS + step
        at = pl.ds(row, SUBLANES, stride=2 * STEPS)
        return injected[0][at, :] + injected[1][at, :]

    return strip


def ends(planes, tiles, strip):
    for tile in range(tiles):
        strip(0, tile, True)
        strip(planes - 1, tile, False)


def sides(planes, tiles, strip):
    def work(i):
        strip(i, 0, False)
        strip(i, tiles - 1, False)

    between(planes, work, planes - 2)


def core(planes, tiles, strip):
    def work(i):
        for tile in range(1, tiles - 1):
            strip(i, tile, False)

    between(planes, work, 6)


def take_row(source, row, target):
    def plane(i, _):
        for h in range(2):
            target[h, pl.ds(i, 1), :] = source[i, pl.ds(row, 1), cols(h)]
        return _

    lax.fori_loop(0, source.shape[0], plane, 0, unroll=16)


class Exchange:
    def __init__(self, send_sems, recv_sems):
        self.send_sems, self.recv_sems = send_sems, recv_sems
        self.place = (lax.axis_index("xline"), lax.axis_index("inline"))
        self.count = (lax.axis_size("xline"), lax.axis_size("inline"))
        self.copies = []

    def has(self, axis, step):
        return self.place[axis] < self.count[axis] - 1 if step > 0 else self.place[axis] > 0

    def partner(self, axis, step):
        there = list(self.place)
        there[axis] = jnp.clip(there[axis] + step, 0, self.count[axis] - 1)
        return tuple(there)

    def greet(self, barrier):
        for axis in range(2):
            for step in (-1, 1):
                @pl.when(self.has(axis, step))
                def _():
                    pl.semaphore_signal(
                        barrier, inc=1, device_id=self.partner(axis, step), device_id_type=MESH
                    )

    def met(self, barrier):
        partners = [self.has(axis, step).astype(jnp.int32) for axis in range(2) for step in (-1, 1)]
        pl.semaphore_wait(barrier, sum(partners))

    def send(self, source, target, axis, step, number):
        copy = pltpu.make_async_remote_copy(
            src_ref=source,
            dst_ref=target,
            send_sem=self.send_sems.at[number],
            recv_sem=self.recv_sems.at[number],
            device_id=self.partner(axis, step),
            device_id_type=MESH,
        )

        @pl.when(self.has(axis, step))
        def _():
            copy.start()

        self.copies.append((copy, axis, step))

    def finish(self):
        for copy, axis, step in self.copies:
            @pl.when(self.has(axis, step))
            def _():
                copy.wait_send()

            @pl.when(self.has(axis, -step))
            def _():
                copy.wait_recv()

        self.copies = []


def split(value):
    high = value.astype(jnp.bfloat16).astype(F32)
    return high, value - high


def dot_t(a, b):
    return lax.dot_general(
        a.astype(jnp.bfloat16),
        b.astype(jnp.bfloat16),
        (((1,), (1,)), ((), ())),
        preferred_element_type=F32,
    )


def pack(traces, owner, cell, resample, devices):
    held = traces.shape[0]
    owner_row = owner[...]
    cell_row = cell[...]
    member = lax.broadcasted_iota(jnp.int32, (devices, held), 0) == owner_row
    member = jnp.where(member, 1.0, 0.0)
    earlier = lax.broadcasted_iota(jnp.int32, (LANES, LANES), 0) < lax.broadcasted_iota(
        jnp.int32, (LANES, LANES), 1
    )
    earlier = jnp.where(earlier, 1.0, 0.0).astype(jnp.bfloat16)
    running = jnp.zeros((devices, 1), F32)
    position = []
    for block in range(held // LANES):
        part = member[:, block * LANES : (block + 1) * LANES]
        before = jnp.dot(part.astype(jnp.bfloat16), earlier, preferred_element_type=F32) + running
        position.append(jnp.sum(part * before, axis=0, keepdims=True))
        running = running + jnp.sum(part, axis=1, keepdims=True)
    position = jnp.concatenate(position, axis=1).astype(jnp.int32)

    steps = resample.shape[0]
    filt = jnp.concatenate([resample[...], jnp.zeros((SLOT - steps, resample.shape[1]), F32)], 0)
    filt_high, filt_low = split(filt)
    trace_high, trace_low = split(traces[...])
    both = dot_t(jnp.concatenate([filt_high, filt_low], 0), trace_high)
    fields = both[:SLOT] + both[SLOT:] + dot_t(filt_high, trace_low)
    kind = lax.broadcasted_iota(jnp.int32, (SLOT, held), 0)
    fields = jnp.where(kind == steps, cell_row.astype(F32), fields)
    first, rest = split(fields)
    second, third = split(rest)
    packed = []
    for piece in (third, second, first):
        spread = [
            jnp.where(position == q, piece, 0.0) for q in range(LANES // SLOT)
        ]
        packed.append(dot_t(member, jnp.concatenate(spread, 0)))
    return (packed[0] + packed[1]) + packed[2]


def route(
    p_hbm, vi_hbm, vx_hbm, vd_hbm, m_hbm, b_hbm, traces_hbm, owner_hbm, cell_hbm, resample_hbm,
    p, vi, vx, vd, modulus, buoyancy, ghost_i, ghost_x, ghost_bi, ghost_bx, index, values, injected_a, injected_b,
    outbox, inbox, behind_i, ahead_i, behind_x, ahead_x, from_vi, from_bi, from_vx, from_bx,
    first_x, last_x, last_vx, last_bx,
    traces, owner, cell, resample,
    load_sems, node_sems, send_sems, recv_sems, post_sem, mail_sem,
):
    devices = lax.axis_size("xline") * lax.axis_size("inline")
    lines = lax.axis_size("inline")
    planes, tiles = p.shape[0], p.shape[1] // SUBLANES
    injected = (injected_a, injected_b)
    loads = [
        pltpu.make_async_copy(source, target, load_sems.at[k])
        for k, (source, target) in enumerate(
            ((p_hbm, p), (b_hbm, buoyancy), (vx_hbm, vx), (vi_hbm, vi), (vd_hbm, vd), (m_hbm, modulus))
        )
    ]
    node_loads = [
        pltpu.make_async_copy(source, target, node_sems.at[k])
        for k, (source, target) in enumerate(
            ((owner_hbm, owner), (cell_hbm, cell.at[0]), (resample_hbm, resample), (traces_hbm, traces))
        )
    ]
    for load in node_loads:
        load.start()
    barrier = pltpu.get_barrier_semaphore()
    xline, inline = lax.axis_index("xline"), lax.axis_index("inline")
    wide, blocks = lax.axis_size("xline"), lines // NEAR
    block, near = inline // NEAR, lax.rem(inline, NEAR)
    me = xline * lines + inline
    xlines = [lax.rem(xline + k, wide) for k in range(wide)]
    block_starts = [lax.rem(block + k, blocks) * NEAR for k in range(blocks)]
    nears = [lax.rem(near + k, NEAR) for k in range(NEAR)]

    def hops(offset, length):
        return min(offset, length - offset)

    offsets = [(dx, dy, dn) for dx in range(wide) for dy in range(blocks) for dn in range(NEAR)]
    offsets = sorted(
        offsets[1:],
        key=lambda o: -(hops(o[0], wide) + hops(o[1], blocks) + hops(o[2], NEAR) / 2),
    )

    def partner(dx, dy, dn):
        return (xlines[dx], block_starts[dy] + nears[dn])

    for offset in offsets:
        pl.semaphore_signal(barrier, inc=1, device_id=partner(*offset), device_id_type=MESH)
    for load in loads[:2]:
        load.start()
    for load in node_loads:
        load.wait()
    for load in loads[2:]:
        load.start()
    packed = pack(traces, owner, cell, resample, devices)
    for row in range(devices):
        outbox[row] = packed[row : row + 1]
    inbox[me] = outbox[me]
    pl.semaphore_wait(barrier, len(offsets))

    halo = Exchange(send_sems, recv_sems)
    for ref in (behind_i, from_vi, from_bi):
        @pl.when(jnp.logical_not(halo.has(1, -1)))
        def _():
            ref[...] = jnp.zeros_like(ref)
    for ref in (behind_x, from_vx, from_bx):
        @pl.when(jnp.logical_not(halo.has(0, -1)))
        def _():
            ref[...] = jnp.zeros_like(ref)

    @pl.when(jnp.logical_not(halo.has(1, 1)))
    def _():
        ahead_i[...] = jnp.zeros_like(ahead_i)

    @pl.when(jnp.logical_not(halo.has(0, 1)))
    def _():
        ahead_x[...] = jnp.zeros_like(ahead_x)

    last = planes - 1
    halo.send(p_hbm.at[last], behind_i, 1, 1, 0)
    halo.send(p_hbm.at[0], ahead_i, 1, -1, 1)
    halo.send(vi_hbm.at[last], from_vi, 1, 1, 6)
    halo.send(b_hbm.at[last], from_bi, 1, 1, 4)

    def post(dx, dy, dn):
        device = partner(dx, dy, dn)
        pltpu.make_async_remote_copy(
            src_ref=outbox.at[device[0] * lines + device[1]],
            dst_ref=inbox.at[me],
            send_sem=post_sem,
            recv_sem=mail_sem,
            device_id=device,
            device_id_type=MESH,
        ).start()

    for offset in offsets:
        post(*offset)

    loads[0].wait()
    take_row(p, 0, first_x)
    halo.send(first_x, ahead_x, 0, -1, 2)
    take_row(p, p.shape[1] - 1, last_x)
    halo.send(last_x, behind_x, 0, 1, 3)
    loads[1].wait()
    take_row(buoyancy, p.shape[1] - 1, last_bx)
    halo.send(last_bx, from_bx, 0, 1, 5)
    loads[2].wait()
    take_row(vx, p.shape[1] - 1, last_vx)
    halo.send(last_vx, from_vx, 0, 1, 7)

    def clear(k, _):
        for ref in injected:
            ref[pl.ds(pl.multiple_of(k * 64, 64), 64), :] = jnp.zeros((64, LANES), F32)
        return _

    lax.fori_loop(0, injected[0].shape[0] // 64, clear, 0)
    loads[3].wait()
    loads[4].wait()
    v = (vi, vx, vd)
    velocity_inside(p, v, v, buoyancy)
    loads[5].wait()

    def strip(i, tile, first):
        pressure(p, p, v, (ghost_i, ghost_x), modulus, i, tile, first, None)

    core(planes, tiles, strip)
    halo.finish()
    velocity_next(p, v, v, buoyancy, ahead_i)
    for i in (0, planes - 1):
        velocity_side(p, v, v, buoyancy, ahead_x, i)
    between(planes, lambda i: velocity_side(p, v, v, buoyancy, ahead_x, i), 15)
    ghosts(p, first_x, behind_i, behind_x, (from_vi, from_vx), (ghost_i, ghost_x), (from_bi, from_bx))
    ghost_bi[...] = from_bi[...]
    ghost_bx[...] = from_bx[...]
    ends(planes, tiles, strip)
    sides(planes, tiles, strip)

    mail = pltpu.make_async_remote_copy(
        src_ref=outbox.at[pl.ds(0, devices - 1)],
        dst_ref=inbox.at[pl.ds(0, devices - 1)],
        send_sem=post_sem,
        recv_sem=mail_sem,
        device_id=partner(0, 0, 1),
        device_id_type=MESH,
    )
    mail.wait_send()
    mail.wait_recv()
    values[...] = inbox[...].reshape(devices, LANES).T
    index[...] = values[pl.ds(STEPS, LANES // SLOT, stride=SLOT), :].astype(jnp.int32)


def scatter(index_ref, values, _a, _b, injected_a, injected_b, index, sem):
    load = pltpu.make_async_copy(index_ref, index, sem)
    load.start()
    injected = (injected_a, injected_b)
    share = values.shape[1] // len(injected)
    lane = lax.broadcasted_iota(jnp.int32, (STEPS, LANES), 1)
    slots, group = 15, 2

    def spread(d):
        pick = jnp.full((SUBLANES, LANES), d, jnp.int32)
        return [
            jnp.take_along_axis(values[pl.ds(q * SLOT, SLOT), :], pick, axis=1)[:STEPS]
            for q in range(slots)
        ]

    def add(target, d, now, numbers):
        tiles, adds = [], []
        for q in numbers:
            cell = index[q, d]
            tiles.append(lax.shift_right_logical(cell, 7))
            depth = jnp.full(lane.shape, cell, jnp.int32) & (LANES - 1)
            adds.append(jnp.where(lane == depth, now[q], 0.0))
        spots = [pl.ds(pl.multiple_of(tile * STEPS, STEPS), STEPS) for tile in tiles]
        old = [target[spot, :] for spot in spots]
        for b in range(len(numbers)):
            new = old[b] + adds[b]
            for a in range(b):
                new = new + jnp.where(tiles[a] == tiles[b], adds[a], 0.0)
            target[spots[b], :] = new

    def sender(d, now):
        later = [
            spread(jnp.minimum(d + 1, share - 1) + k * share) for k in range(len(injected))
        ]
        for start in range(0, slots, group):
            for k, target in enumerate(injected):
                add(target, d + k * share, now[k], range(start, min(start + group, slots)))
        return later

    first = [spread(k * share) for k in range(len(injected))]
    load.wait()
    lax.fori_loop(0, share, sender, first, unroll=4)


def advance(
    p_in, vi_in, vx_in, vd_in, modulus, buoyancy, ghost_i_in, ghost_x_in, ghost_bi, ghost_bx, injected_a, injected_b,
    p, vi, vx, vd, ghost_i, ghost_x,
    behind_i, ahead_i, behind_x, ahead_x, first_x, last_x, send_sems, recv_sems,
):
    planes, tiles = p.shape[0], p.shape[1] // SUBLANES
    injected = (injected_a, injected_b)
    halo = Exchange(None, None)
    barrier = pltpu.get_barrier_semaphore()
    halo.greet(barrier)

    @pl.when(jnp.logical_not(halo.has(1, -1)))
    def _():
        behind_i[...] = jnp.zeros_like(behind_i)

    @pl.when(jnp.logical_not(halo.has(0, -1)))
    def _():
        behind_x[...] = jnp.zeros_like(behind_x)

    @pl.when(jnp.logical_not(halo.has(1, 1)))
    def _():
        ahead_i[...] = jnp.zeros_like(ahead_i)

    @pl.when(jnp.logical_not(halo.has(0, 1)))
    def _():
        ahead_x[...] = jnp.zeros_like(ahead_x)

    def send_planes(step):
        halo.send_sems, halo.recv_sems = send_sems.at[step], recv_sems.at[step]
        halo.send(p.at[planes - 1], behind_i.at[step], 1, 1, 0)
        halo.send(p.at[0], ahead_i.at[step], 1, -1, 1)

    def send_rows(step):
        take_row(p, 0, first_x.at[step])
        halo.send(first_x.at[step], ahead_x.at[step], 0, -1, 2)
        take_row(p, p.shape[1] - 1, last_x.at[step])
        halo.send(last_x.at[step], behind_x.at[step], 0, 1, 3)

    def inject(i, tile, first):
        del first
        spread = source(injected, p.shape[1], 0)
        for h in range(2):
            at = (i, rows(tile), cols(h))
            p[at] = p_in[at] + COURANT * modulus[at] * spread(i, tile, h)

    ends(planes, tiles, inject)
    sides(planes, tiles, inject)
    halo.met(barrier)
    send_planes(0)
    send_rows(0)
    core(planes, tiles, inject)

    v = (vi, vx, vd)
    for step in range(1, STEPS):
        last = step == STEPS - 1
        v_in = (vi_in, vx_in, vd_in) if step == 1 else v
        ghost_in = (ghost_i_in, ghost_x_in) if step == 1 else (ghost_i, ghost_x)
        spread = source(injected, p.shape[1], step)

        def strip(i, tile, first):
            pressure(p, p, v, (ghost_i, ghost_x), modulus, i, tile, first, spread)

        velocity_inside(p, v_in, v, buoyancy)
        halo.finish()

        def side(i):
            velocity_side(p, v_in, v, buoyancy, ahead_x.at[step - 1], i)

        velocity_next(p, v_in, v, buoyancy, ahead_i.at[step - 1])
        side(0)
        side(planes - 1)
        ghosts(
            p, first_x.at[step - 1], behind_i.at[step - 1], behind_x.at[step - 1],
            ghost_in, (ghost_i, ghost_x), (ghost_bi, ghost_bx),
        )
        if not last:
            ends(planes, tiles, strip)
            send_planes(step)
        between(planes, side, planes - 2)
        if not last:
            sides(planes, tiles, strip)
            send_rows(step)
            core(planes, tiles, strip)


def finish(
    p_in, vi, vx, vd, ghost_i, ghost_x, modulus, injected_a, injected_b,
    p_out, vi_out, vx_out, vd_out,
    p, sems,
):
    planes, tiles = p_in.shape[0], p_in.shape[1] // SUBLANES
    copies = []

    def leave(source_ref, target):
        copies.append(pltpu.make_async_copy(source_ref, target, sems.at[len(copies)]))
        copies[-1].start()

    for source_ref, target in ((vi, vi_out), (vx, vx_out), (vd, vd_out)):
        leave(source_ref, target)
    spread = source((injected_a, injected_b), p_in.shape[1], STEPS - 1)
    size = planes // 4

    def plane(i, first):
        for tile in range(tiles):
            pressure(p_in, p, (vi, vx, vd), (ghost_i, ghost_x), modulus, i, tile, first, spread)

    def inner(i, _):
        plane(i, False)
        return _

    for start in range(0, planes, size):
        if start == 0:
            plane(0, True)
        head = max(start, 1)
        lax.fori_loop(head, start + size, inner, 0, unroll=start + size - head)
        leave(p.at[pl.ds(start, size)], p_out.at[pl.ds(start, size)])
    for copy in copies:
        copy.wait()


def shards(
    pressure_in, vel_inline, vel_xline, vel_depth, modulus, buoyancy, traces, owner, node_cell, resample
):
    planes, wide, deep = pressure_in.shape
    devices = lax.axis_size("xline") * lax.axis_size("inline")
    held = traces.shape[0]
    field = (planes, wide, deep)
    plane, column = (wide, deep), (2, planes, LANES)
    injection = (planes * wide * deep // LANES * STEPS, LANES)
    vmem = pl.BlockSpec(memory_space=VMEM)
    hbm = pl.BlockSpec(memory_space=HBM)
    dma = pltpu.SemaphoreType.DMA

    state = pl.pallas_call(
        route,
        out_shape=[VMEM(field, F32)] * 6
        + [VMEM(plane, F32), VMEM(column, F32)] * 2
        + [VMEM((LANES // SLOT, devices), jnp.int32), VMEM((LANES, devices), F32)]
        + [VMEM(injection, F32)] * 2,
        in_specs=[hbm] * 10,
        out_specs=[vmem] * 14,
        scratch_shapes=[VMEM((devices, 1, LANES), F32)] * 2
        + [VMEM(plane, F32)] * 2
        + [VMEM(column, F32)] * 2
        + [VMEM(plane, F32)] * 2
        + [VMEM(column, F32)] * 6
        + [
            VMEM(traces.shape, F32), VMEM((1, held), jnp.int32), VMEM((1, held), jnp.int32),
            VMEM(resample.shape, F32),
        ]
        + [dma((6,)), dma((4,)), dma((8,)), dma((8,)), dma, dma],
        compiler_params=pltpu.CompilerParams(collective_id=0, has_side_effects=True, vmem_limit_bytes=8 * MIB),
        name="route",
    )(
        *(
            pltpu.with_memory_space_constraint(x, HBM)
            for x in (
                pressure_in, vel_inline, vel_xline, vel_depth, modulus, buoyancy,
                traces, owner.reshape(1, held), node_cell, resample,
            )
        )
    )
    *fields, index, values, cleared_a, cleared_b = state
    injected = pl.pallas_call(
        scatter,
        out_shape=[VMEM(injection, F32)] * 2,
        in_specs=[vmem] * 4,
        out_specs=[vmem] * 2,
        scratch_shapes=[pltpu.SMEM((LANES // SLOT, devices), jnp.int32), dma],
        input_output_aliases={2: 0, 3: 1},
        compiler_params=pltpu.CompilerParams(vmem_limit_bytes=2 * MIB),
        name="scatter",
    )(index, values, cleared_a, cleared_b)
    rounds = STEPS - 1
    *fields, ghost_i, ghost_x = pl.pallas_call(
        advance,
        out_shape=[VMEM(field, F32)] * 4 + [VMEM(plane, F32), VMEM(column, F32)],
        in_specs=[vmem] * 12,
        out_specs=[vmem] * 6,
        scratch_shapes=[VMEM((rounds, *plane), F32)] * 2
        + [VMEM((rounds, *column), F32)] * 4
        + [dma((rounds, 4)), dma((rounds, 4))],
        compiler_params=pltpu.CompilerParams(
            collective_id=1, has_side_effects=True, vmem_limit_bytes=4 * MIB
        ),
        name="advance",
    )(*fields, *injected)
    modulus = state[4]
    return pl.pallas_call(
        finish,
        out_shape=[HBM(field, F32)] * 4,
        in_specs=[vmem] * 9,
        out_specs=[hbm] * 4,
        scratch_shapes=[VMEM(field, F32), dma((8,))],
        compiler_params=pltpu.CompilerParams(vmem_limit_bytes=4 * MIB),
        name="finish",
    )(*fields, ghost_i, ghost_x, modulus, *injected)


def solution(mesh):
    field = P("inline", "xline", None)
    nodes = ("xline", "inline")
    return jax.shard_map(
        shards,
        mesh=mesh,
        in_specs=(field,) * 6 + (P(nodes, None), P(nodes, None), P(nodes), P()),
        out_specs=(field,) * 4,
        check_vma=False,
    )
```

```python
import jax
import jax.numpy as jnp
from jax import lax
from jax.experimental import pallas as pl
from jax.experimental.pallas import tpu as pltpu
from jax.sharding import PartitionSpec as P

COURANT = 0.35
STEPS = 4
LANES = 128
SUBLANES = 8
SLOT = 8
NEAR = 8
MESH = pl.DeviceIdType.MESH
VMEM, HBM = pltpu.MemorySpace.VMEM, pltpu.MemorySpace.HBM
F32 = jnp.float32
MIB = 2**20


def lane_ids():
    return lax.broadcasted_iota(jnp.int32, (SUBLANES, LANES), 1)


def row_ids():
    return lax.broadcasted_iota(jnp.int32, (SUBLANES, LANES), 0)


def cols(half):
    return pl.ds(half * LANES, LANES)


def rows(tile):
    return pl.ds(tile * SUBLANES, SUBLANES)


def velocity(p, v_in, v_out, buoyancy, i, tile, next_plane):
    lane = lane_ids()
    (vi, vx, vd), (vi_out, vx_out, vd_out) = v_in, v_out
    here = [p[i, rows(tile), cols(h)] for h in range(2)]
    turned = [pltpu.roll(x, LANES - 1, 1) for x in here]
    deeper = [jnp.where(lane < LANES - 1, turned[0], turned[1]), jnp.where(lane < LANES - 1, turned[1], 0.0)]
    last = p.shape[1] // SUBLANES - 1
    for h in range(2):
        rb = COURANT * buoyancy[i, rows(tile), cols(h)]
        vd_out[i, rows(tile), cols(h)] = vd[i, rows(tile), cols(h)] - rb * (deeper[h] - here[h])
        if next_plane:
            ahead = p[i + 1, rows(tile), cols(h)]
            vi_out[i, rows(tile), cols(h)] = vi[i, rows(tile), cols(h)] - rb * (ahead - here[h])
        if tile < last:
            ahead = p[i, pl.ds(tile * SUBLANES + 1, SUBLANES), cols(h)]
            vx_out[i, rows(tile), cols(h)] = vx[i, rows(tile), cols(h)] - rb * (ahead - here[h])


def velocity_inside(p, v_in, v_out, buoyancy):
    planes, tiles = p.shape[0], p.shape[1] // SUBLANES

    def plane(i, _):
        for tile in range(tiles):
            velocity(p, v_in, v_out, buoyancy, i, tile, True)
        return _

    lax.fori_loop(0, planes - 1, plane, 0, unroll=6)
    for tile in range(tiles):
        velocity(p, v_in, v_out, buoyancy, planes - 1, tile, False)


def velocity_next(p, v_in, v_out, buoyancy, ahead_i):
    planes, tiles = p.shape[0], p.shape[1] // SUBLANES
    for tile in range(tiles):
        for h in range(2):
            at = (planes - 1, rows(tile), cols(h))
            v_out[0][at] = v_in[0][at] - COURANT * buoyancy[at] * (ahead_i[rows(tile), cols(h)] - p[at])


def velocity_side(p, v_in, v_out, buoyancy, ahead_x, i):
    row = row_ids()
    for h in range(2):
        at = (i, rows(p.shape[1] // SUBLANES - 1), cols(h))
        here = p[at]
        ahead = jnp.where(
            row < SUBLANES - 1,
            pltpu.roll(here, SUBLANES - 1, 0),
            jnp.broadcast_to(ahead_x[h, pl.ds(i, 1), :], here.shape),
        )
        v_out[1][at] = v_in[1][at] - COURANT * buoyancy[at] * (ahead - here)


def between(planes, work, unroll):
    def plane(i, _):
        work(i)
        return _

    lax.fori_loop(1, planes - 1, plane, 0, unroll=unroll)


def ghosts(p, first_x, behind_i, behind_x, ghost_in, ghost_out, ghost_b):
    (vi, vx), (vi_out, vx_out), (bi, bx) = ghost_in, ghost_out, ghost_b
    vi_out[...] = vi[...] - COURANT * bi[...] * (p[0] - behind_i[...])
    vx_out[...] = vx[...] - COURANT * bx[...] * (first_x[...] - behind_x[...])


def pressure(p_in, p_out, v, ghost, modulus, i, tile, first, source):
    lane, row = lane_ids(), row_ids()
    vi, vx, vd = v
    ghost_i, ghost_x = ghost
    here = [vd[i, rows(tile), cols(h)] for h in range(2)]
    turned = [pltpu.roll(x, 1, 1) for x in here]
    upper = [jnp.where(lane > 0, turned[0], 0.0), jnp.where(lane > 0, turned[1], turned[0])]
    for h in range(2):
        at = (i, rows(tile), cols(h))
        before_i = ghost_i[rows(tile), cols(h)] if first else vi[i - 1, rows(tile), cols(h)]
        now_x = vx[at]
        if tile > 0:
            before_x = vx[i, pl.ds(tile * SUBLANES - 1, SUBLANES), cols(h)]
        else:
            before_x = jnp.where(
                row > 0,
                pltpu.roll(now_x, 1, 0),
                jnp.broadcast_to(ghost_x[h, pl.ds(i, 1), :], now_x.shape),
            )
        total = (vi[at] - before_i) + (now_x - before_x) + (here[h] - upper[h])
        if source is not None:
            total = total - source(i, tile, h)
        p_out[at] = p_in[at] - COURANT * modulus[at] * total


def source(injected, wide, step):
    def strip(i, tile, h):
        row = ((i * wide + tile * SUBLANES) * 2 + h) * STEPS + step
        at = pl.ds(row, SUBLANES, stride=2 * STEPS)
        return injected[0][at, :] + injected[1][at, :]

    return strip


def ends(planes, tiles, strip):
    for tile in range(tiles):
        strip(0, tile, True)
        strip(planes - 1, tile, False)


def sides(planes, tiles, strip):
    def work(i):
        strip(i, 0, False)
        strip(i, tiles - 1, False)

    between(planes, work, planes - 2)


def core(planes, tiles, strip):
    def work(i):
        for tile in range(1, tiles - 1):
            strip(i, tile, False)

    between(planes, work, 6)


def take_row(source, row, target):
    def plane(i, _):
        for h in range(2):
            target[h, pl.ds(i, 1), :] = source[i, pl.ds(row, 1), cols(h)]
        return _

    lax.fori_loop(0, source.shape[0], plane, 0, unroll=16)


class Exchange:
    def __init__(self, send_sems, recv_sems):
        self.send_sems, self.recv_sems = send_sems, recv_sems
        self.place = (lax.axis_index("xline"), lax.axis_index("inline"))
        self.count = (lax.axis_size("xline"), lax.axis_size("inline"))
        self.copies = []

    def has(self, axis, step):
        return self.place[axis] < self.count[axis] - 1 if step > 0 else self.place[axis] > 0

    def partner(self, axis, step):
        there = list(self.place)
        there[axis] = jnp.clip(there[axis] + step, 0, self.count[axis] - 1)
        return tuple(there)

    def greet(self, barrier):
        for axis in range(2):
            for step in (-1, 1):
                @pl.when(self.has(axis, step))
                def _():
                    pl.semaphore_signal(
                        barrier, inc=1, device_id=self.partner(axis, step), device_id_type=MESH
                    )

    def met(self, barrier):
        partners = [self.has(axis, step).astype(jnp.int32) for axis in range(2) for step in (-1, 1)]
        pl.semaphore_wait(barrier, sum(partners))

    def send(self, source, target, axis, step, number):
        copy = pltpu.make_async_remote_copy(
            src_ref=source,
            dst_ref=target,
            send_sem=self.send_sems.at[number],
            recv_sem=self.recv_sems.at[number],
            device_id=self.partner(axis, step),
            device_id_type=MESH,
        )

        @pl.when(self.has(axis, step))
        def _():
            copy.start()

        self.copies.append((copy, axis, step))

    def finish(self):
        for copy, axis, step in self.copies:
            @pl.when(self.has(axis, step))
            def _():
                copy.wait_send()

            @pl.when(self.has(axis, -step))
            def _():
                copy.wait_recv()

        self.copies = []


def split(value):
    high = value.astype(jnp.bfloat16).astype(F32)
    return high, value - high


def dot_t(a, b):
    return lax.dot_general(
        a.astype(jnp.bfloat16),
        b.astype(jnp.bfloat16),
        (((1,), (1,)), ((), ())),
        preferred_element_type=F32,
    )


def pack(traces, owner, cell, resample, devices):
    held = traces.shape[0]
    owner_row = owner[...]
    cell_row = cell[...]
    member = lax.broadcasted_iota(jnp.int32, (devices, held), 0) == owner_row
    member = jnp.where(member, 1.0, 0.0)
    earlier = lax.broadcasted_iota(jnp.int32, (LANES, LANES), 0) < lax.broadcasted_iota(
        jnp.int32, (LANES, LANES), 1
    )
    earlier = jnp.where(earlier, 1.0, 0.0).astype(jnp.bfloat16)
    running = jnp.zeros((devices, 1), F32)
    position = []
    for block in range(held // LANES):
        part = member[:, block * LANES : (block + 1) * LANES]
        before = jnp.dot(part.astype(jnp.bfloat16), earlier, preferred_element_type=F32) + running
        position.append(jnp.sum(part * before, axis=0, keepdims=True))
        running = running + jnp.sum(part, axis=1, keepdims=True)
    position = jnp.concatenate(position, axis=1).astype(jnp.int32)

    steps = resample.shape[0]
    filt = jnp.concatenate([resample[...], jnp.zeros((SLOT - steps, resample.shape[1]), F32)], 0)
    filt_high, filt_low = split(filt)
    trace_high, trace_low = split(traces[...])
    both = dot_t(jnp.concatenate([filt_high, filt_low], 0), trace_high)
    fields = both[:SLOT] + both[SLOT:] + dot_t(filt_high, trace_low)
    kind = lax.broadcasted_iota(jnp.int32, (SLOT, held), 0)
    fields = jnp.where(kind == steps, cell_row.astype(F32), fields)
    first, rest = split(fields)
    second, third = split(rest)
    packed = []
    for piece in (third, second, first):
        spread = [
            jnp.where(position == q, piece, 0.0) for q in range(LANES // SLOT)
        ]
        packed.append(dot_t(member, jnp.concatenate(spread, 0)))
    return (packed[0] + packed[1]) + packed[2]


def route(
    p_hbm, vi_hbm, vx_hbm, vd_hbm, m_hbm, b_hbm, traces_hbm, owner_hbm, cell_hbm, resample_hbm,
    p, vi, vx, vd, modulus, buoyancy, ghost_i, ghost_x, ghost_bi, ghost_bx, index, values, injected_a, injected_b,
    outbox, inbox, behind_i, ahead_i, behind_x, ahead_x, from_vi, from_bi, from_vx, from_bx,
    first_x, last_x, last_vx, last_bx,
    traces, owner, cell, resample,
    load_sems, node_sems, send_sems, recv_sems, post_sem, mail_sem,
):
    devices = lax.axis_size("xline") * lax.axis_size("inline")
    lines = lax.axis_size("inline")
    planes, tiles = p.shape[0], p.shape[1] // SUBLANES
    loads = [
        pltpu.make_async_copy(source, target, load_sems.at[k])
        for k, (source, target) in enumerate(
            ((p_hbm, p), (b_hbm, buoyancy), (vx_hbm, vx), (vi_hbm, vi), (vd_hbm, vd), (m_hbm, modulus))
        )
    ]
    node_loads = [
        pltpu.make_async_copy(source, target, node_sems.at[k])
        for k, (source, target) in enumerate(
            ((owner_hbm, owner), (cell_hbm, cell.at[0]), (resample_hbm, resample), (traces_hbm, traces))
        )
    ]
    for load in node_loads:
        load.start()
    barrier = pltpu.get_barrier_semaphore()
    xline, inline = lax.axis_index("xline"), lax.axis_index("inline")
    wide, blocks = lax.axis_size("xline"), lines // NEAR
    block, near = inline // NEAR, lax.rem(inline, NEAR)
    me = xline * lines + inline
    xlines = [lax.rem(xline + k, wide) for k in range(wide)]
    block_starts = [lax.rem(block + k, blocks) * NEAR for k in range(blocks)]
    nears = [lax.rem(near + k, NEAR) for k in range(NEAR)]

    def hops(offset, length):
        return min(offset, length - offset)

    offsets = [(dx, dy, dn) for dx in range(wide) for dy in range(blocks) for dn in range(NEAR)]
    offsets = sorted(
        offsets[1:],
        key=lambda o: -(hops(o[0], wide) + hops(o[1], blocks) + hops(o[2], NEAR) / 2),
    )

    def partner(dx, dy, dn):
        return (xlines[dx], block_starts[dy] + nears[dn])

    for offset in offsets:
        pl.semaphore_signal(barrier, inc=1, device_id=partner(*offset), device_id_type=MESH)
    for load in loads[:2]:
        load.start()
    for load in node_loads:
        load.wait()
    for load in loads[2:]:
        load.start()
    packed = pack(traces, owner, cell, resample, devices)
    for row in range(devices):
        outbox[row] = packed[row : row + 1]
    inbox[me] = outbox[me]
    pl.semaphore_wait(barrier, len(offsets))

    halo = Exchange(send_sems, recv_sems)
    for ref in (behind_i, from_vi, from_bi):
        @pl.when(jnp.logical_not(halo.has(1, -1)))
        def _():
            ref[...] = jnp.zeros_like(ref)
    for ref in (behind_x, from_vx, from_bx):
        @pl.when(jnp.logical_not(halo.has(0, -1)))
        def _():
            ref[...] = jnp.zeros_like(ref)

    @pl.when(jnp.logical_not(halo.has(1, 1)))
    def _():
        ahead_i[...] = jnp.zeros_like(ahead_i)

    @pl.when(jnp.logical_not(halo.has(0, 1)))
    def _():
        ahead_x[...] = jnp.zeros_like(ahead_x)

    last = planes - 1
    halo.send(p_hbm.at[last], behind_i, 1, 1, 0)
    halo.send(p_hbm.at[0], ahead_i, 1, -1, 1)
    halo.send(vi_hbm.at[last], from_vi, 1, 1, 6)
    halo.send(b_hbm.at[last], from_bi, 1, 1, 4)

    def post(dx, dy, dn):
        device = partner(dx, dy, dn)
        pltpu.make_async_remote_copy(
            src_ref=outbox.at[device[0] * lines + device[1]],
            dst_ref=inbox.at[me],
            send_sem=post_sem,
            recv_sem=mail_sem,
            device_id=device,
            device_id_type=MESH,
        ).start()

    for offset in offsets:
        post(*offset)

    loads[0].wait()
    take_row(p, 0, first_x)
    halo.send(first_x, ahead_x, 0, -1, 2)
    take_row(p, p.shape[1] - 1, last_x)
    halo.send(last_x, behind_x, 0, 1, 3)
    loads[1].wait()
    take_row(buoyancy, p.shape[1] - 1, last_bx)
    halo.send(last_bx, from_bx, 0, 1, 5)
    loads[2].wait()
    take_row(vx, p.shape[1] - 1, last_vx)
    halo.send(last_vx, from_vx, 0, 1, 7)

    def clear(ref):
        def part(k, _):
            ref[pl.ds(pl.multiple_of(k * 64, 64), 64), :] = jnp.zeros((64, LANES), F32)
            return _

        lax.fori_loop(0, ref.shape[0] // 64, part, 0)

    clear(injected_a)
    loads[3].wait()
    loads[4].wait()
    v = (vi, vx, vd)
    velocity_inside(p, v, v, buoyancy)
    loads[5].wait()

    def strip(i, tile, first):
        pressure(p, p, v, (ghost_i, ghost_x), modulus, i, tile, first, None)

    core(planes, tiles, strip)
    clear(injected_b)
    halo.finish()
    velocity_next(p, v, v, buoyancy, ahead_i)
    for i in (0, planes - 1):
        velocity_side(p, v, v, buoyancy, ahead_x, i)
    between(planes, lambda i: velocity_side(p, v, v, buoyancy, ahead_x, i), 15)
    ghosts(p, first_x, behind_i, behind_x, (from_vi, from_vx), (ghost_i, ghost_x), (from_bi, from_bx))
    ghost_bi[...] = from_bi[...]
    ghost_bx[...] = from_bx[...]
    ends(planes, tiles, strip)
    sides(planes, tiles, strip)

    mail = pltpu.make_async_remote_copy(
        src_ref=outbox.at[pl.ds(0, devices - 1)],
        dst_ref=inbox.at[pl.ds(0, devices - 1)],
        send_sem=post_sem,
        recv_sem=mail_sem,
        device_id=partner(0, 0, 1),
        device_id_type=MESH,
    )
    mail.wait_send()
    mail.wait_recv()
    values[...] = inbox[...].reshape(devices, LANES).T
    index[...] = values[pl.ds(STEPS, LANES // SLOT, stride=SLOT), :].astype(jnp.int32)


def scatter(index_ref, values, _a, _b, injected_a, injected_b, index, sem):
    load = pltpu.make_async_copy(index_ref, index, sem)
    load.start()
    injected = (injected_a, injected_b)
    share = values.shape[1] // len(injected)
    lane = lax.broadcasted_iota(jnp.int32, (STEPS, LANES), 1)
    slots, group = 15, 2

    def spread(d):
        pick = jnp.full((SUBLANES, LANES), d, jnp.int32)
        return [
            jnp.take_along_axis(values[pl.ds(q * SLOT, SLOT), :], pick, axis=1)[:STEPS]
            for q in range(slots)
        ]

    def add(target, d, now, numbers):
        tiles, adds = [], []
        for q in numbers:
            cell = index[q, d]
            tiles.append(lax.shift_right_logical(cell, 7))
            depth = jnp.full(lane.shape, cell, jnp.int32) & (LANES - 1)
            adds.append(jnp.where(lane == depth, now[q], 0.0))
        spots = [pl.ds(pl.multiple_of(tile * STEPS, STEPS), STEPS) for tile in tiles]
        old = [target[spot, :] for spot in spots]
        for b in range(len(numbers)):
            new = old[b] + adds[b]
            for a in range(b):
                new = new + jnp.where(tiles[a] == tiles[b], adds[a], 0.0)
            target[spots[b], :] = new

    def sender(d, now):
        later = [
            spread(jnp.minimum(d + 1, share - 1) + k * share) for k in range(len(injected))
        ]
        for start in range(0, slots, group):
            for k, target in enumerate(injected):
                add(target, d + k * share, now[k], range(start, min(start + group, slots)))
        return later

    first = [spread(k * share) for k in range(len(injected))]
    load.wait()
    lax.fori_loop(0, share, sender, first, unroll=4)


def advance(
    p_in, vi_in, vx_in, vd_in, modulus, buoyancy, ghost_i_in, ghost_x_in, ghost_bi, ghost_bx, injected_a, injected_b,
    p, vi, vx, vd, ghost_i, ghost_x,
    behind_i, ahead_i, behind_x, ahead_x, first_x, last_x, send_sems, recv_sems,
):
    planes, tiles = p.shape[0], p.shape[1] // SUBLANES
    injected = (injected_a, injected_b)
    halo = Exchange(None, None)
    barrier = pltpu.get_barrier_semaphore()
    halo.greet(barrier)

    @pl.when(jnp.logical_not(halo.has(1, -1)))
    def _():
        behind_i[...] = jnp.zeros_like(behind_i)

    @pl.when(jnp.logical_not(halo.has(0, -1)))
    def _():
        behind_x[...] = jnp.zeros_like(behind_x)

    @pl.when(jnp.logical_not(halo.has(1, 1)))
    def _():
        ahead_i[...] = jnp.zeros_like(ahead_i)

    @pl.when(jnp.logical_not(halo.has(0, 1)))
    def _():
        ahead_x[...] = jnp.zeros_like(ahead_x)

    def send_planes(step):
        halo.send_sems, halo.recv_sems = send_sems.at[step], recv_sems.at[step]
        halo.send(p.at[planes - 1], behind_i.at[step], 1, 1, 0)
        halo.send(p.at[0], ahead_i.at[step], 1, -1, 1)

    def send_rows(step):
        take_row(p, 0, first_x.at[step])
        halo.send(first_x.at[step], ahead_x.at[step], 0, -1, 2)
        take_row(p, p.shape[1] - 1, last_x.at[step])
        halo.send(last_x.at[step], behind_x.at[step], 0, 1, 3)

    def inject(i, tile, first):
        del first
        spread = source(injected, p.shape[1], 0)
        for h in range(2):
            at = (i, rows(tile), cols(h))
            p[at] = p_in[at] + COURANT * modulus[at] * spread(i, tile, h)

    ends(planes, tiles, inject)
    sides(planes, tiles, inject)
    halo.met(barrier)
    send_planes(0)
    send_rows(0)
    core(planes, tiles, inject)

    v = (vi, vx, vd)
    for step in range(1, STEPS):
        last = step == STEPS - 1
        v_in = (vi_in, vx_in, vd_in) if step == 1 else v
        ghost_in = (ghost_i_in, ghost_x_in) if step == 1 else (ghost_i, ghost_x)
        spread = source(injected, p.shape[1], step)

        def strip(i, tile, first):
            pressure(p, p, v, (ghost_i, ghost_x), modulus, i, tile, first, spread)

        velocity_inside(p, v_in, v, buoyancy)
        halo.finish()

        def side(i):
            velocity_side(p, v_in, v, buoyancy, ahead_x.at[step - 1], i)

        velocity_next(p, v_in, v, buoyancy, ahead_i.at[step - 1])
        side(0)
        side(planes - 1)
        ghosts(
            p, first_x.at[step - 1], behind_i.at[step - 1], behind_x.at[step - 1],
            ghost_in, (ghost_i, ghost_x), (ghost_bi, ghost_bx),
        )
        if not last:
            ends(planes, tiles, strip)
            send_planes(step)
        between(planes, side, planes - 2)
        if not last:
            sides(planes, tiles, strip)
            send_rows(step)
            core(planes, tiles, strip)


def finish(
    p_in, vi, vx, vd, ghost_i, ghost_x, modulus, injected_a, injected_b,
    p_out, vi_out, vx_out, vd_out,
    p, sems,
):
    planes, tiles = p_in.shape[0], p_in.shape[1] // SUBLANES
    copies = []

    def leave(source_ref, target):
        copies.append(pltpu.make_async_copy(source_ref, target, sems.at[len(copies)]))
        copies[-1].start()

    for source_ref, target in ((vi, vi_out), (vx, vx_out), (vd, vd_out)):
        leave(source_ref, target)
    spread = source((injected_a, injected_b), p_in.shape[1], STEPS - 1)
    size = planes // 4

    def plane(i, first):
        for tile in range(tiles):
            pressure(p_in, p, (vi, vx, vd), (ghost_i, ghost_x), modulus, i, tile, first, spread)

    def inner(i, _):
        plane(i, False)
        return _

    for start in range(0, planes, size):
        if start == 0:
            plane(0, True)
        head = max(start, 1)
        lax.fori_loop(head, start + size, inner, 0, unroll=start + size - head)
        leave(p.at[pl.ds(start, size)], p_out.at[pl.ds(start, size)])
    for copy in copies:
        copy.wait()


def shards(
    pressure_in, vel_inline, vel_xline, vel_depth, modulus, buoyancy, traces, owner, node_cell, resample
):
    planes, wide, deep = pressure_in.shape
    devices = lax.axis_size("xline") * lax.axis_size("inline")
    held = traces.shape[0]
    field = (planes, wide, deep)
    plane, column = (wide, deep), (2, planes, LANES)
    injection = (planes * wide * deep // LANES * STEPS, LANES)
    vmem = pl.BlockSpec(memory_space=VMEM)
    hbm = pl.BlockSpec(memory_space=HBM)
    dma = pltpu.SemaphoreType.DMA

    state = pl.pallas_call(
        route,
        out_shape=[VMEM(field, F32)] * 6
        + [VMEM(plane, F32), VMEM(column, F32)] * 2
        + [VMEM((LANES // SLOT, devices), jnp.int32), VMEM((LANES, devices), F32)]
        + [VMEM(injection, F32)] * 2,
        in_specs=[hbm] * 10,
        out_specs=[vmem] * 14,
        scratch_shapes=[VMEM((devices, 1, LANES), F32)] * 2
        + [VMEM(plane, F32)] * 2
        + [VMEM(column, F32)] * 2
        + [VMEM(plane, F32)] * 2
        + [VMEM(column, F32)] * 6
        + [
            VMEM(traces.shape, F32), VMEM((1, held), jnp.int32), VMEM((1, held), jnp.int32),
            VMEM(resample.shape, F32),
        ]
        + [dma((6,)), dma((4,)), dma((8,)), dma((8,)), dma, dma],
        compiler_params=pltpu.CompilerParams(collective_id=0, has_side_effects=True, vmem_limit_bytes=8 * MIB),
        name="route",
    )(
        *(
            pltpu.with_memory_space_constraint(x, HBM)
            for x in (
                pressure_in, vel_inline, vel_xline, vel_depth, modulus, buoyancy,
                traces, owner.reshape(1, held), node_cell, resample,
            )
        )
    )
    *fields, index, values, cleared_a, cleared_b = state
    injected = pl.pallas_call(
        scatter,
        out_shape=[VMEM(injection, F32)] * 2,
        in_specs=[vmem] * 4,
        out_specs=[vmem] * 2,
        scratch_shapes=[pltpu.SMEM((LANES // SLOT, devices), jnp.int32), dma],
        input_output_aliases={2: 0, 3: 1},
        compiler_params=pltpu.CompilerParams(vmem_limit_bytes=2 * MIB),
        name="scatter",
    )(index, values, cleared_a, cleared_b)
    rounds = STEPS - 1
    *fields, ghost_i, ghost_x = pl.pallas_call(
        advance,
        out_shape=[VMEM(field, F32)] * 4 + [VMEM(plane, F32), VMEM(column, F32)],
        in_specs=[vmem] * 12,
        out_specs=[vmem] * 6,
        scratch_shapes=[VMEM((rounds, *plane), F32)] * 2
        + [VMEM((rounds, *column), F32)] * 4
        + [dma((rounds, 4)), dma((rounds, 4))],
        compiler_params=pltpu.CompilerParams(
            collective_id=1, has_side_effects=True, vmem_limit_bytes=4 * MIB
        ),
        name="advance",
    )(*fields, *injected)
    modulus = state[4]
    return pl.pallas_call(
        finish,
        out_shape=[HBM(field, F32)] * 4,
        in_specs=[vmem] * 9,
        out_specs=[hbm] * 4,
        scratch_shapes=[VMEM(field, F32), dma((8,))],
        compiler_params=pltpu.CompilerParams(vmem_limit_bytes=4 * MIB),
        name="finish",
    )(*fields, ghost_i, ghost_x, modulus, *injected)


def solution(mesh):
    field = P("inline", "xline", None)
    nodes = ("xline", "inline")
    return jax.shard_map(
        shards,
        mesh=mesh,
        in_specs=(field,) * 6 + (P(nodes, None), P(nodes, None), P(nodes), P()),
        out_specs=(field,) * 4,
        check_vma=False,
    )
```
